32 devices in a mesh: wide: 8 (over z, y), narrow: 4 (over x, core).
Axes of the slice: x: 2, y: 2, z: 4, core: 2. Of those that a mesh axis runs over, the one named last changes fastest.
Arguments:
- material_flow_vector: float32 [3, 256, 256, 512], P(None, 'wide', 'narrow'), may hold values from -6 to 6
- tool_push_density: float32 [3, 256, 256, 512], P(None, 'wide', 'narrow'), may hold values from -6 to 6
- tool_warmth_excess: float32 [256, 256, 512], P('wide', 'narrow'), may hold values from 0.7 to 1.3
- substrate_warmth_excess: float32 [128, 128, 128], P('wide', 'narrow'), may hold values from -6 to 6
- spread_coefficient: float32 [128, 128, 128], P('wide', 'narrow'), may hold values from 0.02 to 0.08
- source_owner_sheet: int32 [262144, 1], P(('wide', 'narrow')), may hold values from 0 to 7; in each aligned block of 8192 rows (0 to 8191, 8192 to 16383, ...) at most 3072 rows name the same one
- source_part_line: int32 [262144], P(('wide', 'narrow')), may hold values from 0 to 511
Outputs:
- corrected_flow_vector: float32 [3, 256, 256, 512], P(None, 'wide', 'narrow')
- part_out: float32 [128, 128, 128], P('wide', 'narrow')
The draws below stay inside these ranges and needn't reach their ends.
Inputs may be any that keep to these rules, and one draw needn't show every extreme that they name: `source_owner_sheet`: among the 8192 blocks of one device, no slab is named by more than 3072 of them.
All inputs are finite; a program needn't handle non-finite values.
Results may differ from the reference program's by a relative error of at most 0.00012.
Values sent between devices are 32-bit elements; how exact they have to be, the bound alone decides.
No kernel may reach another device: no remote copies, remote signals or barrier semaphores. Data moves between devices by JAX's collectives and lax.ppermute only.
A program may use at most 256 MiB of HBM per device.

```python
import math
import jax
import jax.numpy as jnp
import numpy as np

NX = 256
NY = 256
NZ = 512
PASSES = 2
STEPS = 3
SPAN_DEPTH = 128
PZD = 16
PYD = 32
XL = 32
YL = 64
NZB = 4
HBLK = 8192
CAP = 3072
PR = 512
SPAN_ALTITUDE = 128
SPAN_BREADTH = 128
N_WIDE = 8
N_NARROW = 4


def place_ends(result, stream_key, low, top_value):
    spot = [jax.random.randint(jax.random.fold_in(stream_key, axis), (), 0, length) for axis, length in enumerate(result.shape)]
    main_axis = result.shape.index(max(result.shape))
    neighbour = spot[:main_axis] + [(spot[main_axis] + 1) % result.shape[main_axis]] + spot[main_axis + 1:]
    return result.at[tuple(spot)].set(low).at[tuple(neighbour)].set(top_value)


def block_levels(stream_key, extent, split, low, largest):
    def one(dim, parts):
        heights = jax.random.uniform(jax.random.fold_in(jax.random.fold_in(stream_key, 6), dim), (parts,), jnp.float32, low / len(split), largest / len(split))
        return jnp.repeat(jnp.exp(heights), extent[dim] // parts).reshape((-1,) + (1,) * (len(extent) - dim - 1))

    level = one(*split[0])
    for cut in split[1:]:
        level = level * one(*cut)
    return level


def routed_block(rng, own, number, rows, count, top, most, slope):
    ranking = jax.random.permutation(rng, count)
    heavy_load, common = load_shares(count, rows * top, most, slope, True), load_shares(count, rows * top, most, slope, False)
    places = jnp.arange(count)

    def named(tallies, offset_by):
        used = int((tallies > 0).sum())
        fixed = max(1, used // 4)
        shifted = fixed + (places - fixed + offset_by * (used - fixed)) % max(1, count - fixed)
        return jnp.zeros((count,), jnp.int32).at[ranking[jnp.where(places < fixed, places, shifted)]].set(jnp.asarray(tallies, jnp.int32))

    tallies = jnp.where(number % 4 == 0, named(heavy_load, number // 4), named(common, number - number // 4 - 1))
    mixed = jax.random.permutation(jax.random.fold_in(own, 3), count)
    donor, sink = mixed[0:count // 2 * 2:2], mixed[1:count // 2 * 2:2]
    room = jnp.minimum(tallies[donor] - 1, most - tallies[sink]) // 2
    room = jnp.where((donor == ranking[0]) | (sink == ranking[0]) | (tallies[sink] == 0), 0, jnp.maximum(room, 0))
    shifted = jax.random.randint(jax.random.fold_in(own, 4), (count // 2,), 0, 1 << 20) % (room + 1)
    tallies = tallies.at[donor].add(-shifted).at[sink].add(shifted)
    items = jnp.searchsorted(jnp.cumsum(tallies), jnp.arange(rows * top), side="right").astype(jnp.int32)
    listing = items.reshape(top, rows).T
    listing = listing[jax.random.permutation(jax.random.fold_in(own, 1), rows)]
    offset_by = jax.random.randint(jax.random.fold_in(own, 2), (rows, 1), 0, top)
    return jnp.take_along_axis(listing, (jnp.arange(top)[None, :] + offset_by) % top, axis=1)


def load_shares(number_of, total, limit, slope, full):
    weights = [(1 << 20) // math.isqrt(standing ** slope) + 1 for standing in range(1, number_of + 1)]
    largest = limit if full else min(limit, max(-(-total // number_of), total * weights[0] // sum(weights)))
    least = 1 if total - largest >= number_of - 1 else 0
    given, spare = [largest] + [least] * (number_of - 1), total - largest - least * (number_of - 1)
    while spare > 0:
        candidates = [i for i in range(1, number_of) if given[i] < largest] or [i for i in range(1, number_of) if given[i] < limit]
        mass, budget = sum([weights[i] for i in candidates]), spare
        for i in candidates:
            addition = min(limit - given[i], max(1, budget * weights[i] // mass), spare)
            given[i] = given[i] + addition
            spare = spare - addition
    return np.array(given)


def scatter_about(stream_key, dims, deviation, bound, cuts=(), held_as=jnp.bfloat16):
    loudness = block_levels(stream_key, dims, cuts, -0.22, 0.18) if cuts else 1.0
    drawn = jax.random.normal(stream_key, dims, jnp.float32) * deviation * loudness
    return jnp.minimum(jnp.maximum(drawn, -bound), bound).astype(held_as)


def setup_inputs(seed: int = 0) -> dict:
    keys = jax.random.split(jax.random.key(seed), 8)
    material_flow_vector = scatter_about(keys[0], (3, NX, NY, NZ), 1.0, 6.0, ((1, 8), (2, 4)), jnp.float32)
    tool_push_density = scatter_about(keys[1], (3, NX, NY, NZ), 1.0, 6.0, ((1, 8), (2, 4)), jnp.float32)
    tool_warmth_excess = jnp.clip(0.7 + 0.59999996 * jax.random.uniform(keys[2], (NX, NY, NZ), jnp.float32) ** block_levels(keys[2], (NX, NY, NZ), ((0, 8), (1, 4)), -0.2, 0.2), 0.7, 1.3)
    substrate_warmth_excess = scatter_about(keys[3], (SPAN_ALTITUDE, SPAN_BREADTH, SPAN_DEPTH), 1.0, 6.0, ((0, 8), (1, 4)), jnp.float32)
    spread_coefficient = jnp.clip(jnp.exp(math.log(0.08) - 1.3862944 * jax.random.uniform(keys[4], (SPAN_ALTITUDE, SPAN_BREADTH, SPAN_DEPTH), jnp.float32) ** block_levels(keys[4], (SPAN_ALTITUDE, SPAN_BREADTH, SPAN_DEPTH), ((0, 8), (1, 4)), -0.2, 0.2)), 0.02, 0.08)
    source_owner_sheet_keys = jax.random.split(jax.random.fold_in(keys[5], 1), (N_WIDE * N_NARROW * HBLK) // HBLK)
    source_owner_sheet_turns = jax.random.permutation(jax.random.fold_in(keys[5], 3), (N_WIDE * N_NARROW * HBLK) // HBLK)
    source_owner_sheet = jax.vmap(lambda own, number: routed_block(jax.random.fold_in(keys[5], 2), own, number, HBLK, N_WIDE, 1, CAP, 2))(source_owner_sheet_keys, source_owner_sheet_turns).reshape((N_WIDE * N_NARROW * HBLK, 1))
    source_part_line = place_ends(jax.random.randint(keys[6], (N_WIDE * N_NARROW * HBLK,), 0, PR), jax.random.fold_in(keys[6], 1), 0, PR - 1).astype(jnp.int32)
    return dict(material_flow_vector=material_flow_vector, tool_push_density=tool_push_density, tool_warmth_excess=tool_warmth_excess, substrate_warmth_excess=substrate_warmth_excess, spread_coefficient=spread_coefficient, source_owner_sheet=source_owner_sheet, source_part_line=source_part_line)


time_step = 0.15
rate_base = 0.5
zener_energy = 4.0
stress_exponent = 5.0
penalty = 0.001
dissipation_factor = 0.1

def central(field, axis):
    return (jnp.roll(field, -1, axis) - jnp.roll(field, 1, axis)) * 0.5

def rate_squared(current):
    s_xx = central(current[0], 0)
    s_yy = central(current[1], 1)
    s_zz = central(current[2], 2)
    s_xy = 0.5 * (central(current[0], 1) + central(current[1], 0))
    s_xz = 0.5 * (central(current[0], 2) + central(current[2], 0))
    s_yz = 0.5 * (central(current[1], 2) + central(current[2], 1))
    total = s_xx ** 2 + s_yy ** 2 + s_zz ** 2 + 2.0 * (s_xy ** 2 + s_xz ** 2 + s_yz ** 2)
    return rate_base ** 2 + 2.0 * total

def inverse_sinh(value):
    return jnp.log(value + jnp.sqrt(value * value + 1.0))

def viscosity(rate_sq, zener):
    rate = jnp.sqrt(rate_sq)
    return inverse_sinh((rate * zener) ** (1.0 / stress_exponent)) / (3.0 * rate)

def viscous_term(mu_field, current):
    total = jnp.zeros_like(current)
    for axis in range(3):
        mu_ahead = jnp.roll(mu_field, -1, axis)
        mu_behind = jnp.roll(mu_field, 1, axis)
        vel_ahead = jnp.roll(current, -1, axis + 1)
        vel_behind = jnp.roll(current, 1, axis + 1)
        total = total + 0.5 * (mu_field + mu_ahead) * (vel_ahead - current) - 0.5 * (mu_field + mu_behind) * (current - vel_behind)
    return total

def sine_squared(count):
    waves = jnp.arange(count, dtype=jnp.int32).astype(jnp.float32)
    return jnp.sin(waves * (2.0 * math.pi / count)) ** 2

def reference(material_flow_vector, tool_push_density, tool_warmth_excess, substrate_warmth_excess, spread_coefficient, source_owner_sheet, source_part_line):
    zener = jnp.exp(zener_energy * (1.0 / tool_warmth_excess - 1.0))
    current = material_flow_vector
    rate_sq = rate_squared(current)
    mu_field = viscosity(rate_sq, zener)
    for section in range(PASSES):
        rate_sq = rate_squared(current)
        mu_field = viscosity(rate_sq, zener)
        current = material_flow_vector + time_step * (viscous_term(mu_field, material_flow_vector) + tool_push_density)
    heat = mu_field * (rate_sq - rate_base ** 2)
    divergence = central(current[0], 0) + central(current[1], 1) + central(current[2], 2)
    spectrum = jnp.fft.fftn(divergence)
    symbol = sine_squared(NX)[:, None, None] + sine_squared(NY)[None, :, None] + sine_squared(NZ)[None, None, :]
    pressure = jnp.real(jnp.fft.ifftn(-spectrum / (symbol + penalty)))
    gradient = jnp.stack([central(pressure, 0), central(pressure, 1), central(pressure, 2)])
    corrected_flow_vector = current - gradient
    blocks = heat.reshape(N_WIDE, XL, N_NARROW, YL, NZB, 128).transpose(0, 2, 1, 3, 4, 5).reshape(-1, 128)
    numbers = jnp.arange(N_WIDE * N_NARROW * HBLK, dtype=jnp.int32)
    narrow_of = numbers // HBLK % N_NARROW
    target = (source_owner_sheet[:, 0] * N_NARROW + narrow_of) * PR + source_part_line
    summed = jnp.zeros((N_WIDE * N_NARROW * PR, 128), jnp.float32).at[target].add(blocks)
    substrate_energy_input = summed.reshape(N_WIDE, N_NARROW, PZD, PYD, 128).transpose(0, 2, 1, 3, 4).reshape(SPAN_ALTITUDE, SPAN_BREADTH, SPAN_DEPTH)
    thermal_profile = substrate_warmth_excess + dissipation_factor * substrate_energy_input
    for section in range(STEPS):
        bordered_array = jnp.pad(thermal_profile, 1)
        neighbour_voxels = bordered_array[2:, 1:-1, 1:-1] + bordered_array[:-2, 1:-1, 1:-1]
        neighbour_voxels = neighbour_voxels + bordered_array[1:-1, 2:, 1:-1] + bordered_array[1:-1, :-2, 1:-1]
        neighbour_voxels = neighbour_voxels + bordered_array[1:-1, 1:-1, 2:] + bordered_array[1:-1, 1:-1, :-2]
        thermal_profile = thermal_profile + spread_coefficient * (neighbour_voxels - 6.0 * thermal_profile)
    return (corrected_flow_vector, thermal_profile)
```

```python
import math

import jax
import jax.numpy as jnp
import numpy as np
from jax import lax
from jax.experimental import pallas as pl
from jax.experimental.pallas import tpu as pltpu
from jax.sharding import PartitionSpec as P

PASSES = 2
STEPS = 3


time_step = 0.15
rate_base = 0.5
zener_energy = 4.0
stress_exponent = 5.0
penalty = 0.001
dissipation_factor = 0.1


def with_halo(x, sides, width, wrap):
    for axis, dim in sides:
        size, length = (lax.axis_size(axis), x.shape[dim])
        up = [(i, (i + 1) % size) for i in range(size if wrap else size - 1)]
        down = [(j, i) for i, j in up]
        last = lax.slice_in_dim(x, length - width, length, axis=dim)
        initial = lax.slice_in_dim(x, 0, width, axis=dim)
        before = lax.ppermute(last, axis, up)
        after = lax.ppermute(initial, axis, down)
        x = jnp.concatenate([before, x, after], axis=dim)
    return x


def pad_cells(field):
    return with_halo(field, (("wide", 1), ("narrow", 2)), 1, True)


def gradients(bordered_array):
    center = bordered_array[:, 1:-1, 1:-1]
    along_x = (bordered_array[:, 2:, 1:-1] - bordered_array[:, :-2, 1:-1]) * 0.5
    along_y = (bordered_array[:, 1:-1, 2:] - bordered_array[:, 1:-1, :-2]) * 0.5
    along_z = (jnp.roll(center, -1, 3) - jnp.roll(center, 1, 3)) * 0.5
    return (along_x, along_y, along_z)


def rate_squared(bordered_array):
    along_x, along_y, along_z = gradients(bordered_array)
    s_xy = 0.5 * (along_y[0] + along_x[1])
    s_xz = 0.5 * (along_z[0] + along_x[2])
    s_yz = 0.5 * (along_z[1] + along_y[2])
    total = (
        along_x[0] ** 2 + along_y[1] ** 2 + along_z[2] ** 2 + 2.0 * (s_xy**2 + s_xz**2 + s_yz**2)
    )
    return rate_base**2 + 2.0 * total


def inverse_sinh(value):
    return jnp.log(value + jnp.sqrt(value * value + 1.0))


def viscosity(rate_sq, zener):
    rate = jnp.sqrt(rate_sq)
    return inverse_sinh((rate * zener) ** (1.0 / stress_exponent)) / (3.0 * rate)


def viscous_term(mu_padded, vel_padded):
    mu_center = mu_padded[1:-1, 1:-1]
    vel_center = vel_padded[:, 1:-1, 1:-1]
    total = 0.5 * (mu_center + mu_padded[2:, 1:-1]) * (
        vel_padded[:, 2:, 1:-1] - vel_center
    ) - 0.5 * (mu_center + mu_padded[:-2, 1:-1]) * (vel_center - vel_padded[:, :-2, 1:-1])
    total = (
        total
        + 0.5 * (mu_center + mu_padded[1:-1, 2:]) * (vel_padded[:, 1:-1, 2:] - vel_center)
        - 0.5 * (mu_center + mu_padded[1:-1, :-2]) * (vel_center - vel_padded[:, 1:-1, :-2])
    )
    total = (
        total
        + 0.5
        * (mu_center + jnp.roll(mu_center, -1, 2))
        * (jnp.roll(vel_center, -1, 3) - vel_center)
        - 0.5 * (mu_center + jnp.roll(mu_center, 1, 2)) * (vel_center - jnp.roll(vel_center, 1, 3))
    )
    return total


def cosine_sine_basis(points, period, waves):
    columns, eigen = [], []
    for wave in waves:
        angle = 2.0 * np.pi * ((wave * np.arange(points)) % period) / period
        single = wave % period == 0 or 2 * wave == period
        size = math.sqrt((1.0 if single else 2.0) / period)
        columns.append(np.cos(angle) * size)
        eigen.append(math.sin(2.0 * math.pi * wave / period) ** 2)
        if not single:
            columns.append(np.sin(angle) * size)
            eigen.append(eigen[-1])
    return np.stack(columns, 1), np.array(eigen)


def halves(table):
    table = np.asarray(table, np.float32)
    high = table.astype(jnp.bfloat16)
    low = (table - high.astype(np.float32)).astype(jnp.bfloat16)
    return jnp.asarray(high), jnp.asarray(low)


def split(value):
    high = value.astype(jnp.bfloat16)
    return high, (value - high.astype(jnp.float32)).astype(jnp.bfloat16)


def triple_product(left, right):
    def product(one, two):
        return lax.dot_general(
            one, two, (((1,), (0,)), ((), ())), preferred_element_type=jnp.float32
        )

    return product(left[0], right[0]) + (product(left[0], right[1]) + product(left[1], right[0]))


def z_tables(z_cells):
    half = z_cells // 2
    even, eigen_even = cosine_sine_basis(half, z_cells, range(0, half + 1, 2))
    odd, eigen_odd = cosine_sine_basis(half, z_cells, range(1, half, 2))
    return even, odd, np.concatenate([eigen_even, eigen_odd])


def whole(*shape):
    return pl.BlockSpec(shape, lambda *index: (0,) * len(shape))


def z_forward(divergence, count):
    x_local, y_local, z_cells = divergence.shape
    half, piece = z_cells // 2, z_cells // count
    step = min(8, x_local)
    even, odd, _ = z_tables(z_cells)
    tables = halves(even) + halves(odd)

    def kernel(div_ref, even_high, even_low, odd_high, odd_low, out_ref):
        rows = div_ref[...].reshape(step * y_local, z_cells)
        first, second = rows[:, :half], rows[:, half:]
        modes = jnp.concatenate(
            [
                triple_product(split(first + second), (even_high[...], even_low[...])),
                triple_product(split(first - second), (odd_high[...], odd_low[...])),
            ],
            1,
        )
        for n in range(count):
            out_ref[n] = modes[:, n * piece : (n + 1) * piece].reshape(step, y_local, piece)

    return pl.pallas_call(
        kernel,
        grid=(x_local // step,),
        in_specs=[pl.BlockSpec((step, y_local, z_cells), lambda i: (i, 0, 0))]
        + [whole(half, half)] * 4,
        out_specs=pl.BlockSpec((count, step, y_local, piece), lambda i: (0, i, 0, 0)),
        out_shape=jax.ShapeDtypeStruct((count, x_local, y_local, piece), jnp.float32),
        name="z_forward",
    )(divergence, *tables)


def z_inverse(spectrum):
    count, planes, y_local, piece = spectrum.shape
    z_cells = count * piece
    half, step = z_cells // 2, planes // 2
    even, odd, _ = z_tables(z_cells)
    tables = halves(even.T) + halves(odd.T)

    def kernel(in_ref, even_high, even_low, odd_high, odd_low, out_ref):
        modes = jnp.concatenate(
            [in_ref[n].reshape(step * y_local, piece) for n in range(count)], 1
        )
        first = triple_product(split(modes[:, :half]), (even_high[...], even_low[...]))
        second = triple_product(split(modes[:, half:]), (odd_high[...], odd_low[...]))
        out_ref[...] = jnp.concatenate([first + second, first - second], 1).reshape(
            step, y_local, z_cells
        )

    return pl.pallas_call(
        kernel,
        grid=(planes // step,),
        in_specs=[pl.BlockSpec((count, step, y_local, piece), lambda i: (0, i, 0, 0))]
        + [whole(half, half)] * 4,
        out_specs=pl.BlockSpec((step, y_local, z_cells), lambda i: (i, 0, 0)),
        out_shape=jax.ShapeDtypeStruct((planes, y_local, z_cells), jnp.float32),
        name="z_inverse",
    )(spectrum, *tables)


def y_forward(spectrum, ratio, wide_count):
    count, x_local, y_local, piece = spectrum.shape
    y_cells = count * y_local
    share = y_cells // wide_count
    table, _ = cosine_sine_basis(y_cells, y_cells, range(y_cells // 2 + 1))
    tables = halves(table.T)

    def kernel(in_ref, high_ref, low_ref, ratio_ref, modes_ref, carry_ref, sums, power):
        @pl.when(pl.program_id(0) == 0)
        def _():
            sums[...] = jnp.zeros_like(sums)
            power[...] = jnp.ones_like(power)

        planes = [
            jnp.concatenate([in_ref[n, side] for n in range(count)], 0) for side in range(2)
        ]
        modes = triple_product(
            (high_ref[...], low_ref[...]), split(jnp.concatenate(planes, 1))
        )
        r, pw = ratio_ref[...], power[...]
        for side in range(2):
            plane = modes[:, side * piece : (side + 1) * piece]
            modes_ref[side] = plane
            sums[side] = plane + r * sums[side]
            sums[2 + side] = sums[2 + side] + pw * plane
        power[...] = pw * r

        @pl.when(pl.program_id(0) == x_local // 2 - 1)
        def _():
            for kind in range(4):
                carry_ref[:, kind] = sums[kind].reshape(wide_count, share, piece)

    return pl.pallas_call(
        kernel,
        grid=(x_local // 2,),
        in_specs=[
            pl.BlockSpec((count, 2, y_local, piece), lambda i: (0, i, 0, 0)),
            whole(y_cells, y_cells),
            whole(y_cells, y_cells),
            whole(y_cells, piece),
        ],
        out_specs=[
            pl.BlockSpec((2, y_cells, piece), lambda i: (i, 0, 0)),
            whole(wide_count, 4, share, piece),
        ],
        out_shape=[
            jax.ShapeDtypeStruct((x_local, y_cells, piece), jnp.float32),
            jax.ShapeDtypeStruct((wide_count, 4, share, piece), jnp.float32),
        ],
        scratch_shapes=[
            pltpu.VMEM((4, y_cells, piece), jnp.float32),
            pltpu.VMEM((y_cells, piece), jnp.float32),
        ],
        name="y_forward",
    )(spectrum, *tables, ratio)


def power_of(value, exponent):
    result = None
    while exponent:
        if exponent & 1:
            result = value if result is None else result * value
        value = value * value
        exponent >>= 1
    return result


def join_carries(carries, ratio, block):
    count, kinds, share, piece = carries.shape

    def kernel(in_ref, ratio_ref, out_ref):
        step = power_of(ratio_ref[...], block)
        scale = 1.0 / (1.0 - power_of(step, count))
        for kind in range(kinds):
            order = list(range(count)) if kind < 2 else list(range(count))[::-1]
            total = in_ref[order[0], kind]
            for w in order[1:]:
                total = in_ref[w, kind] + step * total
            total = total * scale
            for w in order:
                out_ref[w, kind] = total
                total = in_ref[w, kind] + step * total

    return pl.pallas_call(
        kernel,
        out_shape=jax.ShapeDtypeStruct(carries.shape, jnp.float32),
        name="join_carries",
    )(carries, ratio)


def y_inverse(modes, carries, ratio, gain, count):
    x_local, y_cells, piece = modes.shape
    y_local, pairs = y_cells // count, x_local // 2
    wide_count, _, share, _ = carries.shape
    table, _ = cosine_sine_basis(y_cells, y_cells, range(y_cells // 2 + 1))
    tables = halves(table)

    def kernel(modes_ref, carry_ref, high_ref, low_ref, ratio_ref, gain_ref, out_ref, behind, ahead):
        step = pl.program_id(0)
        r = ratio_ref[...]

        def carry(kind):
            return carry_ref[:, kind].reshape(y_cells, piece)

        @pl.when(step == 0)
        def _():
            ahead[0] = carry(0)
            ahead[1] = carry(1)
            behind[2 * pairs + 1] = carry(2)

            def back(i, state):
                even, odd = state
                m = pairs - 1 - i
                behind[2 * m + 2] = r * odd
                behind[2 * m + 1] = r * even
                return (
                    modes_ref[2 * m] + r * even,
                    modes_ref[2 * m + 1] + r * odd,
                )

            _, odd = lax.fori_loop(0, pairs, back, (carry(2), carry(3)))
            behind[0] = r * odd

        even_plane = modes_ref[jnp.minimum(2 * step, x_local - 2)]
        odd_plane = modes_ref[jnp.maximum(2 * step - 1, 1)]
        even = r * ahead[0] + jnp.where(step < pairs, even_plane, 0.0)
        odd = jnp.where(step > 0, odd_plane + r * ahead[1], ahead[1])
        ahead[0] = even
        ahead[1] = odd
        gain_value = gain_ref[...]
        planes = jnp.concatenate(
            [gain_value * (odd + behind[2 * step]), gain_value * (even + behind[2 * step + 1])], 1
        )
        cells = triple_product((high_ref[...], low_ref[...]), split(planes))
        for n in range(count):
            for side in range(2):
                out_ref[n, side] = cells[
                    n * y_local : (n + 1) * y_local, side * piece : (side + 1) * piece
                ]

    return pl.pallas_call(
        kernel,
        grid=(pairs + 1,),
        in_specs=[
            whole(x_local, y_cells, piece),
            whole(wide_count, 4, share, piece),
            whole(y_cells, y_cells),
            whole(y_cells, y_cells),
            whole(y_cells, piece),
            whole(y_cells, piece),
        ],
        out_specs=pl.BlockSpec((count, 2, y_local, piece), lambda i: (0, i, 0, 0)),
        out_shape=jax.ShapeDtypeStruct((count, x_local + 2, y_local, piece), jnp.float32),
        scratch_shapes=[
            pltpu.VMEM((x_local + 2, y_cells, piece), jnp.float32),
            pltpu.VMEM((2, y_cells, piece), jnp.float32),
        ],
        name="y_inverse",
    )(modes, carries, *tables, ratio, gain)


def turn(value, axis):
    return lax.all_to_all(value, axis, split_axis=0, concat_axis=0, tiled=True)


def project(spectrum):
    count, x_local, y_local, piece = spectrum.shape
    y_cells, z_cells = count * y_local, count * piece
    wide_count = lax.axis_size("wide")
    _, eigen_y = cosine_sine_basis(y_cells, y_cells, range(y_cells // 2 + 1))
    eigen_z = jnp.asarray(z_tables(z_cells)[2], jnp.float32)
    own_z = lax.dynamic_slice_in_dim(eigen_z, lax.axis_index("narrow") * piece, piece)
    excess = 4.0 * (jnp.asarray(eigen_y, jnp.float32)[:, None] + own_z[None, :] + penalty)
    root = jnp.sqrt(excess * (4.0 + excess))
    ratio = 2.0 / (2.0 + excess + root)
    gain = -4.0 / root
    share = y_cells // wide_count
    own_ratio = lax.dynamic_slice_in_dim(ratio, lax.axis_index("wide") * share, share)
    modes, carries = y_forward(turn(spectrum, "narrow"), ratio, wide_count)
    carries = turn(join_carries(turn(carries, "wide"), own_ratio, x_local // 2), "wide")
    return z_inverse(turn(y_inverse(modes, carries, ratio, gain, count), "narrow"))


def ring(value_up, value_down, axis):
    size = lax.axis_size(axis)
    up = [(i, (i + 1) % size) for i in range(size)]
    down = [(j, i) for i, j in up]
    return lax.ppermute(value_up, axis, up), lax.ppermute(value_down, axis, down)


def substrate_advance(thermal_profile, spread_coefficient):
    bordered_array = with_halo(thermal_profile, (("wide", 0), ("narrow", 1)), 1, False)
    center = bordered_array[1:-1, 1:-1]
    neighbour_voxels = (
        bordered_array[2:, 1:-1]
        + bordered_array[:-2, 1:-1]
        + bordered_array[1:-1, 2:]
        + bordered_array[1:-1, :-2]
    )
    ahead = jnp.pad(center[:, :, 1:], ((0, 0), (0, 0), (0, 1)))
    behind = jnp.pad(center[:, :, :-1], ((0, 0), (0, 0), (1, 0)))
    return center + spread_coefficient * (neighbour_voxels + ahead + behind - 6.0 * center)


def per_device(
    material_flow_vector,
    tool_push_density,
    tool_warmth_excess,
    substrate_warmth_excess,
    spread_coefficient,
    source_owner_sheet,
    source_part_line,
):
    zener = jnp.exp(zener_energy * (1.0 / tool_warmth_excess - 1.0))
    base_pad = pad_cells(material_flow_vector)
    current_pad = base_pad
    current = material_flow_vector
    for section in range(PASSES):
        rate_sq = rate_squared(current_pad)
        mu_field = viscosity(rate_sq, zener)
        mu_padded = pad_cells(mu_field[None])[0]
        current = material_flow_vector + time_step * (
            viscous_term(mu_padded, base_pad) + tool_push_density
        )
        if section + 1 < PASSES:
            current_pad = pad_cells(current)
    heat_cells = mu_field * (rate_sq - rate_base**2)
    along_x, along_y, along_z = gradients(pad_cells(current))
    divergence = along_x[0] + along_y[1] + along_z[2]
    pressure = project(z_forward(divergence, lax.axis_size("narrow")))
    inner = pressure[1:-1]
    below, above = ring(inner[:, -1:], inner[:, :1], "narrow")
    tall = jnp.concatenate([below, inner, above], 1)
    press_x = (pressure[2:] - pressure[:-2]) * 0.5
    press_y = (tall[:, 2:] - tall[:, :-2]) * 0.5
    press_z = (jnp.roll(inner, -1, 2) - jnp.roll(inner, 1, 2)) * 0.5
    corrected_flow_vector = current - jnp.stack([press_x, press_y, press_z], 0)
    blocks = heat_cells.reshape(-1, 128)
    slab_ids = source_owner_sheet[:, 0]
    slab_count = lax.axis_size("wide")
    component_lines = substrate_warmth_excess.shape[0] * substrate_warmth_excess.shape[1]
    partial_value = (
        jnp.zeros((slab_count * component_lines, 128), jnp.float32)
        .at[slab_ids * component_lines + source_part_line]
        .add(blocks)
    )
    substrate_energy_input = lax.psum_scatter(
        partial_value.reshape(slab_count, component_lines, 128),
        "wide",
        scatter_dimension=0,
        tiled=True,
    )
    thermal_profile = substrate_warmth_excess + dissipation_factor * substrate_energy_input.reshape(
        substrate_warmth_excess.shape
    )
    for section in range(STEPS):
        thermal_profile = substrate_advance(thermal_profile, spread_coefficient)
    return (corrected_flow_vector, thermal_profile)


def solution(mesh):
    return jax.shard_map(
        per_device,
        mesh=mesh,
        in_specs=(
            P(None, "wide", "narrow", None),
            P(None, "wide", "narrow", None),
            P("wide", "narrow", None),
            P("wide", "narrow", None),
            P("wide", "narrow", None),
            P(("wide", "narrow"), None),
            P(("wide", "narrow")),
        ),
        out_specs=(P(None, "wide", "narrow", None), P("wide", "narrow", None)),
        check_vma=False,
    )
```

```python
import math

import jax
import jax.numpy as jnp
import numpy as np
from jax import lax
from jax.experimental import pallas as pl
from jax.experimental.pallas import tpu as pltpu
from jax.sharding import PartitionSpec as P

PASSES = 2
STEPS = 3


time_step = 0.15
rate_base = 0.5
zener_energy = 4.0
stress_exponent = 5.0
penalty = 0.001
dissipation_factor = 0.1


def with_halo(x, sides, width, wrap):
    for axis, dim in sides:
        size, length = (lax.axis_size(axis), x.shape[dim])
        up = [(i, (i + 1) % size) for i in range(size if wrap else size - 1)]
        down = [(j, i) for i, j in up]
        last = lax.slice_in_dim(x, length - width, length, axis=dim)
        initial = lax.slice_in_dim(x, 0, width, axis=dim)
        before = lax.ppermute(last, axis, up)
        after = lax.ppermute(initial, axis, down)
        x = jnp.concatenate([before, x, after], axis=dim)
    return x


def ring(value, axis, dim):
    size, length = lax.axis_size(axis), value.shape[dim]
    up = [(i, (i + 1) % size) for i in range(size)]
    down = [(j, i) for i, j in up]
    last = lax.slice_in_dim(value, length - 1, length, axis=dim)
    initial = lax.slice_in_dim(value, 0, 1, axis=dim)
    return lax.ppermute(last, axis, up), lax.ppermute(initial, axis, down)


def row_numbers(width):
    return lax.broadcasted_iota(jnp.int32, (8, width), 0)


def rows_of(strip):
    return pl.ds(8 * strip, 8)


def ahead_row(strip, value, take, edge, strips, rows):
    following = take(8 * strip + 8) if strip + 1 < strips else edge
    return jnp.where(rows == 7, following, pltpu.roll(value, 7, 0))


def behind_row(strip, value, take, edge, rows):
    previous = take(8 * strip - 1) if strip else edge
    return jnp.where(rows == 0, previous, pltpu.roll(value, 1, 0))


def plane_copies(source, low, high, target, semaphores, count):
    def pick(ref, index):
        return ref.at[:, index] if len(ref.shape) == 4 else ref.at[index]

    def start_all():
        pltpu.make_async_copy(pick(low, 0), pick(target, 0), semaphores.at[0]).start()

        def body(i, state):
            pltpu.make_async_copy(
                pick(source, i), pick(target, i + 1), semaphores.at[i + 1]
            ).start()
            return state

        lax.fori_loop(0, count, body, 0)
        pltpu.make_async_copy(
            pick(high, 0), pick(target, count + 1), semaphores.at[count + 1]
        ).start()

    def wait(index):
        pltpu.make_async_copy(pick(low, 0), pick(target, index), semaphores.at[index]).wait()

    return start_all, wait


def await_planes(wait, step, planes):
    @pl.when(step == 0)
    def _():
        wait(0)
        wait(1)

    for i in range(planes):
        wait(step * planes + i + 2)


anywhere = pl.BlockSpec(memory_space=pl.ANY)


def viscosity_kernel_call(flow, x_sides, y_sides, warmth, with_heat):
    _, x_local, y_local, z_cells = flow.shape
    planes, strips, z_blocks = 2, y_local // 8, z_cells // 128

    def kernel(flow_ref, low_ref, high_ref, before_ref, after_ref, warmth_ref, *rest):
        outs, (cells, semaphores) = rest[:-2], rest[-2:]
        step = pl.program_id(0)
        start_all, wait = plane_copies(flow_ref, low_ref, high_ref, cells, semaphores, x_local)
        pl.when(step == 0)(start_all)
        await_planes(wait, step, planes)
        rows = row_numbers(z_cells)

        def plane(i, state):
            j = step * planes + i
            for s in range(strips):
                along_x, along_y, along_z = [], [], []
                for c in range(3):
                    value = cells[c, j + 1, rows_of(s), :]

                    def take(row):
                        return cells[c, j + 1, pl.ds(row, 1), :]

                    along_x.append(cells[c, j + 2, rows_of(s), :] - cells[c, j, rows_of(s), :])
                    along_y.append(
                        ahead_row(s, value, take, after_ref[c, i], strips, rows)
                        - behind_row(s, value, take, before_ref[c, i], rows)
                    )
                    along_z.append(
                        pltpu.roll(value, z_cells - 1, 1) - pltpu.roll(value, 1, 1)
                    )
                s_xy = along_y[0] + along_x[1]
                s_xz = along_z[0] + along_x[2]
                s_yz = along_z[1] + along_y[2]
                extra = 0.5 * (
                    along_x[0] * along_x[0] + along_y[1] * along_y[1] + along_z[2] * along_z[2]
                ) + 0.25 * (s_xy * s_xy + s_xz * s_xz + s_yz * s_yz)
                rate_sq = rate_base**2 + extra
                value = jnp.exp(
                    (0.5 / stress_exponent) * jnp.log(rate_sq)
                    + (zener_energy / stress_exponent)
                    * (1.0 / warmth_ref[i, rows_of(s), :] - 1.0)
                )
                mu = (
                    jnp.log(value + jnp.sqrt(value * value + 1.0))
                    * lax.rsqrt(rate_sq)
                    * (1.0 / 3.0)
                )
                outs[0][i, rows_of(s), :] = mu
                if with_heat:
                    heat = mu * (rate_sq - rate_base**2)
                    for b in range(z_blocks):
                        outs[1][b, i, rows_of(s), :] = heat[:, b * 128 : (b + 1) * 128]
            return state

        lax.fori_loop(0, planes, plane, 0)

    row_spec = pl.BlockSpec((3, planes, 1, z_cells), lambda i: (0, i, 0, 0))
    cell_spec = pl.BlockSpec((planes, y_local, z_cells), lambda i: (i, 0, 0))
    out_specs = [cell_spec]
    out_shape = [jax.ShapeDtypeStruct((x_local, y_local, z_cells), jnp.float32)]
    if with_heat:
        out_specs.append(pl.BlockSpec((z_blocks, planes, y_local, 128), lambda i: (0, i, 0, 0)))
        out_shape.append(jax.ShapeDtypeStruct((z_blocks, x_local, y_local, 128), jnp.float32))
    return pl.pallas_call(
        kernel,
        grid=(x_local // planes,),
        in_specs=[anywhere] * 3 + [row_spec, row_spec, cell_spec],
        out_specs=out_specs,
        out_shape=out_shape,
        scratch_shapes=[
            pltpu.VMEM((3, x_local + 2, y_local, z_cells), jnp.float32),
            pltpu.SemaphoreType.DMA((x_local + 2,)),
        ],
        name="viscosity",
    )(flow, *x_sides, *y_sides, warmth)


def advance_kernel_call(flow, flow_x, flow_y, mu, mu_x, mu_y, push):
    _, x_local, y_local, z_cells = flow.shape
    planes, strips = 2, y_local // 8

    def kernel(
        flow_ref, flow_low, flow_high, flow_before, flow_after,
        mu_ref, mu_low, mu_high, mu_before, mu_after, push_ref,
        out_ref, cells, semaphores, mu_cells, mu_semaphores,
    ):
        step = pl.program_id(0)
        start_flow, wait_flow = plane_copies(
            flow_ref, flow_low, flow_high, cells, semaphores, x_local
        )
        start_mu, wait_mu = plane_copies(
            mu_ref, mu_low, mu_high, mu_cells, mu_semaphores, x_local
        )

        @pl.when(step == 0)
        def _():
            start_mu()
            start_flow()

        await_planes(wait_mu, step, planes)
        await_planes(wait_flow, step, planes)
        rows = row_numbers(z_cells)

        def plane(i, state):
            j = step * planes + i
            for s in range(strips):
                m = mu_cells[j + 1, rows_of(s), :]

                def take_mu(row):
                    return mu_cells[j + 1, pl.ds(row, 1), :]

                sum_x_ahead = m + mu_cells[j + 2, rows_of(s), :]
                sum_x_behind = m + mu_cells[j, rows_of(s), :]
                sum_y_ahead = m + ahead_row(s, m, take_mu, mu_after[i], strips, rows)
                sum_y_behind = m + behind_row(s, m, take_mu, mu_before[i], rows)
                sum_z_ahead = m + pltpu.roll(m, z_cells - 1, 1)
                for c in range(3):
                    value = cells[c, j + 1, rows_of(s), :]

                    def take(row):
                        return cells[c, j + 1, pl.ds(row, 1), :]

                    flux_z = sum_z_ahead * (pltpu.roll(value, z_cells - 1, 1) - value)
                    total = (
                        sum_x_ahead * (cells[c, j + 2, rows_of(s), :] - value)
                        - sum_x_behind * (value - cells[c, j, rows_of(s), :])
                        + sum_y_ahead
                        * (ahead_row(s, value, take, flow_after[c, i], strips, rows) - value)
                        - sum_y_behind
                        * (value - behind_row(s, value, take, flow_before[c, i], rows))
                        + (flux_z - pltpu.roll(flux_z, 1, 1))
                    )
                    out_ref[c, i, rows_of(s), :] = value + time_step * (
                        0.5 * total + push_ref[c, i, rows_of(s), :]
                    )
            return state

        lax.fori_loop(0, planes, plane, 0)

    row_spec = pl.BlockSpec((3, planes, 1, z_cells), lambda i: (0, i, 0, 0))
    mu_row_spec = pl.BlockSpec((planes, 1, z_cells), lambda i: (i, 0, 0))
    block = pl.BlockSpec((3, planes, y_local, z_cells), lambda i: (0, i, 0, 0))
    return pl.pallas_call(
        kernel,
        grid=(x_local // planes,),
        in_specs=[anywhere] * 3
        + [row_spec, row_spec]
        + [anywhere] * 3
        + [mu_row_spec, mu_row_spec, block],
        out_specs=block,
        out_shape=jax.ShapeDtypeStruct(flow.shape, jnp.float32),
        scratch_shapes=[
            pltpu.VMEM((3, x_local + 2, y_local, z_cells), jnp.float32),
            pltpu.SemaphoreType.DMA((x_local + 2,)),
            pltpu.VMEM((x_local + 2, y_local, z_cells), jnp.float32),
            pltpu.SemaphoreType.DMA((x_local + 2,)),
        ],
        name="advance",
    )(flow, *flow_x, *flow_y, mu, *mu_x, *mu_y, push)


def cosine_sine_basis(points, period, waves):
    columns, eigen = [], []
    for wave in waves:
        angle = 2.0 * np.pi * ((wave * np.arange(points)) % period) / period
        single = wave % period == 0 or 2 * wave == period
        size = math.sqrt((1.0 if single else 2.0) / period)
        columns.append(np.cos(angle) * size)
        eigen.append(math.sin(2.0 * math.pi * wave / period) ** 2)
        if not single:
            columns.append(np.sin(angle) * size)
            eigen.append(eigen[-1])
    return np.stack(columns, 1), np.array(eigen)


def halves(table):
    table = np.asarray(table, np.float32)
    high = table.astype(jnp.bfloat16)
    low = (table - high.astype(np.float32)).astype(jnp.bfloat16)
    return jnp.asarray(high), jnp.asarray(low)


def split(value):
    high = value.astype(jnp.bfloat16)
    return high, (value - high.astype(jnp.float32)).astype(jnp.bfloat16)


def triple_product(left, right):
    def product(one, two):
        return lax.dot_general(
            one, two, (((1,), (0,)), ((), ())), preferred_element_type=jnp.float32
        )

    return product(left[0], right[0]) + (product(left[0], right[1]) + product(left[1], right[0]))


def z_tables(z_cells):
    half = z_cells // 2
    even, eigen_even = cosine_sine_basis(half, z_cells, range(0, half + 1, 2))
    odd, eigen_odd = cosine_sine_basis(half, z_cells, range(1, half, 2))
    return even, odd, np.concatenate([eigen_even, eigen_odd])


def whole(*shape):
    return pl.BlockSpec(shape, lambda *index: (0,) * len(shape))


def divergence_modes(flow, x_sides, y_sides, count):
    _, x_local, y_local, z_cells = flow.shape
    half, piece, strips = z_cells // 2, z_cells // count, y_local // 8
    step = min(8, x_local)
    even, odd, _ = z_tables(z_cells)
    tables = halves(even) + halves(odd)

    def kernel(
        first_ref, low_ref, high_ref, second_ref, before_ref, after_ref, third_ref,
        even_high, even_low, odd_high, odd_low, out_ref, cells, semaphores, work,
    ):
        start_all, wait = plane_copies(
            first_ref.at[0], low_ref, high_ref, cells, semaphores, x_local
        )
        grid_step = pl.program_id(0)
        pl.when(grid_step == 0)(start_all)
        await_planes(wait, grid_step, step)
        rows = row_numbers(z_cells)

        def plane(i, state):
            j = grid_step * step + i
            for s in range(strips):
                value = second_ref[0, i, rows_of(s), :]

                def take(row):
                    return second_ref[0, i, pl.ds(row, 1), :]

                along = third_ref[0, i, rows_of(s), :]
                work[i, rows_of(s), :] = 0.5 * (
                    (cells[j + 2, rows_of(s), :] - cells[j, rows_of(s), :])
                    + (
                        ahead_row(s, value, take, after_ref[i], strips, rows)
                        - behind_row(s, value, take, before_ref[i], rows)
                    )
                    + (pltpu.roll(along, z_cells - 1, 1) - pltpu.roll(along, 1, 1))
                )
            return state

        lax.fori_loop(0, step, plane, 0)
        lines = work[...].reshape(step * y_local, z_cells)
        first, second = lines[:, :half], lines[:, half:]
        modes = jnp.concatenate(
            [
                triple_product(split(first + second), (even_high[...], even_low[...])),
                triple_product(split(first - second), (odd_high[...], odd_low[...])),
            ],
            1,
        )
        for n in range(count):
            out_ref[n] = modes[:, n * piece : (n + 1) * piece].reshape(step, y_local, piece)

    row_spec = pl.BlockSpec((step, 1, z_cells), lambda i: (i, 0, 0))
    return pl.pallas_call(
        kernel,
        grid=(x_local // step,),
        in_specs=[
            anywhere,
            anywhere,
            anywhere,
            pl.BlockSpec((1, step, y_local, z_cells), lambda i: (1, i, 0, 0)),
            row_spec,
            row_spec,
            pl.BlockSpec((1, step, y_local, z_cells), lambda i: (2, i, 0, 0)),
        ]
        + [whole(half, half)] * 4,
        out_specs=pl.BlockSpec((count, step, y_local, piece), lambda i: (0, i, 0, 0)),
        out_shape=jax.ShapeDtypeStruct((count, x_local, y_local, piece), jnp.float32),
        scratch_shapes=[
            pltpu.VMEM((x_local + 2, y_local, z_cells), jnp.float32),
            pltpu.SemaphoreType.DMA((x_local + 2,)),
            pltpu.VMEM((step, y_local, z_cells), jnp.float32),
        ],
        name="divergence_modes",
    )(flow, *x_sides, flow, *y_sides, flow, *tables)


def z_inverse(spectrum):
    count, planes, y_local, piece = spectrum.shape
    z_cells = count * piece
    half, step = z_cells // 2, planes // 2
    even, odd, _ = z_tables(z_cells)
    tables = halves(even.T) + halves(odd.T)

    def kernel(in_ref, even_high, even_low, odd_high, odd_low, out_ref):
        modes = jnp.concatenate(
            [in_ref[n].reshape(step * y_local, piece) for n in range(count)], 1
        )
        first = triple_product(split(modes[:, :half]), (even_high[...], even_low[...]))
        second = triple_product(split(modes[:, half:]), (odd_high[...], odd_low[...]))
        out_ref[...] = jnp.concatenate([first + second, first - second], 1).reshape(
            step, y_local, z_cells
        )

    return pl.pallas_call(
        kernel,
        grid=(planes // step,),
        in_specs=[pl.BlockSpec((count, step, y_local, piece), lambda i: (0, i, 0, 0))]
        + [whole(half, half)] * 4,
        out_specs=pl.BlockSpec((step, y_local, z_cells), lambda i: (i, 0, 0)),
        out_shape=jax.ShapeDtypeStruct((planes, y_local, z_cells), jnp.float32),
        name="z_inverse",
    )(spectrum, *tables)


def y_forward(spectrum, ratio, wide_count):
    count, x_local, y_local, piece = spectrum.shape
    y_cells = count * y_local
    share = y_cells // wide_count
    table, _ = cosine_sine_basis(y_cells, y_cells, range(y_cells // 2 + 1))
    tables = halves(table.T)

    def kernel(in_ref, high_ref, low_ref, ratio_ref, modes_ref, carry_ref, sums, power):
        @pl.when(pl.program_id(0) == 0)
        def _():
            sums[...] = jnp.zeros_like(sums)
            power[...] = jnp.ones_like(power)

        planes = [
            jnp.concatenate([in_ref[n, side] for n in range(count)], 0) for side in range(2)
        ]
        modes = triple_product(
            (high_ref[...], low_ref[...]), split(jnp.concatenate(planes, 1))
        )
        r, pw = ratio_ref[...], power[...]
        for side in range(2):
            plane = modes[:, side * piece : (side + 1) * piece]
            modes_ref[side] = plane
            sums[side] = plane + r * sums[side]
            sums[2 + side] = sums[2 + side] + pw * plane
        power[...] = pw * r

        @pl.when(pl.program_id(0) == x_local // 2 - 1)
        def _():
            for kind in range(4):
                carry_ref[:, kind] = sums[kind].reshape(wide_count, share, piece)

    return pl.pallas_call(
        kernel,
        grid=(x_local // 2,),
        in_specs=[
            pl.BlockSpec((count, 2, y_local, piece), lambda i: (0, i, 0, 0)),
            whole(y_cells, y_cells),
            whole(y_cells, y_cells),
            whole(y_cells, piece),
        ],
        out_specs=[
            pl.BlockSpec((2, y_cells, piece), lambda i: (i, 0, 0)),
            whole(wide_count, 4, share, piece),
        ],
        out_shape=[
            jax.ShapeDtypeStruct((x_local, y_cells, piece), jnp.float32),
            jax.ShapeDtypeStruct((wide_count, 4, share, piece), jnp.float32),
        ],
        scratch_shapes=[
            pltpu.VMEM((4, y_cells, piece), jnp.float32),
            pltpu.VMEM((y_cells, piece), jnp.float32),
        ],
        name="y_forward",
    )(spectrum, *tables, ratio)


def power_of(value, exponent):
    result = None
    while exponent:
        if exponent & 1:
            result = value if result is None else result * value
        value = value * value
        exponent >>= 1
    return result


def join_carries(carries, ratio, block):
    count, kinds, share, piece = carries.shape

    def kernel(in_ref, ratio_ref, out_ref):
        step = power_of(ratio_ref[...], block)
        scale = 1.0 / (1.0 - power_of(step, count))
        for kind in range(kinds):
            order = list(range(count)) if kind < 2 else list(range(count))[::-1]
            total = in_ref[order[0], kind]
            for w in order[1:]:
                total = in_ref[w, kind] + step * total
            total = total * scale
            for w in order:
                out_ref[w, kind] = total
                total = in_ref[w, kind] + step * total

    return pl.pallas_call(
        kernel,
        out_shape=jax.ShapeDtypeStruct(carries.shape, jnp.float32),
        name="join_carries",
    )(carries, ratio)


def y_inverse(modes, carries, ratio, gain, count):
    x_local, y_cells, piece = modes.shape
    y_local, pairs = y_cells // count, x_local // 2
    wide_count, _, share, _ = carries.shape
    table, _ = cosine_sine_basis(y_cells, y_cells, range(y_cells // 2 + 1))
    tables = halves(table)

    def kernel(modes_ref, carry_ref, high_ref, low_ref, ratio_ref, gain_ref, out_ref, behind, ahead):
        step = pl.program_id(0)
        r = ratio_ref[...]

        def carry(kind):
            return carry_ref[:, kind].reshape(y_cells, piece)

        @pl.when(step == 0)
        def _():
            ahead[0] = carry(0)
            ahead[1] = carry(1)
            behind[2 * pairs + 1] = carry(2)

            def back(i, state):
                even, odd = state
                m = pairs - 1 - i
                behind[2 * m + 2] = r * odd
                behind[2 * m + 1] = r * even
                return (
                    modes_ref[2 * m] + r * even,
                    modes_ref[2 * m + 1] + r * odd,
                )

            _, odd = lax.fori_loop(0, pairs, back, (carry(2), carry(3)))
            behind[0] = r * odd

        even_plane = modes_ref[jnp.minimum(2 * step, x_local - 2)]
        odd_plane = modes_ref[jnp.maximum(2 * step - 1, 1)]
        even = r * ahead[0] + jnp.where(step < pairs, even_plane, 0.0)
        odd = jnp.where(step > 0, odd_plane + r * ahead[1], ahead[1])
        ahead[0] = even
        ahead[1] = odd
        gain_value = gain_ref[...]
        planes = jnp.concatenate(
            [gain_value * (odd + behind[2 * step]), gain_value * (even + behind[2 * step + 1])], 1
        )
        cells = triple_product((high_ref[...], low_ref[...]), split(planes))
        for n in range(count):
            for side in range(2):
                out_ref[n, side] = cells[
                    n * y_local : (n + 1) * y_local, side * piece : (side + 1) * piece
                ]

    return pl.pallas_call(
        kernel,
        grid=(pairs + 1,),
        in_specs=[
            whole(x_local, y_cells, piece),
            whole(wide_count, 4, share, piece),
            whole(y_cells, y_cells),
            whole(y_cells, y_cells),
            whole(y_cells, piece),
            whole(y_cells, piece),
        ],
        out_specs=pl.BlockSpec((count, 2, y_local, piece), lambda i: (0, i, 0, 0)),
        out_shape=jax.ShapeDtypeStruct((count, x_local + 2, y_local, piece), jnp.float32),
        scratch_shapes=[
            pltpu.VMEM((x_local + 2, y_cells, piece), jnp.float32),
            pltpu.VMEM((2, y_cells, piece), jnp.float32),
        ],
        name="y_inverse",
    )(modes, carries, *tables, ratio, gain)


def turn(value, axis):
    return lax.all_to_all(value, axis, split_axis=0, concat_axis=0, tiled=True)


def project(spectrum):
    count, x_local, y_local, piece = spectrum.shape
    y_cells, z_cells = count * y_local, count * piece
    wide_count = lax.axis_size("wide")
    _, eigen_y = cosine_sine_basis(y_cells, y_cells, range(y_cells // 2 + 1))
    eigen_z = jnp.asarray(z_tables(z_cells)[2], jnp.float32)
    own_z = lax.dynamic_slice_in_dim(eigen_z, lax.axis_index("narrow") * piece, piece)
    excess = 4.0 * (jnp.asarray(eigen_y, jnp.float32)[:, None] + own_z[None, :] + penalty)
    root = jnp.sqrt(excess * (4.0 + excess))
    ratio = 2.0 / (2.0 + excess + root)
    gain = -4.0 / root
    share = y_cells // wide_count
    own_ratio = lax.dynamic_slice_in_dim(ratio, lax.axis_index("wide") * share, share)
    modes, carries = y_forward(turn(spectrum, "narrow"), ratio, wide_count)
    carries = turn(join_carries(turn(carries, "wide"), own_ratio, x_local // 2), "wide")
    return z_inverse(turn(y_inverse(modes, carries, ratio, gain, count), "narrow"))


def correct(flow, pressure, y_sides):
    _, x_local, y_local, z_cells = flow.shape
    planes, strips = 2, y_local // 8

    def kernel(flow_ref, pressure_ref, before_ref, after_ref, out_ref):
        step = pl.program_id(0)
        rows = row_numbers(z_cells)

        def plane(i, state):
            j = step * planes + i
            for s in range(strips):
                value = pressure_ref[j + 1, rows_of(s), :]

                def take(row):
                    return pressure_ref[j + 1, pl.ds(row, 1), :]

                slopes = (
                    pressure_ref[j + 2, rows_of(s), :] - pressure_ref[j, rows_of(s), :],
                    ahead_row(s, value, take, after_ref[i], strips, rows)
                    - behind_row(s, value, take, before_ref[i], rows),
                    pltpu.roll(value, z_cells - 1, 1) - pltpu.roll(value, 1, 1),
                )
                for c in range(3):
                    out_ref[c, i, rows_of(s), :] = flow_ref[c, i, rows_of(s), :] - 0.5 * slopes[c]
            return state

        lax.fori_loop(0, planes, plane, 0)

    row_spec = pl.BlockSpec((planes, 1, z_cells), lambda i: (i, 0, 0))
    block = pl.BlockSpec((3, planes, y_local, z_cells), lambda i: (0, i, 0, 0))
    return pl.pallas_call(
        kernel,
        grid=(x_local // planes,),
        in_specs=[block, whole(x_local + 2, y_local, z_cells), row_spec, row_spec],
        out_specs=block,
        out_shape=jax.ShapeDtypeStruct(flow.shape, jnp.float32),
        name="correct",
    )(flow, pressure, *y_sides)


def conduct(profile, spread):
    sides = (("wide", 0), ("narrow", 1))
    spread = with_halo(spread, sides, STEPS - 1, False)
    profile = with_halo(profile, sides, STEPS, False)
    for step in range(STEPS):
        center = profile[1:-1, 1:-1]
        near = (
            profile[2:, 1:-1] + profile[:-2, 1:-1] + profile[1:-1, 2:] + profile[1:-1, :-2]
        )
        ahead = jnp.pad(center[:, :, 1:], ((0, 0), (0, 0), (0, 1)))
        behind = jnp.pad(center[:, :, :-1], ((0, 0), (0, 0), (1, 0)))
        profile = center + spread * (near + ahead + behind - 6.0 * center)
        spread = spread[1:-1, 1:-1]
    return profile


def per_device(
    material_flow_vector,
    tool_push_density,
    tool_warmth_excess,
    substrate_warmth_excess,
    spread_coefficient,
    source_owner_sheet,
    source_part_line,
):
    flow_x = ring(material_flow_vector, "wide", 1)
    flow_y = ring(material_flow_vector, "narrow", 2)
    current, current_x, current_y = material_flow_vector, flow_x, flow_y
    for section in range(PASSES):
        last = section + 1 == PASSES
        fields = viscosity_kernel_call(current, current_x, current_y, tool_warmth_excess, last)
        mu_field = fields[0]
        current = advance_kernel_call(
            material_flow_vector,
            flow_x,
            flow_y,
            mu_field,
            ring(mu_field, "wide", 0),
            ring(mu_field, "narrow", 1),
            tool_push_density,
        )
        if not last:
            current_x = ring(current, "wide", 1)
            current_y = ring(current, "narrow", 2)
    heat_cells = fields[1]
    modes = divergence_modes(
        current,
        ring(current[0], "wide", 0),
        ring(current[1], "narrow", 1),
        lax.axis_size("narrow"),
    )
    pressure = project(modes)
    corrected_flow_vector = correct(current, pressure, ring(pressure[1:-1], "narrow", 1))
    z_blocks = heat_cells.shape[0]
    slab_count = lax.axis_size("wide")
    component_lines = substrate_warmth_excess.shape[0] * substrate_warmth_excess.shape[1]
    targets = source_owner_sheet[:, 0] * component_lines + source_part_line
    partial_value = (
        jnp.zeros((slab_count * component_lines, 128), jnp.float32)
        .at[targets.reshape(-1, z_blocks).T.reshape(-1)]
        .add(heat_cells.reshape(-1, 128))
    )
    substrate_energy_input = lax.psum_scatter(
        partial_value.reshape(slab_count, component_lines, 128),
        "wide",
        scatter_dimension=0,
        tiled=True,
    )
    thermal_profile = substrate_warmth_excess + dissipation_factor * substrate_energy_input.reshape(
        substrate_warmth_excess.shape
    )
    return (corrected_flow_vector, conduct(thermal_profile, spread_coefficient))


def solution(mesh):
    return jax.shard_map(
        per_device,
        mesh=mesh,
        in_specs=(
            P(None, "wide", "narrow", None),
            P(None, "wide", "narrow", None),
            P("wide", "narrow", None),
            P("wide", "narrow", None),
            P("wide", "narrow", None),
            P(("wide", "narrow"), None),
            P(("wide", "narrow")),
        ),
        out_specs=(P(None, "wide", "narrow", None), P("wide", "narrow", None)),
        check_vma=False,
    )
```

```python
import math

import jax
import jax.numpy as jnp
import numpy as np
from jax import lax
from jax.experimental import pallas as pl
from jax.experimental.pallas import tpu as pltpu
from jax.sharding import PartitionSpec as P

PASSES = 2
STEPS = 3


time_step = 0.15
rate_base = 0.5
zener_energy = 4.0
stress_exponent = 5.0
penalty = 0.001
dissipation_factor = 0.1


def with_halo(x, sides, width, wrap):
    for axis, dim in sides:
        size, length = (lax.axis_size(axis), x.shape[dim])
        up = [(i, (i + 1) % size) for i in range(size if wrap else size - 1)]
        down = [(j, i) for i, j in up]
        last = lax.slice_in_dim(x, length - width, length, axis=dim)
        initial = lax.slice_in_dim(x, 0, width, axis=dim)
        before = lax.ppermute(last, axis, up)
        after = lax.ppermute(initial, axis, down)
        x = jnp.concatenate([before, x, after], axis=dim)
    return x


def ring(value, axis, dim):
    size, length = lax.axis_size(axis), value.shape[dim]
    up = [(i, (i + 1) % size) for i in range(size)]
    down = [(j, i) for i, j in up]
    last = lax.slice_in_dim(value, length - 1, length, axis=dim)
    initial = lax.slice_in_dim(value, 0, 1, axis=dim)
    return lax.ppermute(last, axis, up), lax.ppermute(initial, axis, down)


anywhere = pl.BlockSpec(memory_space=pl.ANY)
in_vmem = pl.BlockSpec(memory_space=pltpu.VMEM)
scaled_mu = 0.5 * time_step


def row_numbers(width):
    return lax.broadcasted_iota(jnp.int32, (8, width), 0)


def rows_of(strip):
    return pl.ds(8 * strip, 8)


def pick(ref, index):
    return ref.at[:, index] if len(ref.shape) == 4 else ref.at[index]


class Planes:
    def __init__(self, source, target, semaphores, listed=None):
        self.source, self.target, self.semaphores = source, target, semaphores
        self.listed = listed

    def copy(self, slot, ref, plane):
        return pltpu.make_async_copy(
            pick(ref, plane), pick(self.target, slot), self.semaphores.at[slot]
        )

    def start(self, slot, plane=None):
        if self.listed is None:
            self.copy(slot, self.source, slot if plane is None else plane).start()
        else:
            self.copy(slot, *self.listed[slot]).start()

    def wait(self, slot):
        self.copy(slot, self.source, 0).wait()


def edge_list(ref, low, high, x_local):
    return [(low, 0), (ref, 0), (ref, 1), (ref, x_local - 2), (ref, x_local - 1), (high, 0)]


def viscosity_plane(cells, slot, edges, warmth, warm_slot, outs, out_slot, y_local, z_cells):
    strips, rows = y_local // 8, row_numbers(z_cells)
    before, after = edges
    values = [[cells[c, slot, rows_of(s), :] for s in range(strips)] for c in range(3)]
    up = [[pltpu.roll(v, 7, 0) for v in row] for row in values]
    down = [[pltpu.roll(v, 1, 0) for v in row] for row in values]
    for s in range(strips):
        along_x, along_y, along_z = [], [], []
        for c in range(3):
            value = values[c][s]
            along_x.append(cells[c, slot + 1, rows_of(s), :] - cells[c, slot - 1, rows_of(s), :])
            ahead = jnp.where(rows == 7, up[c][s + 1] if s + 1 < strips else after(c), up[c][s])
            behind = jnp.where(rows == 0, down[c][s - 1] if s else before(c), down[c][s])
            along_y.append(ahead - behind)
            along_z.append(pltpu.roll(value, z_cells - 1, 1) - pltpu.roll(value, 1, 1))
        s_xy = along_y[0] + along_x[1]
        s_xz = along_z[0] + along_x[2]
        s_yz = along_z[1] + along_y[2]
        extra = 0.5 * (
            along_x[0] * along_x[0] + along_y[1] * along_y[1] + along_z[2] * along_z[2]
        ) + 0.25 * (s_xy * s_xy + s_xz * s_xz + s_yz * s_yz)
        rate_sq = rate_base**2 + extra
        value = jnp.exp(
            (0.5 / stress_exponent) * jnp.log(rate_sq)
            + (zener_energy / stress_exponent) * (1.0 / warmth[warm_slot, rows_of(s), :] - 1.0)
        )
        square = value * value + 1.0
        mu = jnp.log(value + square * lax.rsqrt(square)) * lax.rsqrt(rate_sq)
        outs[0][out_slot, rows_of(s), :] = mu * (scaled_mu / 3.0)
        if len(outs) > 1:
            heat = (mu * (1.0 / 3.0)) * extra
            for b in range(z_cells // 128):
                outs[1][b, out_slot, rows_of(s), :] = heat[:, b * 128 : (b + 1) * 128]


def viscosity_call(flow, y_sides, warmth, with_heat, x_sides=None, inner=None):
    _, x_local, y_local, z_cells = flow.shape
    z_blocks = z_cells // 128
    edge = x_sides is not None
    slots, made = (6, 2) if edge else (x_local, x_local - 2)
    outputs = 2 if with_heat else 1

    def kernel(*refs):
        flow_ref, before_ref, after_ref, warmth_ref = refs[:4]
        rest = list(refs[4:])
        listed = None
        if edge:
            low, high = rest[:2]
            listed = edge_list(flow_ref, low, high, x_local)
            rest = rest[2 + outputs :]
        out_refs, rest = rest[:outputs], rest[outputs:]
        cells, cell_sem, warm, warm_sem = rest[:4]
        outs, out_sems = rest[4 : 4 + outputs], rest[4 + outputs :]
        flow_planes = Planes(flow_ref, cells, cell_sem, listed)
        warm_planes = Planes(warmth_ref, warm, warm_sem)

        def plane_of(i):
            return i * (x_local - 1) if edge else i + 1

        def slot_of(i):
            return 3 * i + 1 if edge else i + 1

        def stored(k, i):
            return pltpu.make_async_copy(
                pick(outs[k], i), pick(out_refs[k], plane_of(i)), out_sems[k].at[i]
            )

        if edge:
            for slot in range(6):
                flow_planes.start(slot)
            for i in range(2):
                warm_planes.start(i, plane_of(i))
        else:
            flow_planes.start(0)
            flow_planes.start(1)

            def begin(i, state):
                flow_planes.start(i + 2)
                warm_planes.start(i, i + 1)
                return state

            lax.fori_loop(0, made, begin, 0)
            flow_planes.wait(0)
            flow_planes.wait(1)

        def body(i, state):
            slot, plane = slot_of(i), plane_of(i)
            if edge:
                flow_planes.wait(slot - 1)
                flow_planes.wait(slot)
            flow_planes.wait(slot + 1)
            warm_planes.wait(i)
            viscosity_plane(
                cells,
                slot,
                (lambda c: before_ref[c, plane], lambda c: after_ref[c, plane]),
                warm,
                i,
                outs,
                i,
                y_local,
                z_cells,
            )
            for k in range(outputs):
                stored(k, i).start()
            return state

        lax.fori_loop(0, made, body, 0)

        def finish(i, state):
            for k in range(outputs):
                stored(k, i).wait()
            return state

        lax.fori_loop(0, made, finish, 0)

    shapes = [(x_local, y_local, z_cells), (z_blocks, x_local, y_local, 128)][:outputs]
    held = [(made, y_local, z_cells), (z_blocks, made, y_local, 128)][:outputs]
    operands = [flow, *y_sides, warmth]
    specs = [anywhere, in_vmem, in_vmem, anywhere]
    aliases = {}
    if edge:
        operands += [*x_sides, *inner]
        specs += [anywhere] * (2 + outputs)
        aliases = {6 + k: k for k in range(outputs)}
    return pl.pallas_call(
        kernel,
        in_specs=specs,
        out_specs=[anywhere] * outputs,
        out_shape=[jax.ShapeDtypeStruct(shape, jnp.float32) for shape in shapes],
        input_output_aliases=aliases,
        scratch_shapes=[
            pltpu.VMEM((3, slots, y_local, z_cells), jnp.float32),
            pltpu.SemaphoreType.DMA((slots,)),
            pltpu.VMEM((made, y_local, z_cells), jnp.float32),
            pltpu.SemaphoreType.DMA((made,)),
        ]
        + [pltpu.VMEM(shape, jnp.float32) for shape in held]
        + [pltpu.SemaphoreType.DMA((made,))] * outputs,
        compiler_params=pltpu.CompilerParams(vmem_limit_bytes=vmem_limit),
        name="viscosity_edge" if edge else "viscosity_inner",
    )(*operands)


vmem_limit = 48 << 20


def advance_plane(cells, mu, slot, edges, push, out_slot, flux, y_local, z_cells):
    strips, rows = y_local // 8, row_numbers(z_cells)
    flow_before, flow_after, mu_before, mu_after = edges
    m = [mu[slot, rows_of(s), :] for s in range(strips)]
    m_up = [pltpu.roll(v, 7, 0) for v in m]
    sums_y = [
        m[s] + jnp.where(rows == 7, m_up[s + 1] if s + 1 < strips else mu_after(), m_up[s])
        for s in range(strips)
    ]
    first_sum = mu_before() + mu[slot, pl.ds(0, 1), :]
    values = [[cells[c, slot, rows_of(s), :] for s in range(strips)] for c in range(3)]
    up = [[pltpu.roll(v, 7, 0) for v in row] for row in values]
    carried = [
        first_sum * (cells[c, slot, pl.ds(0, 1), :] - flow_before(c)) for c in range(3)
    ]
    for s in range(strips):
        sum_x = m[s] + mu[slot + 1, rows_of(s), :]
        sum_z = m[s] + pltpu.roll(m[s], z_cells - 1, 1)
        for c in range(3):
            value = values[c][s]
            flux_x = sum_x * (cells[c, slot + 1, rows_of(s), :] - value)
            ahead = jnp.where(
                rows == 7, up[c][s + 1] if s + 1 < strips else flow_after(c), up[c][s]
            )
            flux_y = sums_y[s] * (ahead - value)
            flux_z = sum_z * (pltpu.roll(value, z_cells - 1, 1) - value)
            turned = pltpu.roll(flux_y, 1, 0)
            total = (flux_x - flux[c, rows_of(s), :]) + (
                flux_y - jnp.where(rows == 0, carried[c], turned)
            ) + (flux_z - pltpu.roll(flux_z, 1, 1))
            flux[c, rows_of(s), :] = flux_x
            carried[c] = turned
            push[c, out_slot, rows_of(s), :] = (
                value + time_step * push[c, out_slot, rows_of(s), :] + total
            )


def first_flux(cells, mu, slot, flux, y_local):
    for s in range(y_local // 8):
        sum_x = mu[slot - 1, rows_of(s), :] + mu[slot, rows_of(s), :]
        for c in range(3):
            flux[c, rows_of(s), :] = sum_x * (
                cells[c, slot, rows_of(s), :] - cells[c, slot - 1, rows_of(s), :]
            )


def advance_call(flow, flow_y, mu, mu_y, push, flow_x=None, mu_x=None, inner=None):
    _, x_local, y_local, z_cells = flow.shape
    edge = flow_x is not None
    slots, made = (6, 2) if edge else (x_local, x_local - 2)

    def kernel(*refs):
        flow_ref, flow_before, flow_after, mu_ref, mu_before, mu_after, push_ref = refs[:7]
        rest = refs[7:]
        flow_listed = mu_listed = None
        if edge:
            flow_listed = edge_list(flow_ref, rest[0], rest[1], x_local)
            mu_listed = edge_list(mu_ref, rest[2], rest[3], x_local)
            rest = rest[5:]
        out_ref, cells, cell_sem, mu_cells, mu_sem, work, work_sem, out_sem, flux = rest
        flow_planes = Planes(flow_ref, cells, cell_sem, flow_listed)
        mu_planes = Planes(mu_ref, mu_cells, mu_sem, mu_listed)
        push_planes = Planes(push_ref, work, work_sem)

        def plane_of(i):
            return i * (x_local - 1) if edge else i + 1

        def stored(i):
            return pltpu.make_async_copy(
                pick(work, i), pick(out_ref, plane_of(i)), out_sem.at[i]
            )

        if edge:
            for slot in range(6):
                flow_planes.start(slot)
                mu_planes.start(slot)
            for i in range(2):
                push_planes.start(i, plane_of(i))
        else:
            for slot in range(2):
                flow_planes.start(slot)
                mu_planes.start(slot)

            def begin(i, state):
                flow_planes.start(i + 2)
                mu_planes.start(i + 2)
                push_planes.start(i, i + 1)
                return state

            lax.fori_loop(0, made, begin, 0)
            for slot in range(2):
                flow_planes.wait(slot)
                mu_planes.wait(slot)
            first_flux(cells, mu_cells, 1, flux, y_local)

        def body(i, state):
            slot, plane = (3 * i + 1 if edge else i + 1), plane_of(i)
            if edge:
                for back in range(2):
                    flow_planes.wait(slot - back)
                    mu_planes.wait(slot - back)
                first_flux(cells, mu_cells, slot, flux, y_local)
            flow_planes.wait(slot + 1)
            mu_planes.wait(slot + 1)
            push_planes.wait(i)
            advance_plane(
                cells,
                mu_cells,
                slot,
                (
                    lambda c: flow_before[c, plane],
                    lambda c: flow_after[c, plane],
                    lambda: mu_before[plane],
                    lambda: mu_after[plane],
                ),
                work,
                i,
                flux,
                y_local,
                z_cells,
            )
            stored(i).start()
            return state

        lax.fori_loop(0, made, body, 0)

        def finish(i, state):
            stored(i).wait()
            return state

        lax.fori_loop(0, made, finish, 0)

    operands = [flow, *flow_y, mu, *mu_y, push]
    specs = [anywhere, in_vmem, in_vmem, anywhere, in_vmem, in_vmem, anywhere]
    aliases = {}
    if edge:
        operands += [*flow_x, *mu_x, inner]
        specs += [anywhere] * 5
        aliases = {11: 0}
    return pl.pallas_call(
        kernel,
        in_specs=specs,
        out_specs=anywhere,
        out_shape=jax.ShapeDtypeStruct(flow.shape, jnp.float32),
        input_output_aliases=aliases,
        scratch_shapes=[
            pltpu.VMEM((3, slots, y_local, z_cells), jnp.float32),
            pltpu.SemaphoreType.DMA((slots,)),
            pltpu.VMEM((slots, y_local, z_cells), jnp.float32),
            pltpu.SemaphoreType.DMA((slots,)),
            pltpu.VMEM((3, made, y_local, z_cells), jnp.float32),
            pltpu.SemaphoreType.DMA((made,)),
            pltpu.SemaphoreType.DMA((made,)),
            pltpu.VMEM((3, y_local, z_cells), jnp.float32),
        ],
        compiler_params=pltpu.CompilerParams(vmem_limit_bytes=vmem_limit),
        name="advance_edge" if edge else "advance_inner",
    )(*operands)


def cosine_sine_basis(points, period, waves):
    columns, eigen = [], []
    for wave in waves:
        angle = 2.0 * np.pi * ((wave * np.arange(points)) % period) / period
        single = wave % period == 0 or 2 * wave == period
        size = math.sqrt((1.0 if single else 2.0) / period)
        columns.append(np.cos(angle) * size)
        eigen.append(math.sin(2.0 * math.pi * wave / period) ** 2)
        if not single:
            columns.append(np.sin(angle) * size)
            eigen.append(eigen[-1])
    return np.stack(columns, 1), np.array(eigen)


def halves(table):
    table = np.asarray(table, np.float32)
    high = table.astype(jnp.bfloat16)
    low = (table - high.astype(np.float32)).astype(jnp.bfloat16)
    return jnp.asarray(high), jnp.asarray(low)


def split(value):
    high = value.astype(jnp.bfloat16)
    return high, (value - high.astype(jnp.float32)).astype(jnp.bfloat16)


def triple_product(left, right):
    def product(one, two):
        return lax.dot_general(
            one, two, (((1,), (0,)), ((), ())), preferred_element_type=jnp.float32
        )

    return product(left[0], right[0]) + (product(left[0], right[1]) + product(left[1], right[0]))


def z_tables(z_cells):
    half = z_cells // 2
    even, eigen_even = cosine_sine_basis(half, z_cells, range(0, half + 1, 2))
    odd, eigen_odd = cosine_sine_basis(half, z_cells, range(1, half, 2))
    return even, odd, np.concatenate([eigen_even, eigen_odd])


def whole(*shape):
    return pl.BlockSpec(shape, lambda *index: (0,) * len(shape))


def modes_of(lines, even_high, even_low, odd_high, odd_low):
    half = lines.shape[1] // 2
    first, second = lines[:, :half], lines[:, half:]
    return jnp.concatenate(
        [
            triple_product(split(first + second), (even_high[...], even_low[...])),
            triple_product(split(first - second), (odd_high[...], odd_low[...])),
        ],
        1,
    )


def cells_of(modes, even_high, even_low, odd_high, odd_low):
    half = modes.shape[1] // 2
    first = triple_product(split(modes[:, :half]), (even_high[...], even_low[...]))
    second = triple_product(split(modes[:, half:]), (odd_high[...], odd_low[...]))
    return jnp.concatenate([first + second, first - second], 1)


def divergence_modes(flow, count):
    _, x_local, y_local, z_cells = flow.shape
    half, piece, strips = z_cells // 2, z_cells // count, y_local // 8
    step = min(8, x_local)
    even, odd, _ = z_tables(z_cells)
    tables = halves(even) + halves(odd)

    def kernel(
        flow_ref, even_high, even_low, odd_high, odd_low, out_ref,
        cells, semaphores, work, made, out_sem,
    ):
        planes = Planes(flow_ref, cells, semaphores)
        rows = row_numbers(z_cells)

        def begin(i, state):
            planes.start(i)
            return state

        lax.fori_loop(0, x_local, begin, 0)
        planes.wait(0)

        def stored(k):
            part = pl.ds(k * step, step)
            return pltpu.make_async_copy(made.at[:, part], out_ref.at[:, part], out_sem.at[k])

        def group(k, state):
            def plane(i, state):
                j = k * step + i

                @pl.when(j + 1 < x_local)
                def _():
                    planes.wait(j + 1)

                nearer = jnp.where(j > 0, 0.5, 0.0)
                further = jnp.where(j + 1 < x_local, 0.5, 0.0)
                last, following = jnp.maximum(j - 1, 0), jnp.minimum(j + 1, x_local - 1)
                across = [cells[1, j, rows_of(s), :] for s in range(strips)]
                up = [pltpu.roll(v, 7, 0) for v in across]
                down = [pltpu.roll(v, 1, 0) for v in across]
                for s in range(strips):
                    ahead = jnp.where(rows == 7, up[s + 1] if s + 1 < strips else 0.0, up[s])
                    behind = jnp.where(rows == 0, down[s - 1] if s else 0.0, down[s])
                    along = cells[2, j, rows_of(s), :]
                    work[i, rows_of(s), :] = (
                        further * cells[0, following, rows_of(s), :]
                        - nearer * cells[0, last, rows_of(s), :]
                    ) + 0.5 * (
                        (ahead - behind)
                        + (pltpu.roll(along, z_cells - 1, 1) - pltpu.roll(along, 1, 1))
                    )
                return state

            lax.fori_loop(0, step, plane, 0)
            modes = modes_of(
                work[...].reshape(step * y_local, z_cells), even_high, even_low, odd_high, odd_low
            )
            for n in range(count):
                made[n, pl.ds(k * step, step)] = modes[:, n * piece : (n + 1) * piece].reshape(
                    step, y_local, piece
                )
            stored(k).start()
            return state

        groups = x_local // step
        lax.fori_loop(0, groups, group, 0)
        for k in range(groups):
            stored(k).wait()

    return pl.pallas_call(
        kernel,
        in_specs=[anywhere] + [in_vmem] * 4,
        out_specs=anywhere,
        out_shape=jax.ShapeDtypeStruct((count, x_local, y_local, piece), jnp.float32),
        scratch_shapes=[
            pltpu.VMEM((3, x_local, y_local, z_cells), jnp.float32),
            pltpu.SemaphoreType.DMA((x_local,)),
            pltpu.VMEM((step, y_local, z_cells), jnp.float32),
            pltpu.VMEM((count, x_local, y_local, piece), jnp.float32),
            pltpu.SemaphoreType.DMA((x_local // step,)),
        ],
        compiler_params=pltpu.CompilerParams(vmem_limit_bytes=vmem_limit),
        name="divergence_modes",
    )(flow, *tables)


def add_halo_modes(modes, x_sides, y_sides):
    count, x_local, y_local, piece = modes.shape
    z_cells = count * piece
    even, odd, _ = z_tables(z_cells)
    tables = halves(even) + halves(odd)

    def kernel(
        modes_ref, low_ref, high_ref, before_ref, after_ref,
        even_high, even_low, odd_high, odd_low, out_ref, ends, lines, semaphores,
    ):
        def moves(back):
            pairs = [
                (ends.at[k], modes_ref.at[:, plane])
                for k, plane in enumerate((0, x_local - 1))
            ] + [
                (lines.at[k], modes_ref.at[:, 1 : x_local - 1, 8 * s : 8 * s + 8])
                for k, s in enumerate((0, y_local // 8 - 1))
            ]
            if back:
                pairs = [
                    (ends.at[k], out_ref.at[:, plane])
                    for k, plane in enumerate((0, x_local - 1))
                ] + [
                    (lines.at[k], out_ref.at[:, 1 : x_local - 1, 8 * s : 8 * s + 8])
                    for k, s in enumerate((0, y_local // 8 - 1))
                ]
                return [
                    pltpu.make_async_copy(here, there, semaphores.at[4 + i])
                    for i, (here, there) in enumerate(pairs)
                ]
            return [
                pltpu.make_async_copy(there, here, semaphores.at[i])
                for i, (here, there) in enumerate(pairs)
            ]

        loads, stores = moves(False), moves(True)
        for load in loads:
            load.start()
        added = modes_of(
            jnp.concatenate(
                [-0.5 * low_ref[0], 0.5 * high_ref[0], -0.5 * before_ref[...], 0.5 * after_ref[...]],
                0,
            ),
            even_high,
            even_low,
            odd_high,
            odd_low,
        )
        for load in loads:
            load.wait()
        rows = row_numbers(piece)
        for n in range(count):
            block = added[:, n * piece : (n + 1) * piece]
            side = [block[2 * y_local + k * x_local :][:x_local] for k in range(2)]
            for k, plane in enumerate((0, x_local - 1)):
                ends[k, n] = ends[k, n] + block[k * y_local : (k + 1) * y_local]
                for j, (strip, row) in enumerate(((0, 0), (y_local // 8 - 1, 7))):
                    part = pl.ds(8 * strip, 8)
                    ends[k, n, part, :] = ends[k, n, part, :] + jnp.where(
                        rows == row, side[j][plane : plane + 1], 0.0
                    )
            for j, row in enumerate((0, 7)):
                for x in range(1, x_local - 1):
                    lines[j, n, x - 1] = lines[j, n, x - 1] + jnp.where(
                        rows == row, side[j][x : x + 1], 0.0
                    )
        for store in stores:
            store.start()
        for store in stores:
            store.wait()

    return pl.pallas_call(
        kernel,
        in_specs=[anywhere] + [in_vmem] * 8,
        out_specs=anywhere,
        out_shape=jax.ShapeDtypeStruct(modes.shape, jnp.float32),
        input_output_aliases={0: 0},
        scratch_shapes=[
            pltpu.VMEM((2, count, y_local, piece), jnp.float32),
            pltpu.VMEM((2, count, x_local - 2, 8, piece), jnp.float32),
            pltpu.SemaphoreType.DMA((8,)),
        ],
        compiler_params=pltpu.CompilerParams(vmem_limit_bytes=16 << 20),
        name="add_halo_modes",
    )(modes, *x_sides, *y_sides, *tables)


def corrected(flow, spectrum, y_sides):
    count, planes, y_local, piece = spectrum.shape
    x_local, z_cells = planes - 2, count * piece
    strips, part = y_local // 8, planes // 2
    even, odd, _ = z_tables(z_cells)
    tables = halves(even.T) + halves(odd.T)

    def kernel(
        flow_ref, in_ref, before_ref, after_ref,
        even_high, even_low, odd_high, odd_low, out_ref,
        modes, mode_sem, pressure, sides, work, out_sem,
    ):
        table_refs = (even_high, even_low, odd_high, odd_low)

        def load(k):
            span = pl.ds(k * part, part)
            return pltpu.make_async_copy(in_ref.at[:, span], modes.at[:, span], mode_sem.at[k])

        load(0).start()
        load(1).start()
        sides[...] = cells_of(
            jnp.concatenate(
                [
                    jnp.concatenate([ref[n] for n in range(count)], 1)
                    for ref in (before_ref, after_ref)
                ],
                0,
            ),
            *table_refs,
        )
        rows = row_numbers(z_cells)

        def stored(i):
            return pltpu.make_async_copy(pick(work, i), pick(out_ref, i), out_sem.at[i])

        def plane(j, state):
            values = [pressure[j + 1, rows_of(s), :] for s in range(strips)]
            up = [pltpu.roll(v, 7, 0) for v in values]
            down = [pltpu.roll(v, 1, 0) for v in values]
            for s in range(strips):
                ahead = up[s + 1] if s + 1 < strips else sides[pl.ds(x_local + j, 1), :]
                behind = down[s - 1] if s else sides[pl.ds(j, 1), :]
                slopes = (
                    pressure[j + 2, rows_of(s), :] - pressure[j, rows_of(s), :],
                    jnp.where(rows == 7, ahead, up[s]) - jnp.where(rows == 0, behind, down[s]),
                    pltpu.roll(values[s], z_cells - 1, 1) - pltpu.roll(values[s], 1, 1),
                )
                for c in range(3):
                    work[c, j, rows_of(s), :] = flow_ref[c, j, rows_of(s), :] - 0.5 * slopes[c]
            stored(j).start()
            return state

        for k in range(2):
            load(k).wait()
            span = pl.ds(k * part, part)
            pressure[span] = cells_of(
                jnp.concatenate(
                    [modes[n, span].reshape(part * y_local, piece) for n in range(count)], 1
                ),
                *table_refs,
            ).reshape(part, y_local, z_cells)
            lax.fori_loop(k * (part - 2), (part - 2) if k == 0 else x_local, plane, 0)

        def finish(i, state):
            stored(i).wait()
            return state

        lax.fori_loop(0, x_local, finish, 0)

    return pl.pallas_call(
        kernel,
        in_specs=[in_vmem, anywhere] + [in_vmem] * 6,
        out_specs=anywhere,
        out_shape=jax.ShapeDtypeStruct(flow.shape, jnp.float32),
        scratch_shapes=[
            pltpu.VMEM(spectrum.shape, jnp.float32),
            pltpu.SemaphoreType.DMA((2,)),
            pltpu.VMEM((planes, y_local, z_cells), jnp.float32),
            pltpu.VMEM((2 * x_local, z_cells), jnp.float32),
            pltpu.VMEM(flow.shape, jnp.float32),
            pltpu.SemaphoreType.DMA((x_local,)),
        ],
        compiler_params=pltpu.CompilerParams(vmem_limit_bytes=36 << 20),
        name="corrected",
    )(flow, spectrum, *y_sides, *tables)


def y_forward(spectrum, ratio, wide_count):
    count, x_local, y_local, piece = spectrum.shape
    y_cells = count * y_local
    share = y_cells // wide_count
    table, _ = cosine_sine_basis(y_cells, y_cells, range(y_cells // 2 + 1))
    tables = halves(table.T)

    def kernel(in_ref, high_ref, low_ref, ratio_ref, modes_ref, carry_ref, sums, power):
        @pl.when(pl.program_id(0) == 0)
        def _():
            sums[...] = jnp.zeros_like(sums)
            power[...] = jnp.ones_like(power)

        planes = [
            jnp.concatenate([in_ref[n, side] for n in range(count)], 0) for side in range(2)
        ]
        modes = triple_product(
            (high_ref[...], low_ref[...]), split(jnp.concatenate(planes, 1))
        )
        r, pw = ratio_ref[...], power[...]
        for side in range(2):
            plane = modes[:, side * piece : (side + 1) * piece]
            modes_ref[side] = plane
            sums[side] = plane + r * sums[side]
            sums[2 + side] = sums[2 + side] + pw * plane
        power[...] = pw * r

        @pl.when(pl.program_id(0) == x_local // 2 - 1)
        def _():
            for kind in range(4):
                carry_ref[:, kind] = sums[kind].reshape(wide_count, share, piece)

    return pl.pallas_call(
        kernel,
        grid=(x_local // 2,),
        in_specs=[
            pl.BlockSpec((count, 2, y_local, piece), lambda i: (0, i, 0, 0)),
            whole(y_cells, y_cells),
            whole(y_cells, y_cells),
            whole(y_cells, piece),
        ],
        out_specs=[
            pl.BlockSpec((2, y_cells, piece), lambda i: (i, 0, 0)),
            whole(wide_count, 4, share, piece),
        ],
        out_shape=[
            jax.ShapeDtypeStruct((x_local, y_cells, piece), jnp.float32),
            jax.ShapeDtypeStruct((wide_count, 4, share, piece), jnp.float32),
        ],
        scratch_shapes=[
            pltpu.VMEM((4, y_cells, piece), jnp.float32),
            pltpu.VMEM((y_cells, piece), jnp.float32),
        ],
        name="y_forward",
    )(spectrum, *tables, ratio)


def power_of(value, exponent):
    result = None
    while exponent:
        if exponent & 1:
            result = value if result is None else result * value
        value = value * value
        exponent >>= 1
    return result


def join_carries(carries, ratio, block):
    count, kinds, share, piece = carries.shape

    def kernel(in_ref, ratio_ref, out_ref):
        step = power_of(ratio_ref[...], block)
        scale = 1.0 / (1.0 - power_of(step, count))
        for kind in range(kinds):
            order = list(range(count)) if kind < 2 else list(range(count))[::-1]
            total = in_ref[order[0], kind]
            for w in order[1:]:
                total = in_ref[w, kind] + step * total
            total = total * scale
            for w in order:
                out_ref[w, kind] = total
                total = in_ref[w, kind] + step * total

    return pl.pallas_call(
        kernel,
        out_shape=jax.ShapeDtypeStruct(carries.shape, jnp.float32),
        name="join_carries",
    )(carries, ratio)


def y_inverse(modes, carries, ratio, gain, count):
    x_local, y_cells, piece = modes.shape
    y_local, pairs = y_cells // count, x_local // 2
    wide_count, _, share, _ = carries.shape
    table, _ = cosine_sine_basis(y_cells, y_cells, range(y_cells // 2 + 1))
    tables = halves(table)

    def kernel(modes_ref, carry_ref, high_ref, low_ref, ratio_ref, gain_ref, out_ref, behind, ahead):
        step = pl.program_id(0)
        r = ratio_ref[...]

        def carry(kind):
            return carry_ref[:, kind].reshape(y_cells, piece)

        @pl.when(step == 0)
        def _():
            ahead[0] = carry(0)
            ahead[1] = carry(1)
            behind[2 * pairs + 1] = carry(2)

            def back(i, state):
                even, odd = state
                m = pairs - 1 - i
                behind[2 * m + 2] = r * odd
                behind[2 * m + 1] = r * even
                return (
                    modes_ref[2 * m] + r * even,
                    modes_ref[2 * m + 1] + r * odd,
                )

            _, odd = lax.fori_loop(0, pairs, back, (carry(2), carry(3)))
            behind[0] = r * odd

        even_plane = modes_ref[jnp.minimum(2 * step, x_local - 2)]
        odd_plane = modes_ref[jnp.maximum(2 * step - 1, 1)]
        even = r * ahead[0] + jnp.where(step < pairs, even_plane, 0.0)
        odd = jnp.where(step > 0, odd_plane + r * ahead[1], ahead[1])
        ahead[0] = even
        ahead[1] = odd
        gain_value = gain_ref[...]
        planes = jnp.concatenate(
            [gain_value * (odd + behind[2 * step]), gain_value * (even + behind[2 * step + 1])], 1
        )
        cells = triple_product((high_ref[...], low_ref[...]), split(planes))
        for n in range(count):
            for side in range(2):
                out_ref[n, side] = cells[
                    n * y_local : (n + 1) * y_local, side * piece : (side + 1) * piece
                ]

    return pl.pallas_call(
        kernel,
        grid=(pairs + 1,),
        in_specs=[
            whole(x_local, y_cells, piece),
            whole(wide_count, 4, share, piece),
            whole(y_cells, y_cells),
            whole(y_cells, y_cells),
            whole(y_cells, piece),
            whole(y_cells, piece),
        ],
        out_specs=pl.BlockSpec((count, 2, y_local, piece), lambda i: (0, i, 0, 0)),
        out_shape=jax.ShapeDtypeStruct((count, x_local + 2, y_local, piece), jnp.float32),
        scratch_shapes=[
            pltpu.VMEM((x_local + 2, y_cells, piece), jnp.float32),
            pltpu.VMEM((2, y_cells, piece), jnp.float32),
        ],
        name="y_inverse",
    )(modes, carries, *tables, ratio, gain)


def turn(value, axis):
    return lax.all_to_all(value, axis, split_axis=0, concat_axis=0, tiled=True)


def project(spectrum):
    count, x_local, y_local, piece = spectrum.shape
    y_cells, z_cells = count * y_local, count * piece
    wide_count = lax.axis_size("wide")
    _, eigen_y = cosine_sine_basis(y_cells, y_cells, range(y_cells // 2 + 1))
    eigen_z = jnp.asarray(z_tables(z_cells)[2], jnp.float32)
    own_z = lax.dynamic_slice_in_dim(eigen_z, lax.axis_index("narrow") * piece, piece)
    excess = 4.0 * (jnp.asarray(eigen_y, jnp.float32)[:, None] + own_z[None, :] + penalty)
    root = jnp.sqrt(excess * (4.0 + excess))
    ratio = 2.0 / (2.0 + excess + root)
    gain = -4.0 / root
    share = y_cells // wide_count
    own_ratio = lax.dynamic_slice_in_dim(ratio, lax.axis_index("wide") * share, share)
    modes, carries = y_forward(turn(spectrum, "narrow"), ratio, wide_count)
    carries = turn(join_carries(turn(carries, "wide"), own_ratio, x_local // 2), "wide")
    return turn(y_inverse(modes, carries, ratio, gain, count), "narrow")


def conduct(profile, spread):
    sides = (("wide", 0), ("narrow", 1))
    spread = with_halo(spread, sides, STEPS - 1, False)
    profile = with_halo(profile, sides, STEPS, False)
    for step in range(STEPS):
        center = profile[1:-1, 1:-1]
        near = (
            profile[2:, 1:-1] + profile[:-2, 1:-1] + profile[1:-1, 2:] + profile[1:-1, :-2]
        )
        ahead = jnp.pad(center[:, :, 1:], ((0, 0), (0, 0), (0, 1)))
        behind = jnp.pad(center[:, :, :-1], ((0, 0), (0, 0), (1, 0)))
        profile = center + spread * (near + ahead + behind - 6.0 * center)
        spread = spread[1:-1, 1:-1]
    return profile


def per_device(
    material_flow_vector,
    tool_push_density,
    tool_warmth_excess,
    substrate_warmth_excess,
    spread_coefficient,
    source_owner_sheet,
    source_part_line,
):
    flow = material_flow_vector
    flow_x, flow_y = ring(flow, "wide", 1), ring(flow, "narrow", 2)
    current, current_x, current_y = flow, flow_x, flow_y
    for section in range(PASSES):
        last = section + 1 == PASSES
        inner = viscosity_call(current, current_y, tool_warmth_excess, last)
        fields = viscosity_call(current, current_y, tool_warmth_excess, last, current_x, inner)
        mu = fields[0]
        mu_x, mu_y = ring(mu, "wide", 0), ring(mu, "narrow", 1)
        inner = advance_call(flow, flow_y, mu, mu_y, tool_push_density)
        current = advance_call(flow, flow_y, mu, mu_y, tool_push_density, flow_x, mu_x, inner)
        if not last:
            current_x, current_y = ring(current, "wide", 1), ring(current, "narrow", 2)
    heat_cells = fields[1]
    end_x = ring(current[0], "wide", 0)
    end_y = [side[:, 0] for side in ring(current[1], "narrow", 1)]
    modes = divergence_modes(current, lax.axis_size("narrow"))
    spectrum = project(add_halo_modes(modes, end_x, end_y))
    inner = spectrum[:, 1:-1]
    corrected_flow_vector = corrected(
        current, spectrum, [side[:, :, 0] for side in ring(inner, "narrow", 2)]
    )
    z_blocks = heat_cells.shape[0]
    slab_count = lax.axis_size("wide")
    component_lines = substrate_warmth_excess.shape[0] * substrate_warmth_excess.shape[1]
    targets = source_owner_sheet[:, 0] * component_lines + source_part_line
    partial_value = (
        jnp.zeros((slab_count * component_lines, 128), jnp.float32)
        .at[targets.reshape(-1, z_blocks).T.reshape(-1)]
        .add(heat_cells.reshape(-1, 128))
    )
    substrate_energy_input = lax.psum_scatter(
        partial_value.reshape(slab_count, component_lines, 128),
        "wide",
        scatter_dimension=0,
        tiled=True,
    )
    thermal_profile = substrate_warmth_excess + dissipation_factor * substrate_energy_input.reshape(
        substrate_warmth_excess.shape
    )
    return (corrected_flow_vector, conduct(thermal_profile, spread_coefficient))


def solution(mesh):
    return jax.shard_map(
        per_device,
        mesh=mesh,
        in_specs=(
            P(None, "wide", "narrow", None),
            P(None, "wide", "narrow", None),
            P("wide", "narrow", None),
            P("wide", "narrow", None),
            P("wide", "narrow", None),
            P(("wide", "narrow"), None),
            P(("wide", "narrow")),
        ),
        out_specs=(P(None, "wide", "narrow", None), P("wide", "narrow", None)),
        check_vma=False,
    )
```

```python
import math

import jax
import jax.numpy as jnp
import numpy as np
from jax import lax
from jax.experimental import pallas as pl
from jax.experimental.pallas import tpu as pltpu
from jax.sharding import PartitionSpec as P

PASSES = 2
STEPS = 3


time_step = 0.15
rate_base = 0.5
zener_energy = 4.0
stress_exponent = 5.0
penalty = 0.001
dissipation_factor = 0.1


def with_halo(x, sides, width, wrap):
    for axis, dim in sides:
        size, length = (lax.axis_size(axis), x.shape[dim])
        up = [(i, (i + 1) % size) for i in range(size if wrap else size - 1)]
        down = [(j, i) for i, j in up]
        last = lax.slice_in_dim(x, length - width, length, axis=dim)
        initial = lax.slice_in_dim(x, 0, width, axis=dim)
        before = lax.ppermute(last, axis, up)
        after = lax.ppermute(initial, axis, down)
        x = jnp.concatenate([before, x, after], axis=dim)
    return x


def ring(value, axis, dim):
    size, length = lax.axis_size(axis), value.shape[dim]
    up = [(i, (i + 1) % size) for i in range(size)]
    down = [(j, i) for i, j in up]
    last = lax.slice_in_dim(value, length - 1, length, axis=dim)
    initial = lax.slice_in_dim(value, 0, 1, axis=dim)
    return lax.ppermute(last, axis, up), lax.ppermute(initial, axis, down)


anywhere = pl.BlockSpec(memory_space=pl.ANY)
in_vmem = pl.BlockSpec(memory_space=pltpu.VMEM)
scaled_mu = 0.5 * time_step


def row_numbers(width):
    return lax.broadcasted_iota(jnp.int32, (8, width), 0)


def rows_of(strip):
    return pl.ds(8 * strip, 8)


def pick(ref, index):
    return ref.at[:, index] if len(ref.shape) == 4 else ref.at[index]


class Planes:
    def __init__(self, source, target, semaphores, listed=None):
        self.source, self.target, self.semaphores = source, target, semaphores
        self.listed = listed

    def copy(self, slot, ref, plane):
        return pltpu.make_async_copy(
            pick(ref, plane), pick(self.target, slot), self.semaphores.at[slot]
        )

    def start(self, slot, plane=None):
        if self.listed is None:
            self.copy(slot, self.source, slot if plane is None else plane).start()
        else:
            self.copy(slot, *self.listed[slot]).start()

    def wait(self, slot):
        self.copy(slot, self.source, 0).wait()


def edge_list(ref, low, high, x_local):
    return [(low, 0), (ref, 0), (ref, 1), (ref, x_local - 2), (ref, x_local - 1), (high, 0)]


def viscosity_plane(cells, slot, edges, warmth, warm_slot, outs, out_slot, y_local, z_cells):
    strips, rows = y_local // 8, row_numbers(z_cells)
    before, after = edges
    values = [[cells[c, slot, rows_of(s), :] for s in range(strips)] for c in range(3)]
    up = [[pltpu.roll(v, 7, 0) for v in row] for row in values]
    down = [[pltpu.roll(v, 1, 0) for v in row] for row in values]
    for s in range(strips):
        along_x, along_y, along_z = [], [], []
        for c in range(3):
            value = values[c][s]
            along_x.append(cells[c, slot + 1, rows_of(s), :] - cells[c, slot - 1, rows_of(s), :])
            ahead = jnp.where(rows == 7, up[c][s + 1] if s + 1 < strips else after(c), up[c][s])
            behind = jnp.where(rows == 0, down[c][s - 1] if s else before(c), down[c][s])
            along_y.append(ahead - behind)
            along_z.append(pltpu.roll(value, z_cells - 1, 1) - pltpu.roll(value, 1, 1))
        s_xy = along_y[0] + along_x[1]
        s_xz = along_z[0] + along_x[2]
        s_yz = along_z[1] + along_y[2]
        extra = 0.5 * (
            along_x[0] * along_x[0] + along_y[1] * along_y[1] + along_z[2] * along_z[2]
        ) + 0.25 * (s_xy * s_xy + s_xz * s_xz + s_yz * s_yz)
        rate_sq = rate_base**2 + extra
        value = jnp.exp(
            (0.5 / stress_exponent) * jnp.log(rate_sq)
            + (zener_energy / stress_exponent) * (1.0 / warmth[warm_slot, rows_of(s), :] - 1.0)
        )
        square = value * value + 1.0
        mu = jnp.log(value + square * lax.rsqrt(square)) * lax.rsqrt(rate_sq)
        outs[0][out_slot, rows_of(s), :] = mu * (scaled_mu / 3.0)
        if len(outs) > 1:
            heat = (mu * (1.0 / 3.0)) * extra
            for b in range(z_cells // 128):
                outs[1][b, out_slot, rows_of(s), :] = heat[:, b * 128 : (b + 1) * 128]


def viscosity_call(flow, y_sides, warmth, with_heat, x_sides=None, inner=None):
    _, x_local, y_local, z_cells = flow.shape
    z_blocks = z_cells // 128
    edge = x_sides is not None
    slots, made = (6, 2) if edge else (x_local, x_local - 2)
    outputs = 2 if with_heat else 1

    def kernel(*refs):
        flow_ref, before_ref, after_ref, warmth_ref = refs[:4]
        rest = list(refs[4:])
        listed = None
        if edge:
            low, high = rest[:2]
            listed = edge_list(flow_ref, low, high, x_local)
            rest = rest[2 + outputs :]
        out_refs, rest = rest[:outputs], rest[outputs:]
        cells, cell_sem, warm, warm_sem = rest[:4]
        outs, out_sems = rest[4 : 4 + outputs], rest[4 + outputs :]
        flow_planes = Planes(flow_ref, cells, cell_sem, listed)
        warm_planes = Planes(warmth_ref, warm, warm_sem)

        def plane_of(i):
            return i * (x_local - 1) if edge else i + 1

        def slot_of(i):
            return 3 * i + 1 if edge else i + 1

        def stored(k, i):
            return pltpu.make_async_copy(
                pick(outs[k], i), pick(out_refs[k], plane_of(i)), out_sems[k].at[i]
            )

        if edge:
            for slot in range(6):
                flow_planes.start(slot)
            for i in range(2):
                warm_planes.start(i, plane_of(i))
        else:
            flow_planes.start(0)
            flow_planes.start(1)

            def begin(i, state):
                flow_planes.start(i + 2)
                warm_planes.start(i, i + 1)
                return state

            lax.fori_loop(0, made, begin, 0)
            flow_planes.wait(0)
            flow_planes.wait(1)

        def body(i, state):
            slot, plane = slot_of(i), plane_of(i)
            if edge:
                flow_planes.wait(slot - 1)
                flow_planes.wait(slot)
            flow_planes.wait(slot + 1)
            warm_planes.wait(i)
            viscosity_plane(
                cells,
                slot,
                (lambda c: before_ref[c, plane], lambda c: after_ref[c, plane]),
                warm,
                i,
                outs,
                i,
                y_local,
                z_cells,
            )
            for k in range(outputs):
                stored(k, i).start()
            return state

        lax.fori_loop(0, made, body, 0)

        def finish(i, state):
            for k in range(outputs):
                stored(k, i).wait()
            return state

        lax.fori_loop(0, made, finish, 0)

    shapes = [(x_local, y_local, z_cells), (z_blocks, x_local, y_local, 128)][:outputs]
    held = [(made, y_local, z_cells), (z_blocks, made, y_local, 128)][:outputs]
    operands = [flow, *y_sides, warmth]
    specs = [anywhere, in_vmem, in_vmem, anywhere]
    aliases = {}
    if edge:
        operands += [*x_sides, *inner]
        specs += [anywhere] * (2 + outputs)
        aliases = {6 + k: k for k in range(outputs)}
    return pl.pallas_call(
        kernel,
        in_specs=specs,
        out_specs=[anywhere] * outputs,
        out_shape=[jax.ShapeDtypeStruct(shape, jnp.float32) for shape in shapes],
        input_output_aliases=aliases,
        scratch_shapes=[
            pltpu.VMEM((3, slots, y_local, z_cells), jnp.float32),
            pltpu.SemaphoreType.DMA((slots,)),
            pltpu.VMEM((made, y_local, z_cells), jnp.float32),
            pltpu.SemaphoreType.DMA((made,)),
        ]
        + [pltpu.VMEM(shape, jnp.float32) for shape in held]
        + [pltpu.SemaphoreType.DMA((made,))] * outputs,
        compiler_params=pltpu.CompilerParams(vmem_limit_bytes=vmem_limit),
        name="viscosity_edge" if edge else "viscosity_inner",
    )(*operands)


vmem_limit = 48 << 20


def advance_plane(cells, mu, slot, edges, push, out_slot, flux, y_local, z_cells):
    strips, rows = y_local // 8, row_numbers(z_cells)
    flow_before, flow_after, mu_before, mu_after = edges
    m = [mu[slot, rows_of(s), :] for s in range(strips)]
    m_up = [pltpu.roll(v, 7, 0) for v in m]
    sums_y = [
        m[s] + jnp.where(rows == 7, m_up[s + 1] if s + 1 < strips else mu_after(), m_up[s])
        for s in range(strips)
    ]
    first_sum = mu_before() + mu[slot, pl.ds(0, 1), :]
    values = [[cells[c, slot, rows_of(s), :] for s in range(strips)] for c in range(3)]
    up = [[pltpu.roll(v, 7, 0) for v in row] for row in values]
    carried = [
        first_sum * (cells[c, slot, pl.ds(0, 1), :] - flow_before(c)) for c in range(3)
    ]
    for s in range(strips):
        sum_x = m[s] + mu[slot + 1, rows_of(s), :]
        sum_z_ahead = m[s] + pltpu.roll(m[s], z_cells - 1, 1)
        sum_z_behind = m[s] + pltpu.roll(m[s], 1, 1)
        for c in range(3):
            value = values[c][s]
            flux_x = sum_x * (cells[c, slot + 1, rows_of(s), :] - value)
            ahead = jnp.where(
                rows == 7, up[c][s + 1] if s + 1 < strips else flow_after(c), up[c][s]
            )
            flux_y = sums_y[s] * (ahead - value)
            turned = pltpu.roll(flux_y, 1, 0)
            total = (flux_x - flux[c, rows_of(s), :]) + (
                flux_y - jnp.where(rows == 0, carried[c], turned)
            ) + (
                sum_z_ahead * (pltpu.roll(value, z_cells - 1, 1) - value)
                - sum_z_behind * (value - pltpu.roll(value, 1, 1))
            )
            flux[c, rows_of(s), :] = flux_x
            carried[c] = turned
            push[c, out_slot, rows_of(s), :] = (
                value + time_step * push[c, out_slot, rows_of(s), :] + total
            )


def first_flux(cells, mu, slot, flux, y_local):
    for s in range(y_local // 8):
        sum_x = mu[slot - 1, rows_of(s), :] + mu[slot, rows_of(s), :]
        for c in range(3):
            flux[c, rows_of(s), :] = sum_x * (
                cells[c, slot, rows_of(s), :] - cells[c, slot - 1, rows_of(s), :]
            )


def advance_call(flow, flow_y, mu, mu_y, push, flow_x=None, mu_x=None, inner=None):
    _, x_local, y_local, z_cells = flow.shape
    edge = flow_x is not None
    slots, made = (6, 2) if edge else (x_local, x_local - 2)

    def kernel(*refs):
        flow_ref, flow_before, flow_after, mu_ref, mu_before, mu_after, push_ref = refs[:7]
        rest = refs[7:]
        flow_listed = mu_listed = None
        if edge:
            flow_listed = edge_list(flow_ref, rest[0], rest[1], x_local)
            mu_listed = edge_list(mu_ref, rest[2], rest[3], x_local)
            rest = rest[5:]
        out_ref, cells, cell_sem, mu_cells, mu_sem, work, work_sem, out_sem, flux = rest
        flow_planes = Planes(flow_ref, cells, cell_sem, flow_listed)
        mu_planes = Planes(mu_ref, mu_cells, mu_sem, mu_listed)
        push_planes = Planes(push_ref, work, work_sem)

        def plane_of(i):
            return i * (x_local - 1) if edge else i + 1

        def stored(i):
            return pltpu.make_async_copy(
                pick(work, i), pick(out_ref, plane_of(i)), out_sem.at[i]
            )

        if edge:
            for slot in range(6):
                flow_planes.start(slot)
                mu_planes.start(slot)
            for i in range(2):
                push_planes.start(i, plane_of(i))
        else:
            for slot in range(2):
                flow_planes.start(slot)
                mu_planes.start(slot)

            def begin(i, state):
                flow_planes.start(i + 2)
                mu_planes.start(i + 2)
                push_planes.start(i, i + 1)
                return state

            lax.fori_loop(0, made, begin, 0)
            for slot in range(2):
                flow_planes.wait(slot)
                mu_planes.wait(slot)
            first_flux(cells, mu_cells, 1, flux, y_local)

        def body(i, state):
            slot, plane = (3 * i + 1 if edge else i + 1), plane_of(i)
            if edge:
                for back in range(2):
                    flow_planes.wait(slot - back)
                    mu_planes.wait(slot - back)
                first_flux(cells, mu_cells, slot, flux, y_local)
            flow_planes.wait(slot + 1)
            mu_planes.wait(slot + 1)
            push_planes.wait(i)
            advance_plane(
                cells,
                mu_cells,
                slot,
                (
                    lambda c: flow_before[c, plane],
                    lambda c: flow_after[c, plane],
                    lambda: mu_before[plane],
                    lambda: mu_after[plane],
                ),
                work,
                i,
                flux,
                y_local,
                z_cells,
            )
            stored(i).start()
            return state

        lax.fori_loop(0, made, body, 0)

        def finish(i, state):
            stored(i).wait()
            return state

        lax.fori_loop(0, made, finish, 0)

    operands = [flow, *flow_y, mu, *mu_y, push]
    specs = [anywhere, in_vmem, in_vmem, anywhere, in_vmem, in_vmem, anywhere]
    aliases = {}
    if edge:
        operands += [*flow_x, *mu_x, inner]
        specs += [anywhere] * 5
        aliases = {11: 0}
    return pl.pallas_call(
        kernel,
        in_specs=specs,
        out_specs=anywhere,
        out_shape=jax.ShapeDtypeStruct(flow.shape, jnp.float32),
        input_output_aliases=aliases,
        scratch_shapes=[
            pltpu.VMEM((3, slots, y_local, z_cells), jnp.float32),
            pltpu.SemaphoreType.DMA((slots,)),
            pltpu.VMEM((slots, y_local, z_cells), jnp.float32),
            pltpu.SemaphoreType.DMA((slots,)),
            pltpu.VMEM((3, made, y_local, z_cells), jnp.float32),
            pltpu.SemaphoreType.DMA((made,)),
            pltpu.SemaphoreType.DMA((made,)),
            pltpu.VMEM((3, y_local, z_cells), jnp.float32),
        ],
        compiler_params=pltpu.CompilerParams(vmem_limit_bytes=vmem_limit),
        name="advance_edge" if edge else "advance_inner",
    )(*operands)


def cosine_sine_basis(points, period, waves):
    columns, eigen = [], []
    for wave in waves:
        angle = 2.0 * np.pi * ((wave * np.arange(points)) % period) / period
        single = wave % period == 0 or 2 * wave == period
        size = math.sqrt((1.0 if single else 2.0) / period)
        columns.append(np.cos(angle) * size)
        eigen.append(math.sin(2.0 * math.pi * wave / period) ** 2)
        if not single:
            columns.append(np.sin(angle) * size)
            eigen.append(eigen[-1])
    return np.stack(columns, 1), np.array(eigen)


def halves(table):
    table = np.asarray(table, np.float32)
    high = table.astype(jnp.bfloat16)
    low = (table - high.astype(np.float32)).astype(jnp.bfloat16)
    return jnp.asarray(high), jnp.asarray(low)


def split(value):
    high = value.astype(jnp.bfloat16)
    return high, (value - high.astype(jnp.float32)).astype(jnp.bfloat16)


def triple_product(left, right):
    def product(one, two):
        return lax.dot_general(
            one, two, (((1,), (0,)), ((), ())), preferred_element_type=jnp.float32
        )

    return product(left[0], right[0]) + (product(left[0], right[1]) + product(left[1], right[0]))


def z_tables(z_cells):
    half = z_cells // 2
    even, eigen_even = cosine_sine_basis(half, z_cells, range(0, half + 1, 2))
    odd, eigen_odd = cosine_sine_basis(half, z_cells, range(1, half, 2))
    return even, odd, np.concatenate([eigen_even, eigen_odd])


def whole(*shape):
    return pl.BlockSpec(shape, lambda *index: (0,) * len(shape))


def modes_of(lines, even_high, even_low, odd_high, odd_low):
    half = lines.shape[1] // 2
    first, second = lines[:, :half], lines[:, half:]
    return jnp.concatenate(
        [
            triple_product(split(first + second), (even_high[...], even_low[...])),
            triple_product(split(first - second), (odd_high[...], odd_low[...])),
        ],
        1,
    )


def cells_of(modes, even_high, even_low, odd_high, odd_low):
    half = modes.shape[1] // 2
    first = triple_product(split(modes[:, :half]), (even_high[...], even_low[...]))
    second = triple_product(split(modes[:, half:]), (odd_high[...], odd_low[...]))
    return jnp.concatenate([first + second, first - second], 1)


def divergence_modes(flow, count):
    _, x_local, y_local, z_cells = flow.shape
    half, piece, strips = z_cells // 2, z_cells // count, y_local // 8
    step = min(8, x_local)
    even, odd, _ = z_tables(z_cells)
    tables = halves(even) + halves(odd)

    def kernel(
        flow_ref, even_high, even_low, odd_high, odd_low, out_ref,
        cells, semaphores, work, made, out_sem,
    ):
        planes = Planes(flow_ref, cells, semaphores)
        rows = row_numbers(z_cells)

        def begin(i, state):
            planes.start(i)
            return state

        lax.fori_loop(0, x_local, begin, 0)
        planes.wait(0)

        def stored(k):
            part = pl.ds(k * step, step)
            return pltpu.make_async_copy(made.at[:, part], out_ref.at[:, part], out_sem.at[k])

        def group(k, state):
            def plane(i, state):
                j = k * step + i

                @pl.when(j + 1 < x_local)
                def _():
                    planes.wait(j + 1)

                nearer = jnp.where(j > 0, 0.5, 0.0)
                further = jnp.where(j + 1 < x_local, 0.5, 0.0)
                last, following = jnp.maximum(j - 1, 0), jnp.minimum(j + 1, x_local - 1)
                across = [cells[1, j, rows_of(s), :] for s in range(strips)]
                up = [pltpu.roll(v, 7, 0) for v in across]
                down = [pltpu.roll(v, 1, 0) for v in across]
                for s in range(strips):
                    ahead = jnp.where(rows == 7, up[s + 1] if s + 1 < strips else 0.0, up[s])
                    behind = jnp.where(rows == 0, down[s - 1] if s else 0.0, down[s])
                    along = cells[2, j, rows_of(s), :]
                    work[i, rows_of(s), :] = (
                        further * cells[0, following, rows_of(s), :]
                        - nearer * cells[0, last, rows_of(s), :]
                    ) + 0.5 * (
                        (ahead - behind)
                        + (pltpu.roll(along, z_cells - 1, 1) - pltpu.roll(along, 1, 1))
                    )
                return state

            lax.fori_loop(0, step, plane, 0)
            modes = modes_of(
                work[...].reshape(step * y_local, z_cells), even_high, even_low, odd_high, odd_low
            )
            for n in range(count):
                made[n, pl.ds(k * step, step)] = modes[:, n * piece : (n + 1) * piece].reshape(
                    step, y_local, piece
                )
            stored(k).start()
            return state

        groups = x_local // step
        lax.fori_loop(0, groups, group, 0)
        for k in range(groups):
            stored(k).wait()

    return pl.pallas_call(
        kernel,
        in_specs=[anywhere] + [in_vmem] * 4,
        out_specs=anywhere,
        out_shape=jax.ShapeDtypeStruct((count, x_local, y_local, piece), jnp.float32),
        scratch_shapes=[
            pltpu.VMEM((3, x_local, y_local, z_cells), jnp.float32),
            pltpu.SemaphoreType.DMA((x_local,)),
            pltpu.VMEM((step, y_local, z_cells), jnp.float32),
            pltpu.VMEM((count, x_local, y_local, piece), jnp.float32),
            pltpu.SemaphoreType.DMA((x_local // step,)),
        ],
        name="divergence_modes",
    )(flow, *tables)


def add_halo_modes(modes, x_sides, y_sides):
    count, x_local, y_local, piece = modes.shape
    z_cells = count * piece
    even, odd, _ = z_tables(z_cells)
    tables = halves(even) + halves(odd)

    def kernel(
        modes_ref, low_ref, high_ref, before_ref, after_ref,
        even_high, even_low, odd_high, odd_low, out_ref, ends, lines, semaphores,
    ):
        def moves(back):
            pairs = [
                (ends.at[k], modes_ref.at[:, plane])
                for k, plane in enumerate((0, x_local - 1))
            ] + [
                (lines.at[k], modes_ref.at[:, 1 : x_local - 1, 8 * s : 8 * s + 8])
                for k, s in enumerate((0, y_local // 8 - 1))
            ]
            if back:
                pairs = [
                    (ends.at[k], out_ref.at[:, plane])
                    for k, plane in enumerate((0, x_local - 1))
                ] + [
                    (lines.at[k], out_ref.at[:, 1 : x_local - 1, 8 * s : 8 * s + 8])
                    for k, s in enumerate((0, y_local // 8 - 1))
                ]
                return [
                    pltpu.make_async_copy(here, there, semaphores.at[4 + i])
                    for i, (here, there) in enumerate(pairs)
                ]
            return [
                pltpu.make_async_copy(there, here, semaphores.at[i])
                for i, (here, there) in enumerate(pairs)
            ]

        loads, stores = moves(False), moves(True)
        for load in loads:
            load.start()
        added = modes_of(
            jnp.concatenate(
                [-0.5 * low_ref[0], 0.5 * high_ref[0], -0.5 * before_ref[...], 0.5 * after_ref[...]],
                0,
            ),
            even_high,
            even_low,
            odd_high,
            odd_low,
        )
        for load in loads:
            load.wait()
        rows = row_numbers(piece)
        for n in range(count):
            block = added[:, n * piece : (n + 1) * piece]
            side = [block[2 * y_local + k * x_local :][:x_local] for k in range(2)]
            for k, plane in enumerate((0, x_local - 1)):
                ends[k, n] = ends[k, n] + block[k * y_local : (k + 1) * y_local]
                for j, (strip, row) in enumerate(((0, 0), (y_local // 8 - 1, 7))):
                    part = pl.ds(8 * strip, 8)
                    ends[k, n, part, :] = ends[k, n, part, :] + jnp.where(
                        rows == row, side[j][plane : plane + 1], 0.0
                    )
            for j, row in enumerate((0, 7)):
                for x in range(1, x_local - 1):
                    lines[j, n, x - 1] = lines[j, n, x - 1] + jnp.where(
                        rows == row, side[j][x : x + 1], 0.0
                    )
        for store in stores:
            store.start()
        for store in stores:
            store.wait()

    return pl.pallas_call(
        kernel,
        in_specs=[anywhere] + [in_vmem] * 8,
        out_specs=anywhere,
        out_shape=jax.ShapeDtypeStruct(modes.shape, jnp.float32),
        input_output_aliases={0: 0},
        scratch_shapes=[
            pltpu.VMEM((2, count, y_local, piece), jnp.float32),
            pltpu.VMEM((2, count, x_local - 2, 8, piece), jnp.float32),
            pltpu.SemaphoreType.DMA((8,)),
        ],
        name="add_halo_modes",
    )(modes, *x_sides, *y_sides, *tables)


def corrected(flow, spectrum, y_sides):
    count, planes, y_local, piece = spectrum.shape
    x_local, z_cells = planes - 2, count * piece
    strips, part = y_local // 8, planes // 2
    even, odd, _ = z_tables(z_cells)
    tables = halves(even.T) + halves(odd.T)

    def kernel(
        flow_ref, in_ref, before_ref, after_ref,
        even_high, even_low, odd_high, odd_low, out_ref,
        modes, mode_sem, pressure, sides, work, flow_sem, out_sem,
    ):
        flow_planes = Planes(flow_ref, work, flow_sem)
        table_refs = (even_high, even_low, odd_high, odd_low)

        def load(k):
            span = pl.ds(k * part, part)
            return pltpu.make_async_copy(in_ref.at[:, span], modes.at[:, span], mode_sem.at[k])

        load(0).start()
        load(1).start()

        def begin(i, state):
            flow_planes.start(i)
            return state

        lax.fori_loop(0, x_local, begin, 0)
        sides[...] = cells_of(
            jnp.concatenate(
                [
                    jnp.concatenate([ref[n] for n in range(count)], 1)
                    for ref in (before_ref, after_ref)
                ],
                0,
            ),
            *table_refs,
        )
        rows = row_numbers(z_cells)

        def stored(i):
            return pltpu.make_async_copy(pick(work, i), pick(out_ref, i), out_sem.at[i])

        def plane(j, state):
            flow_planes.wait(j)
            values = [pressure[j + 1, rows_of(s), :] for s in range(strips)]
            up = [pltpu.roll(v, 7, 0) for v in values]
            down = [pltpu.roll(v, 1, 0) for v in values]
            for s in range(strips):
                ahead = up[s + 1] if s + 1 < strips else sides[pl.ds(x_local + j, 1), :]
                behind = down[s - 1] if s else sides[pl.ds(j, 1), :]
                slopes = (
                    pressure[j + 2, rows_of(s), :] - pressure[j, rows_of(s), :],
                    jnp.where(rows == 7, ahead, up[s]) - jnp.where(rows == 0, behind, down[s]),
                    pltpu.roll(values[s], z_cells - 1, 1) - pltpu.roll(values[s], 1, 1),
                )
                for c in range(3):
                    work[c, j, rows_of(s), :] = work[c, j, rows_of(s), :] - 0.5 * slopes[c]
            stored(j).start()
            return state

        for k in range(2):
            load(k).wait()
            span = pl.ds(k * part, part)
            pressure[span] = cells_of(
                jnp.concatenate(
                    [modes[n, span].reshape(part * y_local, piece) for n in range(count)], 1
                ),
                *table_refs,
            ).reshape(part, y_local, z_cells)
            lax.fori_loop(k * (part - 2), (part - 2) if k == 0 else x_local, plane, 0)

        def finish(i, state):
            stored(i).wait()
            return state

        lax.fori_loop(0, x_local, finish, 0)

    return pl.pallas_call(
        kernel,
        in_specs=[anywhere, anywhere] + [in_vmem] * 6,
        out_specs=anywhere,
        out_shape=jax.ShapeDtypeStruct(flow.shape, jnp.float32),
        scratch_shapes=[
            pltpu.VMEM(spectrum.shape, jnp.float32),
            pltpu.SemaphoreType.DMA((2,)),
            pltpu.VMEM((planes, y_local, z_cells), jnp.float32),
            pltpu.VMEM((2 * x_local, z_cells), jnp.float32),
            pltpu.VMEM(flow.shape, jnp.float32),
            pltpu.SemaphoreType.DMA((x_local,)),
            pltpu.SemaphoreType.DMA((x_local,)),
        ],
        compiler_params=pltpu.CompilerParams(vmem_limit_bytes=vmem_limit),
        name="corrected",
    )(flow, spectrum, *y_sides, *tables)


def y_forward(spectrum, ratio, wide_count):
    count, x_local, y_local, piece = spectrum.shape
    y_cells = count * y_local
    share = y_cells // wide_count
    table, _ = cosine_sine_basis(y_cells, y_cells, range(y_cells // 2 + 1))
    tables = halves(table.T)

    def kernel(in_ref, high_ref, low_ref, ratio_ref, modes_ref, carry_ref, sums, power):
        @pl.when(pl.program_id(0) == 0)
        def _():
            sums[...] = jnp.zeros_like(sums)
            power[...] = jnp.ones_like(power)

        planes = [
            jnp.concatenate([in_ref[n, side] for n in range(count)], 0) for side in range(2)
        ]
        modes = triple_product(
            (high_ref[...], low_ref[...]), split(jnp.concatenate(planes, 1))
        )
        r, pw = ratio_ref[...], power[...]
        for side in range(2):
            plane = modes[:, side * piece : (side + 1) * piece]
            modes_ref[side] = plane
            sums[side] = plane + r * sums[side]
            sums[2 + side] = sums[2 + side] + pw * plane
        power[...] = pw * r

        @pl.when(pl.program_id(0) == x_local // 2 - 1)
        def _():
            for kind in range(4):
                carry_ref[:, kind] = sums[kind].reshape(wide_count, share, piece)

    return pl.pallas_call(
        kernel,
        grid=(x_local // 2,),
        in_specs=[
            pl.BlockSpec((count, 2, y_local, piece), lambda i: (0, i, 0, 0)),
            whole(y_cells, y_cells),
            whole(y_cells, y_cells),
            whole(y_cells, piece),
        ],
        out_specs=[
            pl.BlockSpec((2, y_cells, piece), lambda i: (i, 0, 0)),
            whole(wide_count, 4, share, piece),
        ],
        out_shape=[
            jax.ShapeDtypeStruct((x_local, y_cells, piece), jnp.float32),
            jax.ShapeDtypeStruct((wide_count, 4, share, piece), jnp.float32),
        ],
        scratch_shapes=[
            pltpu.VMEM((4, y_cells, piece), jnp.float32),
            pltpu.VMEM((y_cells, piece), jnp.float32),
        ],
        name="y_forward",
    )(spectrum, *tables, ratio)


def power_of(value, exponent):
    result = None
    while exponent:
        if exponent & 1:
            result = value if result is None else result * value
        value = value * value
        exponent >>= 1
    return result


def join_carries(carries, ratio, block):
    count, kinds, share, piece = carries.shape

    def kernel(in_ref, ratio_ref, out_ref):
        step = power_of(ratio_ref[...], block)
        scale = 1.0 / (1.0 - power_of(step, count))
        for kind in range(kinds):
            order = list(range(count)) if kind < 2 else list(range(count))[::-1]
            total = in_ref[order[0], kind]
            for w in order[1:]:
                total = in_ref[w, kind] + step * total
            total = total * scale
            for w in order:
                out_ref[w, kind] = total
                total = in_ref[w, kind] + step * total

    return pl.pallas_call(
        kernel,
        out_shape=jax.ShapeDtypeStruct(carries.shape, jnp.float32),
        name="join_carries",
    )(carries, ratio)


def y_inverse(modes, carries, ratio, gain, count):
    x_local, y_cells, piece = modes.shape
    y_local, pairs = y_cells // count, x_local // 2
    wide_count, _, share, _ = carries.shape
    table, _ = cosine_sine_basis(y_cells, y_cells, range(y_cells // 2 + 1))
    tables = halves(table)

    def kernel(modes_ref, carry_ref, high_ref, low_ref, ratio_ref, gain_ref, out_ref, behind, ahead):
        step = pl.program_id(0)
        r = ratio_ref[...]

        def carry(kind):
            return carry_ref[:, kind].reshape(y_cells, piece)

        @pl.when(step == 0)
        def _():
            ahead[0] = carry(0)
            ahead[1] = carry(1)
            behind[2 * pairs + 1] = carry(2)

            def back(i, state):
                even, odd = state
                m = pairs - 1 - i
                behind[2 * m + 2] = r * odd
                behind[2 * m + 1] = r * even
                return (
                    modes_ref[2 * m] + r * even,
                    modes_ref[2 * m + 1] + r * odd,
                )

            _, odd = lax.fori_loop(0, pairs, back, (carry(2), carry(3)))
            behind[0] = r * odd

        even_plane = modes_ref[jnp.minimum(2 * step, x_local - 2)]
        odd_plane = modes_ref[jnp.maximum(2 * step - 1, 1)]
        even = r * ahead[0] + jnp.where(step < pairs, even_plane, 0.0)
        odd = jnp.where(step > 0, odd_plane + r * ahead[1], ahead[1])
        ahead[0] = even
        ahead[1] = odd
        gain_value = gain_ref[...]
        planes = jnp.concatenate(
            [gain_value * (odd + behind[2 * step]), gain_value * (even + behind[2 * step + 1])], 1
        )
        cells = triple_product((high_ref[...], low_ref[...]), split(planes))
        for n in range(count):
            for side in range(2):
                out_ref[n, side] = cells[
                    n * y_local : (n + 1) * y_local, side * piece : (side + 1) * piece
                ]

    return pl.pallas_call(
        kernel,
        grid=(pairs + 1,),
        in_specs=[
            whole(x_local, y_cells, piece),
            whole(wide_count, 4, share, piece),
            whole(y_cells, y_cells),
            whole(y_cells, y_cells),
            whole(y_cells, piece),
            whole(y_cells, piece),
        ],
        out_specs=pl.BlockSpec((count, 2, y_local, piece), lambda i: (0, i, 0, 0)),
        out_shape=jax.ShapeDtypeStruct((count, x_local + 2, y_local, piece), jnp.float32),
        scratch_shapes=[
            pltpu.VMEM((x_local + 2, y_cells, piece), jnp.float32),
            pltpu.VMEM((2, y_cells, piece), jnp.float32),
        ],
        name="y_inverse",
    )(modes, carries, *tables, ratio, gain)


def turn(value, axis):
    return lax.all_to_all(value, axis, split_axis=0, concat_axis=0, tiled=True)


def project(spectrum):
    count, x_local, y_local, piece = spectrum.shape
    y_cells, z_cells = count * y_local, count * piece
    wide_count = lax.axis_size("wide")
    _, eigen_y = cosine_sine_basis(y_cells, y_cells, range(y_cells // 2 + 1))
    eigen_z = jnp.asarray(z_tables(z_cells)[2], jnp.float32)
    own_z = lax.dynamic_slice_in_dim(eigen_z, lax.axis_index("narrow") * piece, piece)
    excess = 4.0 * (jnp.asarray(eigen_y, jnp.float32)[:, None] + own_z[None, :] + penalty)
    root = jnp.sqrt(excess * (4.0 + excess))
    ratio = 2.0 / (2.0 + excess + root)
    gain = -4.0 / root
    share = y_cells // wide_count
    own_ratio = lax.dynamic_slice_in_dim(ratio, lax.axis_index("wide") * share, share)
    modes, carries = y_forward(turn(spectrum, "narrow"), ratio, wide_count)
    carries = turn(join_carries(turn(carries, "wide"), own_ratio, x_local // 2), "wide")
    return turn(y_inverse(modes, carries, ratio, gain, count), "narrow")


def conduct(profile, spread):
    sides = (("wide", 0), ("narrow", 1))
    spread = with_halo(spread, sides, STEPS - 1, False)
    profile = with_halo(profile, sides, STEPS, False)
    for step in range(STEPS):
        center = profile[1:-1, 1:-1]
        near = (
            profile[2:, 1:-1] + profile[:-2, 1:-1] + profile[1:-1, 2:] + profile[1:-1, :-2]
        )
        ahead = jnp.pad(center[:, :, 1:], ((0, 0), (0, 0), (0, 1)))
        behind = jnp.pad(center[:, :, :-1], ((0, 0), (0, 0), (1, 0)))
        profile = center + spread * (near + ahead + behind - 6.0 * center)
        spread = spread[1:-1, 1:-1]
    return profile


def per_device(
    material_flow_vector,
    tool_push_density,
    tool_warmth_excess,
    substrate_warmth_excess,
    spread_coefficient,
    source_owner_sheet,
    source_part_line,
):
    flow = material_flow_vector
    flow_x, flow_y = ring(flow, "wide", 1), ring(flow, "narrow", 2)
    current, current_x, current_y = flow, flow_x, flow_y
    for section in range(PASSES):
        last = section + 1 == PASSES
        inner = viscosity_call(current, current_y, tool_warmth_excess, last)
        fields = viscosity_call(current, current_y, tool_warmth_excess, last, current_x, inner)
        mu = fields[0]
        mu_x, mu_y = ring(mu, "wide", 0), ring(mu, "narrow", 1)
        inner = advance_call(flow, flow_y, mu, mu_y, tool_push_density)
        current = advance_call(flow, flow_y, mu, mu_y, tool_push_density, flow_x, mu_x, inner)
        if not last:
            current_x, current_y = ring(current, "wide", 1), ring(current, "narrow", 2)
    heat_cells = fields[1]
    end_x = ring(current[0], "wide", 0)
    end_y = [side[:, 0] for side in ring(current[1], "narrow", 1)]
    modes = divergence_modes(current, lax.axis_size("narrow"))
    spectrum = project(add_halo_modes(modes, end_x, end_y))
    inner = spectrum[:, 1:-1]
    corrected_flow_vector = corrected(
        current, spectrum, [side[:, :, 0] for side in ring(inner, "narrow", 2)]
    )
    z_blocks = heat_cells.shape[0]
    slab_count = lax.axis_size("wide")
    component_lines = substrate_warmth_excess.shape[0] * substrate_warmth_excess.shape[1]
    targets = source_owner_sheet[:, 0] * component_lines + source_part_line
    partial_value = (
        jnp.zeros((slab_count * component_lines, 128), jnp.float32)
        .at[targets.reshape(-1, z_blocks).T.reshape(-1)]
        .add(heat_cells.reshape(-1, 128))
    )
    substrate_energy_input = lax.psum_scatter(
        partial_value.reshape(slab_count, component_lines, 128),
        "wide",
        scatter_dimension=0,
        tiled=True,
    )
    thermal_profile = substrate_warmth_excess + dissipation_factor * substrate_energy_input.reshape(
        substrate_warmth_excess.shape
    )
    return (corrected_flow_vector, conduct(thermal_profile, spread_coefficient))


def solution(mesh):
    return jax.shard_map(
        per_device,
        mesh=mesh,
        in_specs=(
            P(None, "wide", "narrow", None),
            P(None, "wide", "narrow", None),
            P("wide", "narrow", None),
            P("wide", "narrow", None),
            P("wide", "narrow", None),
            P(("wide", "narrow"), None),
            P(("wide", "narrow")),
        ),
        out_specs=(P(None, "wide", "narrow", None), P("wide", "narrow", None)),
        check_vma=False,
    )
```

```python
import math

import jax
import jax.numpy as jnp
import numpy as np
from jax import lax
from jax.experimental import pallas as pl
from jax.experimental.pallas import tpu as pltpu
from jax.sharding import PartitionSpec as P


PASSES = 2
STEPS = 3


time_step = 0.15
rate_base = 0.5
zener_energy = 4.0
stress_exponent = 5.0
penalty = 0.001
dissipation_factor = 0.1


def with_halo(x, sides, width, wrap):
    for axis, dim in sides:
        size, length = (lax.axis_size(axis), x.shape[dim])
        up = [(i, (i + 1) % size) for i in range(size if wrap else size - 1)]
        down = [(j, i) for i, j in up]
        last = lax.slice_in_dim(x, length - width, length, axis=dim)
        initial = lax.slice_in_dim(x, 0, width, axis=dim)
        before = lax.ppermute(last, axis, up)
        after = lax.ppermute(initial, axis, down)
        x = jnp.concatenate([before, x, after], axis=dim)
    return x


def shift(value, axis, by):
    size = lax.axis_size(axis)
    return lax.ppermute(value, axis, [(i, (i + by) % size) for i in range(size)])


def ring(value, axis, dim):
    length = value.shape[dim]
    last = lax.slice_in_dim(value, length - 1, length, axis=dim)
    initial = lax.slice_in_dim(value, 0, 1, axis=dim)
    return shift(last, axis, 1), shift(initial, axis, -1)


anywhere = pl.BlockSpec(memory_space=pl.ANY)
in_smem = pl.BlockSpec(memory_space=pltpu.SMEM)
in_vmem = pl.BlockSpec(memory_space=pltpu.VMEM)
scaled_mu = 0.5 * time_step


def row_numbers(width):
    return lax.broadcasted_iota(jnp.int32, (8, width), 0)


def rows_of(strip):
    return pl.ds(8 * strip, 8)


def pick(ref, index):
    return ref.at[:, index] if len(ref.shape) == 4 else ref.at[index]


class Planes:
    def __init__(self, source, target, semaphores, listed=None):
        self.source, self.target, self.semaphores = source, target, semaphores
        self.listed = listed

    def copy(self, slot, ref, plane):
        return pltpu.make_async_copy(
            pick(ref, plane), pick(self.target, slot), self.semaphores.at[slot]
        )

    def start(self, slot, plane=None):
        if self.listed is None:
            self.copy(slot, self.source, slot if plane is None else plane).start()
        else:
            self.copy(slot, *self.listed[slot]).start()

    def wait(self, slot):
        self.copy(slot, self.source, 0).wait()


def edge_list(ref, low, high, x_local):
    return [(low, 0), (ref, 0), (ref, 1), (ref, x_local - 2), (ref, x_local - 1), (high, 0)]


def viscosity_plane(cells, slot, edges, warmth, warm_slot, outs, out_slot, y_local, z_cells):
    strips, rows = y_local // 8, row_numbers(z_cells)
    before, after = edges
    values = [[cells[c, slot, rows_of(s), :] for s in range(strips)] for c in range(3)]
    up = [[pltpu.roll(v, 7, 0) for v in row] for row in values]
    down = [[pltpu.roll(v, 1, 0) for v in row] for row in values]
    for s in range(strips):
        along_x, along_y, along_z = [], [], []
        for c in range(3):
            value = values[c][s]
            along_x.append(cells[c, slot + 1, rows_of(s), :] - cells[c, slot - 1, rows_of(s), :])
            ahead = jnp.where(rows == 7, up[c][s + 1] if s + 1 < strips else after(c), up[c][s])
            behind = jnp.where(rows == 0, down[c][s - 1] if s else before(c), down[c][s])
            along_y.append(ahead - behind)
            along_z.append(pltpu.roll(value, z_cells - 1, 1) - pltpu.roll(value, 1, 1))
        s_xy = along_y[0] + along_x[1]
        s_xz = along_z[0] + along_x[2]
        s_yz = along_z[1] + along_y[2]
        extra = 0.5 * (
            along_x[0] * along_x[0] + along_y[1] * along_y[1] + along_z[2] * along_z[2]
        ) + 0.25 * (s_xy * s_xy + s_xz * s_xz + s_yz * s_yz)
        rate_sq = rate_base**2 + extra
        value = jnp.exp(
            (0.5 / stress_exponent) * jnp.log(rate_sq)
            + (zener_energy / stress_exponent) * (1.0 / warmth[warm_slot, rows_of(s), :] - 1.0)
        )
        square = value * value + 1.0
        mu = jnp.log(value + square * lax.rsqrt(square)) * lax.rsqrt(rate_sq)
        outs[0][out_slot, rows_of(s), :] = mu * (scaled_mu / 3.0)
        if len(outs) > 1:
            heat = (mu * (1.0 / 3.0)) * extra
            for b in range(z_cells // 128):
                outs[1][b, out_slot, rows_of(s), :] = heat[:, b * 128 : (b + 1) * 128]


def viscosity_call(flow, y_sides, warmth, with_heat, x_sides=None, inner=None):
    _, x_local, y_local, z_cells = flow.shape
    z_blocks = z_cells // 128
    edge = x_sides is not None
    slots, made = (6, 2) if edge else (x_local, x_local - 2)
    outputs = 2 if with_heat else 1

    def kernel(*refs):
        flow_ref, before_ref, after_ref, warmth_ref = refs[:4]
        rest = list(refs[4:])
        listed = None
        if edge:
            low, high = rest[:2]
            listed = edge_list(flow_ref, low, high, x_local)
            rest = rest[2 + outputs :]
        out_refs, rest = rest[:outputs], rest[outputs:]
        cells, cell_sem, warm, warm_sem = rest[:4]
        outs, out_sems = rest[4 : 4 + outputs], rest[4 + outputs :]
        flow_planes = Planes(flow_ref, cells, cell_sem, listed)
        warm_planes = Planes(warmth_ref, warm, warm_sem)

        def plane_of(i):
            return i * (x_local - 1) if edge else i + 1

        def slot_of(i):
            return 3 * i + 1 if edge else i + 1

        def stored(k, i):
            return pltpu.make_async_copy(
                pick(outs[k], i), pick(out_refs[k], plane_of(i)), out_sems[k].at[i]
            )

        if edge:
            for slot in range(6):
                flow_planes.start(slot)
            for i in range(2):
                warm_planes.start(i, plane_of(i))
        else:
            flow_planes.start(0)
            flow_planes.start(1)

            def begin(i, state):
                flow_planes.start(i + 2)
                warm_planes.start(i, i + 1)
                return state

            lax.fori_loop(0, made, begin, 0)
            flow_planes.wait(0)
            flow_planes.wait(1)

        def body(i, state):
            slot, plane = slot_of(i), plane_of(i)
            if edge:
                flow_planes.wait(slot - 1)
                flow_planes.wait(slot)
            flow_planes.wait(slot + 1)
            warm_planes.wait(i)
            viscosity_plane(
                cells,
                slot,
                (lambda c: before_ref[c, plane], lambda c: after_ref[c, plane]),
                warm,
                i,
                outs,
                i,
                y_local,
                z_cells,
            )
            for k in range(outputs):
                stored(k, i).start()
            return state

        lax.fori_loop(0, made, body, 0)

        def finish(i, state):
            for k in range(outputs):
                stored(k, i).wait()
            return state

        lax.fori_loop(0, made, finish, 0)

    shapes = [(x_local, y_local, z_cells), (z_blocks, x_local, y_local, 128)][:outputs]
    held = [(made, y_local, z_cells), (z_blocks, made, y_local, 128)][:outputs]
    operands = [flow, *y_sides, warmth]
    specs = [anywhere, in_vmem, in_vmem, anywhere]
    aliases = {}
    if edge:
        operands += [*x_sides, *inner]
        specs += [anywhere] * (2 + outputs)
        aliases = {6 + k: k for k in range(outputs)}
    return pl.pallas_call(
        kernel,
        in_specs=specs,
        out_specs=[anywhere] * outputs,
        out_shape=[jax.ShapeDtypeStruct(shape, jnp.float32) for shape in shapes],
        input_output_aliases=aliases,
        scratch_shapes=[
            pltpu.VMEM((3, slots, y_local, z_cells), jnp.float32),
            pltpu.SemaphoreType.DMA((slots,)),
            pltpu.VMEM((made, y_local, z_cells), jnp.float32),
            pltpu.SemaphoreType.DMA((made,)),
        ]
        + [pltpu.VMEM(shape, jnp.float32) for shape in held]
        + [pltpu.SemaphoreType.DMA((made,))] * outputs,
        compiler_params=pltpu.CompilerParams(vmem_limit_bytes=vmem_limit),
        name="viscosity_edge" if edge else "viscosity_inner",
    )(*operands)


vmem_limit = 48 << 20


def advance_plane(cells, mu, slot, edges, push, out_slot, flux, y_local, z_cells):
    strips, rows = y_local // 8, row_numbers(z_cells)
    flow_before, flow_after, mu_before, mu_after = edges
    m = [mu[slot, rows_of(s), :] for s in range(strips)]
    m_up = [pltpu.roll(v, 7, 0) for v in m]
    sums_y = [
        m[s] + jnp.where(rows == 7, m_up[s + 1] if s + 1 < strips else mu_after(), m_up[s])
        for s in range(strips)
    ]
    first_sum = mu_before() + mu[slot, pl.ds(0, 1), :]
    values = [[cells[c, slot, rows_of(s), :] for s in range(strips)] for c in range(3)]
    up = [[pltpu.roll(v, 7, 0) for v in row] for row in values]
    carried = [
        first_sum * (cells[c, slot, pl.ds(0, 1), :] - flow_before(c)) for c in range(3)
    ]
    for s in range(strips):
        sum_x = m[s] + mu[slot + 1, rows_of(s), :]
        sum_z_ahead = m[s] + pltpu.roll(m[s], z_cells - 1, 1)
        sum_z_behind = m[s] + pltpu.roll(m[s], 1, 1)
        for c in range(3):
            value = values[c][s]
            flux_x = sum_x * (cells[c, slot + 1, rows_of(s), :] - value)
            ahead = jnp.where(
                rows == 7, up[c][s + 1] if s + 1 < strips else flow_after(c), up[c][s]
            )
            flux_y = sums_y[s] * (ahead - value)
            turned = pltpu.roll(flux_y, 1, 0)
            total = (flux_x - flux[c, rows_of(s), :]) + (
                flux_y - jnp.where(rows == 0, carried[c], turned)
            ) + (
                sum_z_ahead * (pltpu.roll(value, z_cells - 1, 1) - value)
                - sum_z_behind * (value - pltpu.roll(value, 1, 1))
            )
            flux[c, rows_of(s), :] = flux_x
            carried[c] = turned
            push[c, out_slot, rows_of(s), :] = (
                value + time_step * push[c, out_slot, rows_of(s), :] + total
            )


def first_flux(cells, mu, slot, flux, y_local):
    for s in range(y_local // 8):
        sum_x = mu[slot - 1, rows_of(s), :] + mu[slot, rows_of(s), :]
        for c in range(3):
            flux[c, rows_of(s), :] = sum_x * (
                cells[c, slot, rows_of(s), :] - cells[c, slot - 1, rows_of(s), :]
            )


def advance_call(flow, flow_y, mu, mu_y, push, flow_x=None, mu_x=None, inner=None):
    _, x_local, y_local, z_cells = flow.shape
    edge = flow_x is not None
    slots, made = (6, 2) if edge else (x_local, x_local - 2)

    def kernel(*refs):
        flow_ref, flow_before, flow_after, mu_ref, mu_before, mu_after, push_ref = refs[:7]
        rest = refs[7:]
        flow_listed = mu_listed = None
        if edge:
            flow_listed = edge_list(flow_ref, rest[0], rest[1], x_local)
            mu_listed = edge_list(mu_ref, rest[2], rest[3], x_local)
            rest = rest[5:]
        out_ref, cells, cell_sem, mu_cells, mu_sem, work, work_sem, out_sem, flux = rest
        flow_planes = Planes(flow_ref, cells, cell_sem, flow_listed)
        mu_planes = Planes(mu_ref, mu_cells, mu_sem, mu_listed)
        push_planes = Planes(push_ref, work, work_sem)

        def plane_of(i):
            return i * (x_local - 1) if edge else i + 1

        def stored(i):
            return pltpu.make_async_copy(
                pick(work, i), pick(out_ref, plane_of(i)), out_sem.at[i]
            )

        if edge:
            for slot in range(6):
                flow_planes.start(slot)
                mu_planes.start(slot)
            for i in range(2):
                push_planes.start(i, plane_of(i))
        else:
            for slot in range(2):
                flow_planes.start(slot)
                mu_planes.start(slot)

            def begin(i, state):
                flow_planes.start(i + 2)
                mu_planes.start(i + 2)
                push_planes.start(i, i + 1)
                return state

            lax.fori_loop(0, made, begin, 0)
            for slot in range(2):
                flow_planes.wait(slot)
                mu_planes.wait(slot)
            first_flux(cells, mu_cells, 1, flux, y_local)

        def body(i, state):
            slot, plane = (3 * i + 1 if edge else i + 1), plane_of(i)
            if edge:
                for back in range(2):
                    flow_planes.wait(slot - back)
                    mu_planes.wait(slot - back)
                first_flux(cells, mu_cells, slot, flux, y_local)
            flow_planes.wait(slot + 1)
            mu_planes.wait(slot + 1)
            push_planes.wait(i)
            advance_plane(
                cells,
                mu_cells,
                slot,
                (
                    lambda c: flow_before[c, plane],
                    lambda c: flow_after[c, plane],
                    lambda: mu_before[plane],
                    lambda: mu_after[plane],
                ),
                work,
                i,
                flux,
                y_local,
                z_cells,
            )
            stored(i).start()
            return state

        lax.fori_loop(0, made, body, 0)

        def finish(i, state):
            stored(i).wait()
            return state

        lax.fori_loop(0, made, finish, 0)

    operands = [flow, *flow_y, mu, *mu_y, push]
    specs = [anywhere, in_vmem, in_vmem, anywhere, in_vmem, in_vmem, anywhere]
    aliases = {}
    if edge:
        operands += [*flow_x, *mu_x, inner]
        specs += [anywhere] * 5
        aliases = {11: 0}
    return pl.pallas_call(
        kernel,
        in_specs=specs,
        out_specs=anywhere,
        out_shape=jax.ShapeDtypeStruct(flow.shape, jnp.float32),
        input_output_aliases=aliases,
        scratch_shapes=[
            pltpu.VMEM((3, slots, y_local, z_cells), jnp.float32),
            pltpu.SemaphoreType.DMA((slots,)),
            pltpu.VMEM((slots, y_local, z_cells), jnp.float32),
            pltpu.SemaphoreType.DMA((slots,)),
            pltpu.VMEM((3, made, y_local, z_cells), jnp.float32),
            pltpu.SemaphoreType.DMA((made,)),
            pltpu.SemaphoreType.DMA((made,)),
            pltpu.VMEM((3, y_local, z_cells), jnp.float32),
        ],
        compiler_params=pltpu.CompilerParams(vmem_limit_bytes=vmem_limit),
        name="advance_edge" if edge else "advance_inner",
    )(*operands)


def cosine_sine_basis(points, period, waves):
    columns, eigen = [], []
    for wave in waves:
        angle = 2.0 * np.pi * ((wave * np.arange(points)) % period) / period
        single = wave % period == 0 or 2 * wave == period
        size = math.sqrt((1.0 if single else 2.0) / period)
        columns.append(np.cos(angle) * size)
        eigen.append(math.sin(2.0 * math.pi * wave / period) ** 2)
        if not single:
            columns.append(np.sin(angle) * size)
            eigen.append(eigen[-1])
    return np.stack(columns, 1), np.array(eigen)


def halves(table):
    table = np.asarray(table, np.float32)
    high = table.astype(jnp.bfloat16)
    low = (table - high.astype(np.float32)).astype(jnp.bfloat16)
    return jnp.asarray(high), jnp.asarray(low)


def split(value):
    high = value.astype(jnp.bfloat16)
    return high, (value - high.astype(jnp.float32)).astype(jnp.bfloat16)


def triple_product(left, right):
    def product(one, two):
        return lax.dot_general(
            one, two, (((1,), (0,)), ((), ())), preferred_element_type=jnp.float32
        )

    return product(left[0], right[0]) + (product(left[0], right[1]) + product(left[1], right[0]))


def z_tables(z_cells):
    half = z_cells // 2
    even, eigen_even = cosine_sine_basis(half, z_cells, range(0, half + 1, 2))
    odd, eigen_odd = cosine_sine_basis(half, z_cells, range(1, half, 2))
    return even, odd, np.concatenate([eigen_even, eigen_odd])


def modes_of(lines, even_high, even_low, odd_high, odd_low):
    half = lines.shape[1] // 2
    first, second = lines[:, :half], lines[:, half:]
    return jnp.concatenate(
        [
            triple_product(split(first + second), (even_high[...], even_low[...])),
            triple_product(split(first - second), (odd_high[...], odd_low[...])),
        ],
        1,
    )


def cells_of(modes, even_high, even_low, odd_high, odd_low):
    half = modes.shape[1] // 2
    first = triple_product(split(modes[:, :half]), (even_high[...], even_low[...]))
    second = triple_product(split(modes[:, half:]), (odd_high[...], odd_low[...]))
    return jnp.concatenate([first + second, first - second], 1)


def divergence_modes(flow, own, count):
    _, x_local, y_local, z_cells = flow.shape
    piece, strips = z_cells // count, y_local // 8
    step, pairs = min(8, x_local), x_local // 2
    groups = x_local // step
    even, odd, _ = z_tables(z_cells)
    tables = halves(even) + halves(odd)

    def kernel(
        flow_ref, own_ref, even_high, even_low, odd_high, odd_low, *rest
    ):
        out_refs, rest = rest[: 2 * count], rest[2 * count :]
        cells, semaphores, work, first, second, out_sem = rest
        rows = row_numbers(z_cells)
        me = own_ref[0]

        def load(k):
            part = pl.ds(k * step, step)
            return pltpu.make_async_copy(
                flow_ref.at[:, part], cells.at[:, part], semaphores.at[k]
            )

        for k in range(groups):
            load(k).start()
        load(0).wait()

        def stored(k, parity):
            part = pl.ds(k * (step // 2), step // 2)
            return [
                pltpu.make_async_copy(
                    (first, second)[parity].at[me ^ n, part],
                    out_refs[parity * count + n].at[part],
                    out_sem.at[2 * k + parity, n],
                )
                for n in range(count)
            ]

        def group(k, state):
            @pl.when(k + 1 < groups)
            def _():
                load(k + 1).wait()

            def plane(i, state):
                j = k * step + i
                nearer = jnp.where(j > 0, 0.5, 0.0)
                further = jnp.where(j + 1 < x_local, 0.5, 0.0)
                last, following = jnp.maximum(j - 1, 0), jnp.minimum(j + 1, x_local - 1)
                across = [cells[1, j, rows_of(s), :] for s in range(strips)]
                up = [pltpu.roll(v, 7, 0) for v in across]
                down = [pltpu.roll(v, 1, 0) for v in across]
                for s in range(strips):
                    ahead = jnp.where(rows == 7, up[s + 1] if s + 1 < strips else 0.0, up[s])
                    behind = jnp.where(rows == 0, down[s - 1] if s else 0.0, down[s])
                    along = cells[2, j, rows_of(s), :]
                    work[i, rows_of(s), :] = (
                        further * cells[0, following, rows_of(s), :]
                        - nearer * cells[0, last, rows_of(s), :]
                    ) + 0.5 * (
                        (ahead - behind)
                        + (pltpu.roll(along, z_cells - 1, 1) - pltpu.roll(along, 1, 1))
                    )
                return state

            lax.fori_loop(0, step, plane, 0)
            modes = modes_of(
                work[...].reshape(step * y_local, z_cells), even_high, even_low, odd_high, odd_low
            )
            for n in range(count):
                for i in range(step):
                    (first, second)[i % 2][n, k * (step // 2) + i // 2] = modes[
                        i * y_local : (i + 1) * y_local, n * piece : (n + 1) * piece
                    ]
            for parity in range(2):
                for copy in stored(k, parity):
                    copy.start()
            return state

        lax.fori_loop(0, groups, group, 0)
        for k in range(groups):
            for parity in range(2):
                for copy in stored(k, parity):
                    copy.wait()

    made = (count, pairs, y_local, piece)
    outputs = pl.pallas_call(
        kernel,
        in_specs=[anywhere, in_smem] + [in_vmem] * 4,
        out_specs=[anywhere] * (2 * count),
        out_shape=[jax.ShapeDtypeStruct(made[1:], jnp.float32)] * (2 * count),
        scratch_shapes=[
            pltpu.VMEM((3, x_local, y_local, z_cells), jnp.float32),
            pltpu.SemaphoreType.DMA((groups,)),
            pltpu.VMEM((step, y_local, z_cells), jnp.float32),
            pltpu.VMEM(made, jnp.float32),
            pltpu.VMEM(made, jnp.float32),
            pltpu.SemaphoreType.DMA((2 * groups, count)),
        ],
        name="divergence_modes",
    )(flow, own, *tables)
    return outputs[:count], outputs[count:]


def add_halo_modes(modes, own, end, y_sides, parity):
    count = len(modes)
    pairs, y_local, piece = modes[0].shape
    z_cells = count * piece
    tail = pairs - 1 if parity else 0
    even, odd, _ = z_tables(z_cells)
    tables = halves(even) + halves(odd)
    strips = (0, y_local // 8 - 1)

    def kernel(*refs):
        modes_refs, refs = refs[:count], refs[count:]
        own_ref, end_ref, before_ref, after_ref = refs[:4]
        table_refs, refs = refs[4:8], refs[8:]
        out_refs, (plane, lines, added, semaphores) = refs[:count], refs[count:]

        def moves(refs):
            return [(plane.at[n], refs[n].at[tail]) for n in range(count)] + [
                (lines.at[k, n], refs[n].at[:, 8 * s : 8 * s + 8])
                for k, s in enumerate(strips)
                for n in range(count)
            ]

        loads = [
            pltpu.make_async_copy(there, here, semaphores.at[i])
            for i, (here, there) in enumerate(moves(modes_refs))
        ]
        for load in loads:
            load.start()
        sign = 0.5 if parity else -0.5
        result = modes_of(
            jnp.concatenate(
                [sign * end_ref[0], -0.5 * before_ref[...], 0.5 * after_ref[...]], 0
            ),
            *table_refs,
        )
        for n in range(count):
            added[n] = result[:, n * piece : (n + 1) * piece]
        for load in loads:
            load.wait()
        rows = row_numbers(piece)
        for n in range(count):
            block = added.at[own_ref[0] ^ n]
            for j, row in enumerate((0, 7)):
                for x in range(pairs):
                    side = block[pl.ds(y_local + j * pairs + x, 1), :]
                    lines[j, n, x] = lines[j, n, x] + jnp.where(rows == row, side, 0.0)
            plane[n] = plane[n] + block[pl.ds(0, y_local), :]
            for j, s in enumerate(strips):
                lines[j, n, tail] = lines[j, n, tail] + block[rows_of(s), :]
        inside = [
            (plane.at[n, 8 : y_local - 8], out_refs[n].at[tail, 8 : y_local - 8])
            for n in range(count)
        ]
        stores = [
            pltpu.make_async_copy(here, there, semaphores.at[3 * count + i])
            for i, (here, there) in enumerate(inside + moves(out_refs)[count:])
        ]
        for store in stores:
            store.start()
        for store in stores:
            store.wait()

    return pl.pallas_call(
        kernel,
        in_specs=[anywhere] * count + [in_smem] + [in_vmem] * 7,
        out_specs=[anywhere] * count,
        out_shape=[jax.ShapeDtypeStruct(modes[0].shape, jnp.float32)] * count,
        input_output_aliases={n: n for n in range(count)},
        scratch_shapes=[
            pltpu.VMEM((count, y_local, piece), jnp.float32),
            pltpu.VMEM((2, count, pairs, 8, piece), jnp.float32),
            pltpu.VMEM((count, y_local + 2 * pairs, piece), jnp.float32),
            pltpu.SemaphoreType.DMA((6 * count,)),
        ],
        name="add_halo_modes",
    )(*modes, own, end, *y_sides, *tables)


def pressure_planes(spectrum, own):
    count = len(spectrum)
    planes, y_local, piece = spectrum[0].shape
    z_cells = count * piece
    even, odd, _ = z_tables(z_cells)
    tables = halves(even.T) + halves(odd.T)

    def kernel(*refs):
        in_refs, refs = refs[:count], refs[count:]
        own_ref, table_refs, (out_ref, modes, semaphores) = refs[0], refs[1:5], refs[5:]
        loads = [
            pltpu.make_async_copy(in_refs[k], modes.at[own_ref[0] ^ k], semaphores.at[k])
            for k in range(count)
        ]
        for load in loads:
            load.start()
        for load in loads:
            load.wait()
        out_ref[...] = cells_of(
            jnp.concatenate(
                [modes[n].reshape(planes * y_local, piece) for n in range(count)], 1
            ),
            *table_refs,
        ).reshape(planes, y_local, z_cells)

    return pl.pallas_call(
        kernel,
        in_specs=[anywhere] * count + [in_smem] + [in_vmem] * 4,
        out_specs=in_vmem,
        out_shape=jax.ShapeDtypeStruct((planes, y_local, z_cells), jnp.float32),
        scratch_shapes=[
            pltpu.VMEM((count, planes, y_local, piece), jnp.float32),
            pltpu.SemaphoreType.DMA((count,)),
        ],
        compiler_params=pltpu.CompilerParams(vmem_limit_bytes=vmem_limit),
        name="pressure_planes",
    )(*spectrum, own, *tables)


def corrected(flow, even_pressure, odd_spectrum, own, sides):
    count = len(odd_spectrum)
    planes, y_local, piece = odd_spectrum[0].shape
    pairs = planes - 1
    x_local, z_cells = 2 * pairs, count * piece
    strips, cut = y_local // 8, planes // 2 + 1
    spans = ((0, cut), (cut, planes))
    even, odd, _ = z_tables(z_cells)
    tables = halves(even.T) + halves(odd.T)

    def kernel(*refs):
        in_refs, refs = refs[:count], refs[count:]
        own_ref, flow_ref, even_ref, side_ref = refs[:4]
        table_refs, refs = refs[4:8], refs[8:]
        out_ref, modes, mode_sem, pressure, lines, work, flow_sem, out_sem = refs
        me = own_ref[0]

        def load(k):
            span = pl.ds(spans[k][0], spans[k][1] - spans[k][0])
            return [
                pltpu.make_async_copy(
                    in_refs[n].at[span], modes.at[me ^ n, span], mode_sem.at[k, n]
                )
                for n in range(count)
            ]

        def brought(k):
            span = pl.ds(k * pairs, pairs)
            return pltpu.make_async_copy(flow_ref.at[:, span], work.at[:, span], flow_sem.at[k])

        for k in range(2):
            for copy in load(k):
                copy.start()
        for k in range(2):
            brought(k).start()
        senders = ((me + count - 1) % count, (me + 1) % count)
        lines[...] = cells_of(
            jnp.concatenate(
                [
                    jnp.concatenate([side_ref[i, senders[i % 2] ^ n] for i in range(4)], 0)
                    for n in range(count)
                ],
                1,
            ),
            *table_refs,
        )
        rows = row_numbers(z_cells)

        def stored(i):
            return pltpu.make_async_copy(pick(work, i), pick(out_ref, i), out_sem.at[i])

        def correct(j, center, low, high, side):
            values = [center[rows_of(s), :] for s in range(strips)]
            up = [pltpu.roll(v, 7, 0) for v in values]
            down = [pltpu.roll(v, 1, 0) for v in values]
            for s in range(strips):
                ahead = up[s + 1] if s + 1 < strips else lines[pl.ds(side + pairs, 1), :]
                behind = down[s - 1] if s else lines[pl.ds(side, 1), :]
                slopes = (
                    high[rows_of(s), :] - low[rows_of(s), :],
                    jnp.where(rows == 7, ahead, up[s]) - jnp.where(rows == 0, behind, down[s]),
                    pltpu.roll(values[s], z_cells - 1, 1) - pltpu.roll(values[s], 1, 1),
                )
                for c in range(3):
                    work[c, j, rows_of(s), :] = work[c, j, rows_of(s), :] - 0.5 * slopes[c]
            stored(j).start()

        def pair(k, state):
            correct(2 * k, even_ref.at[k], pressure.at[k], pressure.at[k + 1], k)
            correct(
                2 * k + 1, pressure.at[k + 1], even_ref.at[k], even_ref.at[k + 1], 2 * pairs + k
            )
            return state

        for k in range(2):
            for copy in load(k):
                copy.wait()
            start, stop = spans[k]
            pressure[start:stop] = cells_of(
                jnp.concatenate(
                    [
                        modes[n, start:stop].reshape((stop - start) * y_local, piece)
                        for n in range(count)
                    ],
                    1,
                ),
                *table_refs,
            ).reshape(stop - start, y_local, z_cells)
            brought(k).wait()
            lax.fori_loop(*((0, cut - 1) if k == 0 else (cut - 1, pairs)), pair, 0)

        def finish(i, state):
            stored(i).wait()
            return state

        lax.fori_loop(0, x_local, finish, 0)

    return pl.pallas_call(
        kernel,
        in_specs=[anywhere] * count + [in_smem, anywhere] + [in_vmem] * 6,
        out_specs=anywhere,
        out_shape=jax.ShapeDtypeStruct(flow.shape, jnp.float32),
        scratch_shapes=[
            pltpu.VMEM((count, planes, y_local, piece), jnp.float32),
            pltpu.SemaphoreType.DMA((2, count)),
            pltpu.VMEM((planes, y_local, z_cells), jnp.float32),
            pltpu.VMEM((4 * pairs, z_cells), jnp.float32),
            pltpu.VMEM(flow.shape, jnp.float32),
            pltpu.SemaphoreType.DMA((2,)),
            pltpu.SemaphoreType.DMA((x_local,)),
        ],
        compiler_params=pltpu.CompilerParams(vmem_limit_bytes=vmem_limit),
        name="corrected",
    )(*odd_spectrum, own, flow, even_pressure, sides, *tables)


def y_forward(spectrum, own, ratio, wide_count):
    count = len(spectrum)
    pairs, y_local, piece = spectrum[0].shape
    y_cells = count * y_local
    share, steps, group = y_cells // wide_count, pairs // 2, max(2, pairs // 4)
    table, _ = cosine_sine_basis(y_cells, y_cells, range(y_cells // 2 + 1))
    tables = halves(table.T)

    def kernel(*refs):
        in_refs, refs = refs[:count], refs[count:]
        own_ref, high_ref, low_ref, ratio_ref, modes_ref, carry_ref = refs[:6]
        lines, sems, sums, power = refs[6:]

        def load(k):
            part = pl.ds(k * group, group)
            return [
                pltpu.make_async_copy(
                    in_refs[n].at[part], lines.at[own_ref[0] ^ n, part], sems.at[k, n]
                )
                for n in range(count)
            ]

        for k in range(pairs // group):
            for copy in load(k):
                copy.start()
        sums[...] = jnp.zeros_like(sums)
        power[...] = jnp.ones_like(power)

        def body(k, state):
            @pl.when(k % (group // 2) == 0)
            def _():
                for copy in load(k // (group // 2)):
                    copy.wait()

            planes = [
                jnp.concatenate([lines[n, 2 * k + side] for n in range(count)], 0)
                for side in range(2)
            ]
            modes = triple_product(
                (high_ref[...], low_ref[...]), split(jnp.concatenate(planes, 1))
            )
            r, pw = ratio_ref[...], power[...]
            one, two = modes[:, :piece], modes[:, piece:]
            modes_ref[2 * k] = one
            modes_ref[2 * k + 1] = two
            sums[0] = two + r * (one + r * sums[0])
            sums[1] = sums[1] + pw * (one + r * two)
            power[...] = pw * (r * r)
            return state

        lax.fori_loop(0, steps, body, 0)
        for kind in range(2):
            carry_ref[:, kind] = sums[kind].reshape(wide_count, share, piece)

    return pl.pallas_call(
        kernel,
        in_specs=[anywhere] * count + [in_smem] + [in_vmem] * 3,
        out_specs=[in_vmem, in_vmem],
        out_shape=[
            jax.ShapeDtypeStruct((pairs, y_cells, piece), jnp.float32),
            jax.ShapeDtypeStruct((wide_count, 2, share, piece), jnp.float32),
        ],
        scratch_shapes=[
            pltpu.VMEM((count, pairs, y_local, piece), jnp.float32),
            pltpu.SemaphoreType.DMA((pairs // group, count)),
            pltpu.VMEM((2, y_cells, piece), jnp.float32),
            pltpu.VMEM((y_cells, piece), jnp.float32),
        ],
        compiler_params=pltpu.CompilerParams(vmem_limit_bytes=24 << 20),
        name="y_forward",
    )(*spectrum, own, *tables, ratio)


def power_of(value, exponent):
    result = None
    while exponent:
        if exponent & 1:
            result = value if result is None else result * value
        value = value * value
        exponent >>= 1
    return result


def join_carries(carries, ratio, block):
    count, kinds, _, _ = carries.shape

    def kernel(in_ref, ratio_ref, out_ref):
        step = power_of(ratio_ref[...], block)
        scale = 1.0 / (1.0 - power_of(step, count))
        for kind in range(kinds):
            order = list(range(count)) if kind == 0 else list(range(count))[::-1]
            total = in_ref[order[0], kind]
            for w in order[1:]:
                total = in_ref[w, kind] + step * total
            total = total * scale
            for w in order:
                out_ref[w, kind] = total
                total = in_ref[w, kind] + step * total

    return pl.pallas_call(
        kernel,
        in_specs=[in_vmem] * 2,
        out_specs=in_vmem,
        out_shape=jax.ShapeDtypeStruct(carries.shape, jnp.float32),
        compiler_params=pltpu.CompilerParams(vmem_limit_bytes=24 << 20),
        name="join_carries",
    )(carries, ratio)


def y_inverse(modes, carries, own, ratio, gain, count, parity):
    pairs, y_cells, piece = modes.shape
    y_local = y_cells // count
    table, _ = cosine_sine_basis(y_cells, y_cells, range(y_cells // 2 + 1))
    tables = halves(table)

    def kernel(own_ref, modes_ref, carry_ref, high_ref, low_ref, ratio_ref, gain_ref, *rest):
        out_refs, (behind, state, cells, sems) = rest[:count], rest[count:]

        def carry(kind):
            return carry_ref[:, kind].reshape(y_cells, piece)

        def stored(k, size):
            part = pl.ds(k, size)
            return [
                pltpu.make_async_copy(
                    cells.at[own_ref[0] ^ n, part], out_refs[n].at[part], sems.at[k, n]
                )
                for n in range(count)
            ]

        def emit(planes, k):
            size = len(planes)
            gain_value = gain_ref[...]
            joined = jnp.concatenate([gain_value * plane for plane in planes], 1)
            result = triple_product((high_ref[...], low_ref[...]), split(joined))
            for n in range(count):
                for side in range(size):
                    cells[n, k + side] = result[
                        n * y_local : (n + 1) * y_local, side * piece : (side + 1) * piece
                    ]
            for copy in stored(k, size):
                copy.start()

        r = ratio_ref[...]
        state[0] = carry(0)
        state[1] = carry(1)

        def back(i, done):
            m = pairs - 1 - i
            value = state[1]
            behind[m] = ratio_ref[...] * value
            state[1] = modes_ref[m] + ratio_ref[...] * value
            return done

        lax.fori_loop(0, pairs, back, 0)
        if parity:
            emit([state[0] + r * state[1]], 0)

        def body(t, done):
            r = ratio_ref[...]
            one = modes_ref[2 * t] + r * state[0]
            two = modes_ref[2 * t + 1] + r * one
            state[0] = two
            emit([one + behind[2 * t], two + behind[2 * t + 1]], 2 * t + parity)
            return done

        lax.fori_loop(0, pairs // 2, body, 0)
        if not parity:
            emit([r * state[0] + carry(1)], pairs)
        for copy in stored(0 if parity else pairs, 1):
            copy.wait()

        def finish(t, done):
            for copy in stored(2 * t + parity, 2):
                copy.wait()

            return done

        lax.fori_loop(0, pairs // 2, finish, 0)

    made = (count, pairs + 1, y_local, piece)
    return pl.pallas_call(
        kernel,
        in_specs=[in_smem] + [in_vmem] * 6,
        out_specs=[anywhere] * count,
        out_shape=[jax.ShapeDtypeStruct(made[1:], jnp.float32)] * count,
        scratch_shapes=[
            pltpu.VMEM((pairs, y_cells, piece), jnp.float32),
            pltpu.VMEM((2, y_cells, piece), jnp.float32),
            pltpu.VMEM(made, jnp.float32),
            pltpu.SemaphoreType.DMA((pairs + 1, count)),
        ],
        compiler_params=pltpu.CompilerParams(vmem_limit_bytes=vmem_limit),
        name="y_inverse",
    )(own, modes, carries, *tables, ratio, gain)


def turn(value, axis):
    return lax.all_to_all(value, axis, split_axis=0, concat_axis=0, tiled=True)


def solve_tables(count, y_local, piece):
    y_cells, z_cells = count * y_local, count * piece
    wide_count = lax.axis_size("wide")
    _, eigen_y = cosine_sine_basis(y_cells, y_cells, range(y_cells // 2 + 1))
    eigen_z = jnp.asarray(z_tables(z_cells)[2], jnp.float32)
    own_z = lax.dynamic_slice_in_dim(eigen_z, lax.axis_index("narrow") * piece, piece)
    excess = 4.0 * (jnp.asarray(eigen_y, jnp.float32)[:, None] + own_z[None, :] + penalty)
    root = jnp.sqrt(excess * (4.0 + excess))
    ratio = 2.0 / (2.0 + excess + root)
    share = y_cells // wide_count
    own_ratio = lax.dynamic_slice_in_dim(ratio, lax.axis_index("wide") * share, share)
    return ratio, -4.0 / root, own_ratio


def swap(blocks, axis):
    size = len(blocks)
    return [blocks[0]] + [
        lax.ppermute(blocks[k], axis, [(i, i ^ k) for i in range(size)]) for k in range(1, size)
    ]


def project(spectra, own, tables):
    count, pairs = len(spectra[0]), spectra[0][0].shape[0]
    ratio, gain, own_ratio = tables
    turned = []
    for spectrum in spectra:
        turned.append(swap(spectrum, "narrow"))
    solved = [y_forward(spectrum, own, ratio, lax.axis_size("wide")) for spectrum in turned]
    carries = [turn(carry, "wide") for _, carry in solved]
    joined = [turn(join_carries(carry, own_ratio, pairs), "wide") for carry in carries]
    return [
        swap(y_inverse(solved[p][0], joined[p], own, ratio, gain, count, p), "narrow")
        for p in range(2)
    ]


def conduct(profile, spread):
    sides = (("wide", 0), ("narrow", 1))
    spread = with_halo(spread, sides, STEPS - 1, False)
    profile = with_halo(profile, sides, STEPS, False)
    for _ in range(STEPS):
        center = profile[1:-1, 1:-1]
        near = (
            profile[2:, 1:-1] + profile[:-2, 1:-1] + profile[1:-1, 2:] + profile[1:-1, :-2]
        )
        ahead = jnp.pad(center[:, :, 1:], ((0, 0), (0, 0), (0, 1)))
        behind = jnp.pad(center[:, :, :-1], ((0, 0), (0, 0), (1, 0)))
        profile = center + spread * (near + ahead + behind - 6.0 * center)
        spread = spread[1:-1, 1:-1]
    return profile


def device_step(
    material_flow_vector,
    tool_push_density,
    tool_warmth_excess,
    substrate_warmth_excess,
    spread_coefficient,
    source_owner_sheet,
    source_part_line,
):
    flow = material_flow_vector
    flow_x, flow_y = ring(flow, "wide", 1), ring(flow, "narrow", 2)
    current, current_x, current_y = flow, flow_x, flow_y
    for section in range(PASSES):
        last = section + 1 == PASSES
        inner = viscosity_call(current, current_y, tool_warmth_excess, last)
        fields = viscosity_call(current, current_y, tool_warmth_excess, last, current_x, inner)
        mu = fields[0]
        mu_x, mu_y = ring(mu, "wide", 0), ring(mu, "narrow", 1)
        inner = advance_call(flow, flow_y, mu, mu_y, tool_push_density)
        current = advance_call(flow, flow_y, mu, mu_y, tool_push_density, flow_x, mu_x, inner)
        if not last:
            current_x, current_y = ring(current, "wide", 1), ring(current, "narrow", 2)
    _, x_local, y_local, z_cells = flow.shape
    count = lax.axis_size("narrow")
    pairs, piece = x_local // 2, z_cells // count
    tables = solve_tables(count, y_local, piece)
    end_x = ring(current[0], "wide", 0)
    lowest, highest = current[1, :, :1], current[1, :, y_local - 1 :]
    end_y = [
        side.reshape(pairs, 2, z_cells)
        for side in (shift(highest, "narrow", 1), shift(lowest, "narrow", -1))
    ]
    own = lax.axis_index("narrow").astype(jnp.int32).reshape(1)
    modes = divergence_modes(current, own, count)
    modes = [
        add_halo_modes(modes[p], own, end_x[p], [side[:, p] for side in end_y], p)
        for p in range(2)
    ]
    heat_cells, kept = lax.optimization_barrier((fields[1], (modes[0][0], modes[1][0])))
    modes = [[kept[p], *modes[p][1:]] for p in range(2)]
    spectra = project(modes, own, tables)
    sides = []
    for p in range(2):
        for row, by in ((y_local - 1, 1), (0, -1)):
            lines = jnp.stack([block[p : p + pairs, row] for block in spectra[p]])
            sides.append(shift(lines, "narrow", by))
    z_blocks = heat_cells.shape[0]
    slab_count = lax.axis_size("wide")
    component_lines = substrate_warmth_excess.shape[0] * substrate_warmth_excess.shape[1]
    targets = source_owner_sheet[:, 0] * component_lines + source_part_line
    partial_value = (
        jnp.zeros((slab_count * component_lines, 128), jnp.float32)
        .at[targets.reshape(-1, z_blocks).T.reshape(-1)]
        .add(heat_cells.reshape(-1, 128))
    )
    substrate_energy_input = lax.psum_scatter(
        partial_value.reshape(slab_count, component_lines, 128),
        "wide",
        scatter_dimension=0,
        tiled=True,
    )
    thermal_profile = substrate_warmth_excess + dissipation_factor * substrate_energy_input.reshape(
        substrate_warmth_excess.shape
    )
    part_out = conduct(thermal_profile, spread_coefficient)
    part_out, sides = lax.optimization_barrier((part_out, jnp.stack(sides)))
    corrected_flow_vector = corrected(
        current, pressure_planes(spectra[0], own), spectra[1], own, sides
    )
    return (corrected_flow_vector, part_out)


def solution(mesh):
    return jax.shard_map(
        device_step,
        mesh=mesh,
        in_specs=(
            P(None, "wide", "narrow", None),
            P(None, "wide", "narrow", None),
            P("wide", "narrow", None),
            P("wide", "narrow", None),
            P("wide", "narrow", None),
            P(("wide", "narrow"), None),
            P(("wide", "narrow")),
        ),
        out_specs=(P(None, "wide", "narrow", None), P("wide", "narrow", None)),
        check_vma=False,
    )
```

```python
import math

import jax
import jax.numpy as jnp
import numpy as np
from jax import lax
from jax.experimental import pallas as pl
from jax.experimental.pallas import tpu as pltpu
from jax.sharding import PartitionSpec as P

PASSES = 2
STEPS = 3


time_step = 0.15
rate_base = 0.5
zener_energy = 4.0
stress_exponent = 5.0
penalty = 0.001
dissipation_factor = 0.1


def with_halo(x, sides, width, wrap):
    for axis, dim in sides:
        size, length = (lax.axis_size(axis), x.shape[dim])
        up = [(i, (i + 1) % size) for i in range(size if wrap else size - 1)]
        down = [(j, i) for i, j in up]
        last = lax.slice_in_dim(x, length - width, length, axis=dim)
        initial = lax.slice_in_dim(x, 0, width, axis=dim)
        before = lax.ppermute(last, axis, up)
        after = lax.ppermute(initial, axis, down)
        x = jnp.concatenate([before, x, after], axis=dim)
    return x


def shift(value, axis, by):
    size = lax.axis_size(axis)
    return lax.ppermute(value, axis, [(i, (i + by) % size) for i in range(size)])


def ring(value, axis, dim):
    length = value.shape[dim]
    last = lax.slice_in_dim(value, length - 1, length, axis=dim)
    initial = lax.slice_in_dim(value, 0, 1, axis=dim)
    return shift(last, axis, 1), shift(initial, axis, -1)


anywhere = pl.BlockSpec(memory_space=pl.ANY)
in_vmem = pl.BlockSpec(memory_space=pltpu.VMEM)
scaled_mu = 0.5 * time_step


def row_numbers(width):
    return lax.broadcasted_iota(jnp.int32, (8, width), 0)


def rows_of(strip):
    return pl.ds(8 * strip, 8)


def pick(ref, index):
    return ref.at[:, index] if len(ref.shape) == 4 else ref.at[index]


class Planes:
    def __init__(self, source, target, semaphores, listed=None):
        self.source, self.target, self.semaphores = source, target, semaphores
        self.listed = listed

    def copy(self, slot, ref, plane):
        return pltpu.make_async_copy(
            pick(ref, plane), pick(self.target, slot), self.semaphores.at[slot]
        )

    def start(self, slot, plane=None):
        if self.listed is None:
            self.copy(slot, self.source, slot if plane is None else plane).start()
        else:
            self.copy(slot, *self.listed[slot]).start()

    def wait(self, slot):
        self.copy(slot, self.source, 0).wait()


def in_sections(x_local, size, loads, stores, start_up, body):
    count = x_local // size

    def cut(ref, first, planes):
        part = pl.ds(first, planes)
        return ref.at[:, part] if len(ref.shape) == 4 else ref.at[part]

    def moves(kinds, section, first, planes):
        return [
            pltpu.make_async_copy(
                cut(source, first, planes), cut(target, first, planes), semaphores.at[section]
            )
            for source, target, semaphores in kinds
        ]

    def begin(section, state):
        for move in moves(loads, section, section * size, size):
            move.start()
        return state

    lax.fori_loop(0, count, begin, 0)

    def work(section, first, planes):
        for move in moves(loads, section, section * size, size):
            move.wait()
        if isinstance(first, int):
            start_up()
        lax.fori_loop(first, first + planes, body, 0)
        for move in moves(stores, section, first, planes):
            move.start()

    work(0, 1, size - 2)

    def rest(section, state):
        work(section, section * size - 1, size)
        return state

    lax.fori_loop(1, count, rest, 0)
    for move in moves(stores, 0, 1, size - 2):
        move.wait()

    def finish(section, state):
        for move in moves(stores, section, section * size - 1, size):
            move.wait()
        return state

    lax.fori_loop(1, count, finish, 0)


def edge_list(ref, low, high, x_local):
    return [(low, 0), (ref, 0), (ref, 1), (ref, x_local - 2), (ref, x_local - 1), (high, 0)]


def viscosity_plane(cells, slot, edges, warmth, warm_slot, outs, out_slot, y_local, z_cells):
    strips, rows = y_local // 8, row_numbers(z_cells)
    before, after = edges
    values = [[cells[c, slot, rows_of(s), :] for s in range(strips)] for c in range(3)]
    up = [[pltpu.roll(v, 7, 0) for v in row] for row in values]
    down = [[pltpu.roll(v, 1, 0) for v in row] for row in values]
    for s in range(strips):
        along_x, along_y, along_z = [], [], []
        for c in range(3):
            value = values[c][s]
            along_x.append(cells[c, slot + 1, rows_of(s), :] - cells[c, slot - 1, rows_of(s), :])
            ahead = jnp.where(rows == 7, up[c][s + 1] if s + 1 < strips else after(c), up[c][s])
            behind = jnp.where(rows == 0, down[c][s - 1] if s else before(c), down[c][s])
            along_y.append(ahead - behind)
            along_z.append(pltpu.roll(value, z_cells - 1, 1) - pltpu.roll(value, 1, 1))
        s_xy = along_y[0] + along_x[1]
        s_xz = along_z[0] + along_x[2]
        s_yz = along_z[1] + along_y[2]
        extra = 0.5 * (
            along_x[0] * along_x[0] + along_y[1] * along_y[1] + along_z[2] * along_z[2]
        ) + 0.25 * (s_xy * s_xy + s_xz * s_xz + s_yz * s_yz)
        rate_sq = rate_base**2 + extra
        value = jnp.exp(
            (0.5 / stress_exponent) * jnp.log(rate_sq)
            + (zener_energy / stress_exponent) * (1.0 / warmth[warm_slot, rows_of(s), :] - 1.0)
        )
        square = value * value + 1.0
        mu = jnp.log(value + square * lax.rsqrt(square)) * lax.rsqrt(rate_sq)
        outs[0][out_slot, rows_of(s), :] = mu * (scaled_mu / 3.0)
        if len(outs) > 1:
            heat = (mu * (1.0 / 3.0)) * extra
            for b in range(z_cells // 128):
                outs[1][b, out_slot, rows_of(s), :] = heat[:, b * 128 : (b + 1) * 128]


def viscosity_call(flow, y_sides, warmth, with_heat, x_sides=None, inner=None):
    _, x_local, y_local, z_cells = flow.shape
    z_blocks = z_cells // 128
    edge = x_sides is not None
    slots, made = (6, 2) if edge else (x_local, x_local - 2)
    outputs = 2 if with_heat else 1

    def kernel(*refs):
        flow_ref, before_ref, after_ref, warmth_ref = refs[:4]
        rest = list(refs[4:])
        listed = None
        if edge:
            low, high = rest[:2]
            listed = edge_list(flow_ref, low, high, x_local)
            rest = rest[2 + outputs :]
        out_refs, rest = rest[:outputs], rest[outputs:]
        cells, cell_sem, warm, warm_sem = rest[:4]
        outs, out_sems = rest[4 : 4 + outputs], rest[4 + outputs :]
        flow_planes = Planes(flow_ref, cells, cell_sem, listed)
        warm_planes = Planes(warmth_ref, warm, warm_sem)

        def plane_of(i):
            return i * (x_local - 1) if edge else i + 1

        def slot_of(i):
            return 3 * i + 1 if edge else i + 1

        def stored(k, i):
            return pltpu.make_async_copy(
                pick(outs[k], i), pick(out_refs[k], plane_of(i)), out_sems[k].at[i]
            )

        if edge:
            for slot in range(6):
                flow_planes.start(slot)
            for i in range(2):
                warm_planes.start(i, plane_of(i))
        else:
            flow_planes.start(0)
            flow_planes.start(1)

            def begin(i, state):
                flow_planes.start(i + 2)
                warm_planes.start(i, i + 1)
                return state

            lax.fori_loop(0, made, begin, 0)
            flow_planes.wait(0)
            flow_planes.wait(1)

        def body(i, state):
            slot, plane = slot_of(i), plane_of(i)
            if edge:
                flow_planes.wait(slot - 1)
                flow_planes.wait(slot)
            flow_planes.wait(slot + 1)
            warm_planes.wait(i)
            viscosity_plane(
                cells,
                slot,
                (lambda c: before_ref[c, plane], lambda c: after_ref[c, plane]),
                warm,
                i,
                outs,
                i,
                y_local,
                z_cells,
            )
            for k in range(outputs):
                stored(k, i).start()
            return state

        lax.fori_loop(0, made, body, 0)

        def finish(i, state):
            for k in range(outputs):
                stored(k, i).wait()
            return state

        lax.fori_loop(0, made, finish, 0)

    shapes = [(x_local, y_local, z_cells), (z_blocks, x_local, y_local, 128)][:outputs]
    held = [(made, y_local, z_cells), (z_blocks, made, y_local, 128)][:outputs]
    operands = [flow, *y_sides, warmth]
    specs = [anywhere, in_vmem, in_vmem, anywhere]
    aliases = {}
    if edge:
        operands += [*x_sides, *inner]
        specs += [anywhere] * (2 + outputs)
        aliases = {6 + k: k for k in range(outputs)}
    return pl.pallas_call(
        kernel,
        in_specs=specs,
        out_specs=[anywhere] * outputs,
        out_shape=[jax.ShapeDtypeStruct(shape, jnp.float32) for shape in shapes],
        input_output_aliases=aliases,
        scratch_shapes=[
            pltpu.VMEM((3, slots, y_local, z_cells), jnp.float32),
            pltpu.SemaphoreType.DMA((slots,)),
            pltpu.VMEM((made, y_local, z_cells), jnp.float32),
            pltpu.SemaphoreType.DMA((made,)),
        ]
        + [pltpu.VMEM(shape, jnp.float32) for shape in held]
        + [pltpu.SemaphoreType.DMA((made,))] * outputs,
        compiler_params=pltpu.CompilerParams(vmem_limit_bytes=vmem_limit),
        name="viscosity_edge" if edge else "viscosity_inner",
    )(*operands)


def viscosity_inner(flow, y_sides, warmth, with_heat):
    _, x_local, y_local, z_cells = flow.shape
    z_blocks, size = z_cells // 128, 4
    outputs = 2 if with_heat else 1

    def kernel(flow_ref, before_ref, after_ref, warmth_ref, *rest):
        out_refs, (cells, cell_sem, warm, warm_sem, *heat) = rest[:outputs], rest[outputs:]
        outs = [out_refs[0]] + heat[:1]

        def body(slot, state):
            viscosity_plane(
                cells,
                slot,
                (lambda c: before_ref[c, slot], lambda c: after_ref[c, slot]),
                warm,
                slot,
                outs,
                slot,
                y_local,
                z_cells,
            )
            return state

        in_sections(
            x_local,
            size,
            [(flow_ref, cells, cell_sem), (warmth_ref, warm, warm_sem)],
            [(heat[0], out_refs[1], heat[1])] if with_heat else [],
            lambda: None,
            body,
        )

    shapes = [(x_local, y_local, z_cells), (z_blocks, x_local, y_local, 128)][:outputs]
    sems = pltpu.SemaphoreType.DMA((x_local // size,))
    return pl.pallas_call(
        kernel,
        in_specs=[anywhere, in_vmem, in_vmem, anywhere],
        out_specs=[in_vmem, anywhere][:outputs],
        out_shape=[jax.ShapeDtypeStruct(shape, jnp.float32) for shape in shapes],
        scratch_shapes=[
            pltpu.VMEM(flow.shape, jnp.float32),
            sems,
            pltpu.VMEM(warmth.shape, jnp.float32),
            sems,
        ]
        + ([pltpu.VMEM(shapes[1], jnp.float32), sems] if with_heat else []),
        compiler_params=pltpu.CompilerParams(vmem_limit_bytes=vmem_limit),
        name="viscosity_inner",
    )(flow, *y_sides, warmth)


vmem_limit = 48 << 20


def advance_plane(cells, mu, slot, edges, push, out_slot, flux, y_local, z_cells):
    strips, rows = y_local // 8, row_numbers(z_cells)
    flow_before, flow_after, mu_before, mu_after = edges
    m = [mu[slot, rows_of(s), :] for s in range(strips)]
    m_up = [pltpu.roll(v, 7, 0) for v in m]
    sums_y = [
        m[s] + jnp.where(rows == 7, m_up[s + 1] if s + 1 < strips else mu_after(), m_up[s])
        for s in range(strips)
    ]
    first_sum = mu_before() + mu[slot, pl.ds(0, 1), :]
    values = [[cells[c, slot, rows_of(s), :] for s in range(strips)] for c in range(3)]
    up = [[pltpu.roll(v, 7, 0) for v in row] for row in values]
    carried = [
        first_sum * (cells[c, slot, pl.ds(0, 1), :] - flow_before(c)) for c in range(3)
    ]
    for s in range(strips):
        sum_x = m[s] + mu[slot + 1, rows_of(s), :]
        sum_z_ahead = m[s] + pltpu.roll(m[s], z_cells - 1, 1)
        sum_z_behind = m[s] + pltpu.roll(m[s], 1, 1)
        for c in range(3):
            value = values[c][s]
            flux_x = sum_x * (cells[c, slot + 1, rows_of(s), :] - value)
            ahead = jnp.where(
                rows == 7, up[c][s + 1] if s + 1 < strips else flow_after(c), up[c][s]
            )
            flux_y = sums_y[s] * (ahead - value)
            turned = pltpu.roll(flux_y, 1, 0)
            total = (flux_x - flux[c, rows_of(s), :]) + (
                flux_y - jnp.where(rows == 0, carried[c], turned)
            ) + (
                sum_z_ahead * (pltpu.roll(value, z_cells - 1, 1) - value)
                - sum_z_behind * (value - pltpu.roll(value, 1, 1))
            )
            flux[c, rows_of(s), :] = flux_x
            carried[c] = turned
            push[c, out_slot, rows_of(s), :] = (
                value + time_step * push[c, out_slot, rows_of(s), :] + total
            )


def first_flux(cells, mu, slot, flux, y_local):
    for s in range(y_local // 8):
        sum_x = mu[slot - 1, rows_of(s), :] + mu[slot, rows_of(s), :]
        for c in range(3):
            flux[c, rows_of(s), :] = sum_x * (
                cells[c, slot, rows_of(s), :] - cells[c, slot - 1, rows_of(s), :]
            )


def advance_call(flow, flow_y, mu, mu_y, push, flow_x=None, mu_x=None, inner=None):
    _, x_local, y_local, z_cells = flow.shape
    edge = flow_x is not None
    slots, made = (6, 2) if edge else (x_local, x_local - 2)

    def kernel(*refs):
        flow_ref, flow_before, flow_after, mu_ref, mu_before, mu_after, push_ref = refs[:7]
        rest = refs[7:]
        flow_listed = mu_listed = None
        if edge:
            flow_listed = edge_list(flow_ref, rest[0], rest[1], x_local)
            mu_listed = edge_list(mu_ref, rest[2], rest[3], x_local)
            rest = rest[5:]
        out_ref, cells, cell_sem, mu_cells, mu_sem, work, work_sem, out_sem, flux = rest
        flow_planes = Planes(flow_ref, cells, cell_sem, flow_listed)
        mu_planes = Planes(mu_ref, mu_cells, mu_sem, mu_listed)
        push_planes = Planes(push_ref, work, work_sem)

        def plane_of(i):
            return i * (x_local - 1) if edge else i + 1

        def stored(i):
            return pltpu.make_async_copy(
                pick(work, i), pick(out_ref, plane_of(i)), out_sem.at[i]
            )

        if edge:
            for slot in range(6):
                flow_planes.start(slot)
                mu_planes.start(slot)
            for i in range(2):
                push_planes.start(i, plane_of(i))
        else:
            for slot in range(2):
                flow_planes.start(slot)
                mu_planes.start(slot)

            def begin(i, state):
                flow_planes.start(i + 2)
                mu_planes.start(i + 2)
                push_planes.start(i, i + 1)
                return state

            lax.fori_loop(0, made, begin, 0)
            for slot in range(2):
                flow_planes.wait(slot)
                mu_planes.wait(slot)
            first_flux(cells, mu_cells, 1, flux, y_local)

        def body(i, state):
            slot, plane = (3 * i + 1 if edge else i + 1), plane_of(i)
            if edge:
                for back in range(2):
                    flow_planes.wait(slot - back)
                    mu_planes.wait(slot - back)
                first_flux(cells, mu_cells, slot, flux, y_local)
            flow_planes.wait(slot + 1)
            mu_planes.wait(slot + 1)
            push_planes.wait(i)
            advance_plane(
                cells,
                mu_cells,
                slot,
                (
                    lambda c: flow_before[c, plane],
                    lambda c: flow_after[c, plane],
                    lambda: mu_before[plane],
                    lambda: mu_after[plane],
                ),
                work,
                i,
                flux,
                y_local,
                z_cells,
            )
            stored(i).start()
            return state

        lax.fori_loop(0, made, body, 0)

        def finish(i, state):
            stored(i).wait()
            return state

        lax.fori_loop(0, made, finish, 0)

    operands = [flow, *flow_y, mu, *mu_y, push]
    specs = [anywhere, in_vmem, in_vmem, anywhere, in_vmem, in_vmem, anywhere]
    aliases = {}
    if edge:
        operands += [*flow_x, *mu_x, inner]
        specs += [anywhere] * 5
        aliases = {11: 0}
    return pl.pallas_call(
        kernel,
        in_specs=specs,
        out_specs=anywhere,
        out_shape=jax.ShapeDtypeStruct(flow.shape, jnp.float32),
        input_output_aliases=aliases,
        scratch_shapes=[
            pltpu.VMEM((3, slots, y_local, z_cells), jnp.float32),
            pltpu.SemaphoreType.DMA((slots,)),
            pltpu.VMEM((slots, y_local, z_cells), jnp.float32),
            pltpu.SemaphoreType.DMA((slots,)),
            pltpu.VMEM((3, made, y_local, z_cells), jnp.float32),
            pltpu.SemaphoreType.DMA((made,)),
            pltpu.SemaphoreType.DMA((made,)),
            pltpu.VMEM((3, y_local, z_cells), jnp.float32),
        ],
        compiler_params=pltpu.CompilerParams(vmem_limit_bytes=vmem_limit),
        name="advance_edge" if edge else "advance_inner",
    )(*operands)


def advance_inner(flow, flow_y, mu, mu_y, push):
    _, x_local, y_local, z_cells = flow.shape
    size = 4

    def kernel(
        flow_ref, flow_before, flow_after, mu_ref, mu_before, mu_after, push_ref,
        out_ref, cells, cell_sem, work, work_sem, out_sem, flux,
    ):
        def body(slot, state):
            advance_plane(
                cells,
                mu_ref,
                slot,
                (
                    lambda c: flow_before[c, slot],
                    lambda c: flow_after[c, slot],
                    lambda: mu_before[slot],
                    lambda: mu_after[slot],
                ),
                work,
                slot,
                flux,
                y_local,
                z_cells,
            )
            return state

        in_sections(
            x_local,
            size,
            [(flow_ref, cells, cell_sem), (push_ref, work, work_sem)],
            [(work, out_ref, out_sem)],
            lambda: first_flux(cells, mu_ref, 1, flux, y_local),
            body,
        )

    sems = pltpu.SemaphoreType.DMA((x_local // size,))
    return pl.pallas_call(
        kernel,
        in_specs=[anywhere, in_vmem, in_vmem, in_vmem, in_vmem, in_vmem, anywhere],
        out_specs=anywhere,
        out_shape=jax.ShapeDtypeStruct(flow.shape, jnp.float32),
        scratch_shapes=[
            pltpu.VMEM(flow.shape, jnp.float32),
            sems,
            pltpu.VMEM(flow.shape, jnp.float32),
            sems,
            sems,
            pltpu.VMEM((3, y_local, z_cells), jnp.float32),
        ],
        compiler_params=pltpu.CompilerParams(vmem_limit_bytes=vmem_limit),
        name="advance_inner",
    )(flow, *flow_y, mu, *mu_y, push)


def cosine_sine_basis(points, period, waves):
    columns, eigen = [], []
    for wave in waves:
        angle = 2.0 * np.pi * ((wave * np.arange(points)) % period) / period
        single = wave % period == 0 or 2 * wave == period
        size = math.sqrt((1.0 if single else 2.0) / period)
        columns.append(np.cos(angle) * size)
        eigen.append(math.sin(2.0 * math.pi * wave / period) ** 2)
        if not single:
            columns.append(np.sin(angle) * size)
            eigen.append(eigen[-1])
    return np.stack(columns, 1), np.array(eigen)


def halves(table):
    table = np.asarray(table, np.float32)
    high = table.astype(jnp.bfloat16)
    low = (table - high.astype(np.float32)).astype(jnp.bfloat16)
    return jnp.asarray(high), jnp.asarray(low)


def split(value):
    high = value.astype(jnp.bfloat16)
    return high, (value - high.astype(jnp.float32)).astype(jnp.bfloat16)


def triple_product(left, right):
    def product(one, two):
        return lax.dot_general(
            one, two, (((1,), (0,)), ((), ())), preferred_element_type=jnp.float32
        )

    return product(left[0], right[0]) + (product(left[0], right[1]) + product(left[1], right[0]))


def z_tables(z_cells):
    half = z_cells // 2
    even, eigen_even = cosine_sine_basis(half, z_cells, range(0, half + 1, 2))
    odd, eigen_odd = cosine_sine_basis(half, z_cells, range(1, half, 2))
    return even, odd, np.concatenate([eigen_even, eigen_odd])


def whole(*shape):
    return pl.BlockSpec(shape, lambda *index: (0,) * len(shape))


def modes_of(lines, even_high, even_low, odd_high, odd_low):
    half = lines.shape[1] // 2
    first, second = lines[:, :half], lines[:, half:]
    return jnp.concatenate(
        [
            triple_product(split(first + second), (even_high[...], even_low[...])),
            triple_product(split(first - second), (odd_high[...], odd_low[...])),
        ],
        1,
    )


def cells_of(modes, even_high, even_low, odd_high, odd_low):
    half = modes.shape[1] // 2
    first = triple_product(split(modes[:, :half]), (even_high[...], even_low[...]))
    second = triple_product(split(modes[:, half:]), (odd_high[...], odd_low[...]))
    return jnp.concatenate([first + second, first - second], 1)


def divergence_modes(flow, count):
    _, x_local, y_local, z_cells = flow.shape
    half, piece, strips = z_cells // 2, z_cells // count, y_local // 8
    step = min(8, x_local)
    even, odd, _ = z_tables(z_cells)
    tables = halves(even) + halves(odd)

    def kernel(
        flow_ref, even_high, even_low, odd_high, odd_low, out_ref,
        cells, semaphores, work, made, out_sem,
    ):
        planes = Planes(flow_ref, cells, semaphores)
        rows = row_numbers(z_cells)

        def begin(i, state):
            planes.start(i)
            return state

        lax.fori_loop(0, x_local, begin, 0)
        planes.wait(0)

        def stored(k):
            part = pl.ds(k * step, step)
            return pltpu.make_async_copy(made.at[:, part], out_ref.at[:, part], out_sem.at[k])

        def group(k, state):
            def plane(i, state):
                j = k * step + i

                @pl.when(j + 1 < x_local)
                def _():
                    planes.wait(j + 1)

                nearer = jnp.where(j > 0, 0.5, 0.0)
                further = jnp.where(j + 1 < x_local, 0.5, 0.0)
                last, following = jnp.maximum(j - 1, 0), jnp.minimum(j + 1, x_local - 1)
                across = [cells[1, j, rows_of(s), :] for s in range(strips)]
                up = [pltpu.roll(v, 7, 0) for v in across]
                down = [pltpu.roll(v, 1, 0) for v in across]
                for s in range(strips):
                    ahead = jnp.where(rows == 7, up[s + 1] if s + 1 < strips else 0.0, up[s])
                    behind = jnp.where(rows == 0, down[s - 1] if s else 0.0, down[s])
                    along = cells[2, j, rows_of(s), :]
                    work[i, rows_of(s), :] = (
                        further * cells[0, following, rows_of(s), :]
                        - nearer * cells[0, last, rows_of(s), :]
                    ) + 0.5 * (
                        (ahead - behind)
                        + (pltpu.roll(along, z_cells - 1, 1) - pltpu.roll(along, 1, 1))
                    )
                return state

            lax.fori_loop(0, step, plane, 0)
            modes = modes_of(
                work[...].reshape(step * y_local, z_cells), even_high, even_low, odd_high, odd_low
            )
            for n in range(count):
                made[n, pl.ds(k * step, step)] = modes[:, n * piece : (n + 1) * piece].reshape(
                    step, y_local, piece
                )
            stored(k).start()
            return state

        groups = x_local // step
        lax.fori_loop(0, groups, group, 0)
        for k in range(groups):
            stored(k).wait()

    return pl.pallas_call(
        kernel,
        in_specs=[anywhere] + [in_vmem] * 4,
        out_specs=anywhere,
        out_shape=jax.ShapeDtypeStruct((count, x_local, y_local, piece), jnp.float32),
        scratch_shapes=[
            pltpu.VMEM((3, x_local, y_local, z_cells), jnp.float32),
            pltpu.SemaphoreType.DMA((x_local,)),
            pltpu.VMEM((step, y_local, z_cells), jnp.float32),
            pltpu.VMEM((count, x_local, y_local, piece), jnp.float32),
            pltpu.SemaphoreType.DMA((x_local // step,)),
        ],
        name="divergence_modes",
    )(flow, *tables)


def add_halo_modes(modes, x_sides, y_sides):
    count, x_local, y_local, piece = modes.shape
    z_cells = count * piece
    even, odd, _ = z_tables(z_cells)
    tables = halves(even) + halves(odd)

    def kernel(
        modes_ref, low_ref, high_ref, before_ref, after_ref,
        even_high, even_low, odd_high, odd_low, out_ref, ends, lines, semaphores,
    ):
        def moves(back):
            pairs = [
                (ends.at[k], modes_ref.at[:, plane])
                for k, plane in enumerate((0, x_local - 1))
            ] + [
                (lines.at[k], modes_ref.at[:, 1 : x_local - 1, 8 * s : 8 * s + 8])
                for k, s in enumerate((0, y_local // 8 - 1))
            ]
            if back:
                pairs = [
                    (ends.at[k], out_ref.at[:, plane])
                    for k, plane in enumerate((0, x_local - 1))
                ] + [
                    (lines.at[k], out_ref.at[:, 1 : x_local - 1, 8 * s : 8 * s + 8])
                    for k, s in enumerate((0, y_local // 8 - 1))
                ]
                return [
                    pltpu.make_async_copy(here, there, semaphores.at[4 + i])
                    for i, (here, there) in enumerate(pairs)
                ]
            return [
                pltpu.make_async_copy(there, here, semaphores.at[i])
                for i, (here, there) in enumerate(pairs)
            ]

        loads, stores = moves(False), moves(True)
        for load in loads:
            load.start()
        added = modes_of(
            jnp.concatenate(
                [-0.5 * low_ref[0], 0.5 * high_ref[0], -0.5 * before_ref[...], 0.5 * after_ref[...]],
                0,
            ),
            even_high,
            even_low,
            odd_high,
            odd_low,
        )
        for load in loads:
            load.wait()
        rows = row_numbers(piece)
        for n in range(count):
            block = added[:, n * piece : (n + 1) * piece]
            side = [block[2 * y_local + k * x_local :][:x_local] for k in range(2)]
            for k, plane in enumerate((0, x_local - 1)):
                ends[k, n] = ends[k, n] + block[k * y_local : (k + 1) * y_local]
                for j, (strip, row) in enumerate(((0, 0), (y_local // 8 - 1, 7))):
                    part = pl.ds(8 * strip, 8)
                    ends[k, n, part, :] = ends[k, n, part, :] + jnp.where(
                        rows == row, side[j][plane : plane + 1], 0.0
                    )
            for j, row in enumerate((0, 7)):
                for x in range(1, x_local - 1):
                    lines[j, n, x - 1] = lines[j, n, x - 1] + jnp.where(
                        rows == row, side[j][x : x + 1], 0.0
                    )
        for store in stores:
            store.start()
        for store in stores:
            store.wait()

    return pl.pallas_call(
        kernel,
        in_specs=[anywhere] + [in_vmem] * 8,
        out_specs=anywhere,
        out_shape=jax.ShapeDtypeStruct(modes.shape, jnp.float32),
        input_output_aliases={0: 0},
        scratch_shapes=[
            pltpu.VMEM((2, count, y_local, piece), jnp.float32),
            pltpu.VMEM((2, count, x_local - 2, 8, piece), jnp.float32),
            pltpu.SemaphoreType.DMA((8,)),
        ],
        name="add_halo_modes",
    )(modes, *x_sides, *y_sides, *tables)


def corrected(flow, spectrum, y_sides):
    count, planes, y_local, piece = spectrum.shape
    x_local, z_cells = planes - 2, count * piece
    strips, part = y_local // 8, planes // 2
    even, odd, _ = z_tables(z_cells)
    tables = halves(even.T) + halves(odd.T)

    def kernel(
        flow_ref, in_ref, before_ref, after_ref,
        even_high, even_low, odd_high, odd_low, out_ref,
        modes, mode_sem, pressure, sides, work, flow_sem, out_sem,
    ):
        flow_planes = Planes(flow_ref, work, flow_sem)
        table_refs = (even_high, even_low, odd_high, odd_low)

        def load(k):
            span = pl.ds(k * part, part)
            return pltpu.make_async_copy(in_ref.at[:, span], modes.at[:, span], mode_sem.at[k])

        load(0).start()
        load(1).start()

        def begin(i, state):
            flow_planes.start(i)
            return state

        lax.fori_loop(0, x_local, begin, 0)
        sides[...] = cells_of(
            jnp.concatenate(
                [
                    jnp.concatenate([ref[n] for n in range(count)], 1)
                    for ref in (before_ref, after_ref)
                ],
                0,
            ),
            *table_refs,
        )
        rows = row_numbers(z_cells)

        def stored(i):
            return pltpu.make_async_copy(pick(work, i), pick(out_ref, i), out_sem.at[i])

        def plane(j, state):
            flow_planes.wait(j)
            values = [pressure[j + 1, rows_of(s), :] for s in range(strips)]
            up = [pltpu.roll(v, 7, 0) for v in values]
            down = [pltpu.roll(v, 1, 0) for v in values]
            for s in range(strips):
                ahead = up[s + 1] if s + 1 < strips else sides[pl.ds(x_local + j, 1), :]
                behind = down[s - 1] if s else sides[pl.ds(j, 1), :]
                slopes = (
                    pressure[j + 2, rows_of(s), :] - pressure[j, rows_of(s), :],
                    jnp.where(rows == 7, ahead, up[s]) - jnp.where(rows == 0, behind, down[s]),
                    pltpu.roll(values[s], z_cells - 1, 1) - pltpu.roll(values[s], 1, 1),
                )
                for c in range(3):
                    work[c, j, rows_of(s), :] = work[c, j, rows_of(s), :] - 0.5 * slopes[c]
            stored(j).start()
            return state

        for k in range(2):
            load(k).wait()
            span = pl.ds(k * part, part)
            pressure[span] = cells_of(
                jnp.concatenate(
                    [modes[n, span].reshape(part * y_local, piece) for n in range(count)], 1
                ),
                *table_refs,
            ).reshape(part, y_local, z_cells)
            lax.fori_loop(k * (part - 2), (part - 2) if k == 0 else x_local, plane, 0)

        def finish(i, state):
            stored(i).wait()
            return state

        lax.fori_loop(0, x_local, finish, 0)

    return pl.pallas_call(
        kernel,
        in_specs=[anywhere, anywhere] + [in_vmem] * 6,
        out_specs=anywhere,
        out_shape=jax.ShapeDtypeStruct(flow.shape, jnp.float32),
        scratch_shapes=[
            pltpu.VMEM(spectrum.shape, jnp.float32),
            pltpu.SemaphoreType.DMA((2,)),
            pltpu.VMEM((planes, y_local, z_cells), jnp.float32),
            pltpu.VMEM((2 * x_local, z_cells), jnp.float32),
            pltpu.VMEM(flow.shape, jnp.float32),
            pltpu.SemaphoreType.DMA((x_local,)),
            pltpu.SemaphoreType.DMA((x_local,)),
        ],
        compiler_params=pltpu.CompilerParams(vmem_limit_bytes=vmem_limit),
        name="corrected",
    )(flow, spectrum, *y_sides, *tables)


def y_forward(spectrum, ratio, wide_count):
    count, x_local, y_local, piece = spectrum.shape
    y_cells, pairs = count * y_local, x_local // 2
    share, group = y_cells // wide_count, max(2, x_local // 4)
    table, _ = cosine_sine_basis(y_cells, y_cells, range(y_cells // 2 + 1))
    tables = halves(table.T)

    def kernel(
        in_ref, high_ref, low_ref, ratio_ref, modes_ref, carry_ref,
        lines, in_sems, made, out_sems, sums, power,
    ):
        def load(k):
            part = pl.ds(k * group, group)
            return pltpu.make_async_copy(in_ref.at[:, part], lines.at[:, part], in_sems.at[k])

        def stored(k):
            part = pl.ds(k * group, group)
            return pltpu.make_async_copy(made.at[part], modes_ref.at[part], out_sems.at[k])

        for k in range(x_local // group):
            load(k).start()
        sums[...] = jnp.zeros_like(sums)
        power[...] = jnp.ones_like(power)

        def body(t, state):
            planes = [
                jnp.concatenate([lines[n, 2 * t + side] for n in range(count)], 0)
                for side in range(2)
            ]
            modes = triple_product(
                (high_ref[...], low_ref[...]), split(jnp.concatenate(planes, 1))
            )
            r, pw = ratio_ref[...], power[...]
            for side in range(2):
                plane = modes[:, side * piece : (side + 1) * piece]
                made[2 * t + side] = plane
                sums[side] = plane + r * sums[side]
                sums[2 + side] = sums[2 + side] + pw * plane
            power[...] = pw * r
            return state

        def section(k, state):
            load(k).wait()
            lax.fori_loop(k * (group // 2), (k + 1) * (group // 2), body, 0)
            stored(k).start()
            return state

        lax.fori_loop(0, x_local // group, section, 0)
        for kind in range(4):
            carry_ref[:, kind] = sums[kind].reshape(wide_count, share, piece)
        for k in range(x_local // group):
            stored(k).wait()

    return pl.pallas_call(
        kernel,
        in_specs=[anywhere] + [in_vmem] * 3,
        out_specs=[anywhere, in_vmem],
        out_shape=[
            jax.ShapeDtypeStruct((x_local, y_cells, piece), jnp.float32),
            jax.ShapeDtypeStruct((wide_count, 4, share, piece), jnp.float32),
        ],
        scratch_shapes=[
            pltpu.VMEM(spectrum.shape, jnp.float32),
            pltpu.SemaphoreType.DMA((x_local // group,)),
            pltpu.VMEM((x_local, y_cells, piece), jnp.float32),
            pltpu.SemaphoreType.DMA((x_local // group,)),
            pltpu.VMEM((4, y_cells, piece), jnp.float32),
            pltpu.VMEM((y_cells, piece), jnp.float32),
        ],
        name="y_forward",
    )(spectrum, *tables, ratio)


def power_of(value, exponent):
    result = None
    while exponent:
        if exponent & 1:
            result = value if result is None else result * value
        value = value * value
        exponent >>= 1
    return result


def join_carries(carries, ratio, block):
    count, kinds, share, piece = carries.shape

    def kernel(in_ref, ratio_ref, out_ref):
        step = power_of(ratio_ref[...], block)
        scale = 1.0 / (1.0 - power_of(step, count))
        for kind in range(kinds):
            order = list(range(count)) if kind < 2 else list(range(count))[::-1]
            total = in_ref[order[0], kind]
            for w in order[1:]:
                total = in_ref[w, kind] + step * total
            total = total * scale
            for w in order:
                out_ref[w, kind] = total
                total = in_ref[w, kind] + step * total

    return pl.pallas_call(
        kernel,
        in_specs=[in_vmem] * 2,
        out_specs=in_vmem,
        out_shape=jax.ShapeDtypeStruct(carries.shape, jnp.float32),
        compiler_params=pltpu.CompilerParams(vmem_limit_bytes=vmem_limit),
        name="join_carries",
    )(carries, ratio)


def y_inverse(modes, carries, ratio, gain, count):
    x_local, y_cells, piece = modes.shape
    y_local, pairs, group = y_cells // count, x_local // 2, max(2, x_local // 4)
    table, _ = cosine_sine_basis(y_cells, y_cells, range(y_cells // 2 + 1))
    tables = halves(table)

    def kernel(
        modes_in, carry_ref, high_ref, low_ref, ratio_ref, gain_ref, out_ref,
        planes, in_sems, behind, state, cells, out_sems,
    ):
        def load(k):
            part = pl.ds(k * group, group)
            return pltpu.make_async_copy(modes_in.at[part], planes.at[part], in_sems.at[k])

        def stored(t):
            part = pl.ds(2 * t, 2)
            return pltpu.make_async_copy(cells.at[:, part], out_ref.at[:, part], out_sems.at[t])

        def carry(kind):
            return carry_ref[:, kind].reshape(y_cells, piece)

        groups = x_local // group
        for k in range(groups)[::-1]:
            load(k).start()
        for kind in range(4):
            state[kind] = carry(kind)
        behind[x_local + 1] = carry(2)

        def back(i, done):
            m = pairs - 1 - i
            r = ratio_ref[...]
            for side in range(2):
                value = r * state[2 + side]
                behind[2 * m + 1 + side] = value
                state[2 + side] = planes[2 * m + side] + value
            return done

        def back_section(k, done):
            load(groups - 1 - k).wait()
            lax.fori_loop(k * (group // 2), (k + 1) * (group // 2), back, 0)
            return done

        lax.fori_loop(0, groups, back_section, 0)
        behind[0] = ratio_ref[...] * state[3]

        def body(t, done):
            r, gain_value = ratio_ref[...], gain_ref[...]
            even_plane = planes[jnp.minimum(2 * t, x_local - 2)]
            odd_plane = planes[jnp.maximum(2 * t - 1, 1)]
            even = r * state[0] + jnp.where(t < pairs, even_plane, 0.0)
            odd = jnp.where(t > 0, odd_plane + r * state[1], state[1])
            state[0] = even
            state[1] = odd
            joined = jnp.concatenate(
                [gain_value * (odd + behind[2 * t]), gain_value * (even + behind[2 * t + 1])], 1
            )
            result = triple_product((high_ref[...], low_ref[...]), split(joined))
            for n in range(count):
                for side in range(2):
                    cells[n, 2 * t + side] = result[
                        n * y_local : (n + 1) * y_local, side * piece : (side + 1) * piece
                    ]
            stored(t).start()
            return done

        lax.fori_loop(0, pairs + 1, body, 0)

        def finish(t, done):
            stored(t).wait()
            return done

        lax.fori_loop(0, pairs + 1, finish, 0)

    made = (count, x_local + 2, y_local, piece)
    return pl.pallas_call(
        kernel,
        in_specs=[anywhere] + [in_vmem] * 5,
        out_specs=anywhere,
        out_shape=jax.ShapeDtypeStruct(made, jnp.float32),
        scratch_shapes=[
            pltpu.VMEM(modes.shape, jnp.float32),
            pltpu.SemaphoreType.DMA((x_local // group,)),
            pltpu.VMEM((x_local + 2, y_cells, piece), jnp.float32),
            pltpu.VMEM((4, y_cells, piece), jnp.float32),
            pltpu.VMEM(made, jnp.float32),
            pltpu.SemaphoreType.DMA((pairs + 1,)),
        ],
        name="y_inverse",
    )(modes, carries, *tables, ratio, gain)


def turn(value, axis):
    return lax.all_to_all(value, axis, split_axis=0, concat_axis=0, tiled=True)


def project(spectrum):
    count, x_local, y_local, piece = spectrum.shape
    y_cells, z_cells = count * y_local, count * piece
    wide_count = lax.axis_size("wide")
    _, eigen_y = cosine_sine_basis(y_cells, y_cells, range(y_cells // 2 + 1))
    eigen_z = jnp.asarray(z_tables(z_cells)[2], jnp.float32)
    own_z = lax.dynamic_slice_in_dim(eigen_z, lax.axis_index("narrow") * piece, piece)
    excess = 4.0 * (jnp.asarray(eigen_y, jnp.float32)[:, None] + own_z[None, :] + penalty)
    root = jnp.sqrt(excess * (4.0 + excess))
    ratio = 2.0 / (2.0 + excess + root)
    gain = -4.0 / root
    share = y_cells // wide_count
    own_ratio = lax.dynamic_slice_in_dim(ratio, lax.axis_index("wide") * share, share)
    modes, carries = y_forward(turn(spectrum, "narrow"), ratio, wide_count)
    carries = turn(join_carries(turn(carries, "wide"), own_ratio, x_local // 2), "wide")
    return turn(y_inverse(modes, carries, ratio, gain, count), "narrow")


def conduct(profile, spread):
    sides = (("wide", 0), ("narrow", 1))
    spread = with_halo(spread, sides, STEPS - 1, False)
    profile = with_halo(profile, sides, STEPS, False)
    for step in range(STEPS):
        center = profile[1:-1, 1:-1]
        near = (
            profile[2:, 1:-1] + profile[:-2, 1:-1] + profile[1:-1, 2:] + profile[1:-1, :-2]
        )
        ahead = jnp.pad(center[:, :, 1:], ((0, 0), (0, 0), (0, 1)))
        behind = jnp.pad(center[:, :, :-1], ((0, 0), (0, 0), (1, 0)))
        profile = center + spread * (near + ahead + behind - 6.0 * center)
        spread = spread[1:-1, 1:-1]
    return profile


def per_device(
    material_flow_vector,
    tool_push_density,
    tool_warmth_excess,
    substrate_warmth_excess,
    spread_coefficient,
    source_owner_sheet,
    source_part_line,
):
    flow = material_flow_vector
    flow_x, flow_y = ring(flow, "wide", 1), ring(flow, "narrow", 2)
    current, current_x, current_y = flow, flow_x, flow_y
    for section in range(PASSES):
        last = section + 1 == PASSES
        inner = viscosity_inner(current, current_y, tool_warmth_excess, last)
        fields = viscosity_call(current, current_y, tool_warmth_excess, last, current_x, inner)
        mu = fields[0]
        mu_x, mu_y = ring(mu, "wide", 0), ring(mu, "narrow", 1)
        inner = advance_inner(flow, flow_y, mu, mu_y, tool_push_density)
        current = advance_call(flow, flow_y, mu, mu_y, tool_push_density, flow_x, mu_x, inner)
        if not last:
            current_x, current_y = ring(current, "wide", 1), ring(current, "narrow", 2)
    heat_cells = fields[1]
    end_x = ring(current[0], "wide", 0)
    y_local = flow.shape[2]
    end_y = [
        shift(current[1, :, y_local - 1 :], "narrow", 1)[:, 0],
        shift(current[1, :, :1], "narrow", -1)[:, 0],
    ]
    modes = divergence_modes(current, lax.axis_size("narrow"))
    spectrum = project(add_halo_modes(modes, end_x, end_y))
    inner = spectrum[:, 1:-1]
    corrected_flow_vector = corrected(
        current, spectrum, [side[:, :, 0] for side in ring(inner, "narrow", 2)]
    )
    z_blocks = heat_cells.shape[0]
    slab_count = lax.axis_size("wide")
    component_lines = substrate_warmth_excess.shape[0] * substrate_warmth_excess.shape[1]
    targets = source_owner_sheet[:, 0] * component_lines + source_part_line
    partial_value = (
        jnp.zeros((slab_count * component_lines, 128), jnp.float32)
        .at[targets.reshape(-1, z_blocks).T.reshape(-1)]
        .add(heat_cells.reshape(-1, 128))
    )
    substrate_energy_input = lax.psum_scatter(
        partial_value.reshape(slab_count, component_lines, 128),
        "wide",
        scatter_dimension=0,
        tiled=True,
    )
    thermal_profile = substrate_warmth_excess + dissipation_factor * substrate_energy_input.reshape(
        substrate_warmth_excess.shape
    )
    return (corrected_flow_vector, conduct(thermal_profile, spread_coefficient))


def solution(mesh):
    return jax.shard_map(
        per_device,
        mesh=mesh,
        in_specs=(
            P(None, "wide", "narrow", None),
            P(None, "wide", "narrow", None),
            P("wide", "narrow", None),
            P("wide", "narrow", None),
            P("wide", "narrow", None),
            P(("wide", "narrow"), None),
            P(("wide", "narrow")),
        ),
        out_specs=(P(None, "wide", "narrow", None), P("wide", "narrow", None)),
        check_vma=False,
    )
```

```python
import math

import jax
import jax.numpy as jnp
import numpy as np
from jax import lax
from jax.experimental import pallas as pl
from jax.experimental.pallas import tpu as pltpu
from jax.sharding import PartitionSpec as P

PASSES = 2
STEPS = 3


time_step = 0.15
rate_base = 0.5
zener_energy = 4.0
stress_exponent = 5.0
penalty = 0.001
dissipation_factor = 0.1


def with_halo(x, sides, width, wrap):
    for axis, dim in sides:
        size, length = (lax.axis_size(axis), x.shape[dim])
        up = [(i, (i + 1) % size) for i in range(size if wrap else size - 1)]
        down = [(j, i) for i, j in up]
        last = lax.slice_in_dim(x, length - width, length, axis=dim)
        initial = lax.slice_in_dim(x, 0, width, axis=dim)
        before = lax.ppermute(last, axis, up)
        after = lax.ppermute(initial, axis, down)
        x = jnp.concatenate([before, x, after], axis=dim)
    return x


def shift(value, axis, by):
    size = lax.axis_size(axis)
    return lax.ppermute(value, axis, [(i, (i + by) % size) for i in range(size)])


def ring(value, axis, dim):
    length = value.shape[dim]
    last = lax.slice_in_dim(value, length - 1, length, axis=dim)
    initial = lax.slice_in_dim(value, 0, 1, axis=dim)
    return shift(last, axis, 1), shift(initial, axis, -1)


anywhere = pl.BlockSpec(memory_space=pl.ANY)
in_vmem = pl.BlockSpec(memory_space=pltpu.VMEM)
scaled_mu = 0.5 * time_step
vmem_limit = 48 << 20


def row_numbers(width):
    return lax.broadcasted_iota(jnp.int32, (8, width), 0)


def rows_of(strip):
    return pl.ds(8 * strip, 8)


def pick(ref, index):
    return ref.at[:, index] if len(ref.shape) == 4 else ref.at[index]


class Planes:
    def __init__(self, source, target, semaphores):
        self.source, self.target, self.semaphores = source, target, semaphores

    def copy(self, slot):
        return pltpu.make_async_copy(
            pick(self.source, slot), pick(self.target, slot), self.semaphores.at[slot]
        )

    def start(self, slot):
        self.copy(slot).start()

    def wait(self, slot):
        self.copy(slot).wait()


def cut(ref, first, planes, row, rows):
    part, lines = pl.ds(first, planes), pl.ds(row, rows)
    return ref.at[:, part, lines] if len(ref.shape) == 4 else ref.at[part, lines]


def in_sections(x_local, size, loads, stores, start_up, body):
    count = x_local // size

    def moves(kinds, section, first, planes, row=0):
        return [
            pltpu.make_async_copy(
                cut(source, first, planes, row, source.shape[-2] - 2 * row),
                cut(target, first, planes, row, source.shape[-2] - 2 * row),
                semaphores.at[section],
            )
            for source, target, semaphores in kinds
        ]

    def begin(section, state):
        for move in moves(loads, section, section * size, size):
            move.start()
        return state

    lax.fori_loop(0, count, begin, 0)

    def work(section, first, planes):
        for move in moves(loads, section, section * size, size):
            move.wait()
        if isinstance(first, int):
            start_up()
        lax.fori_loop(first, first + planes, body, 0)
        for move in moves(stores, section, first, planes, 8):
            move.start()

    work(0, 1, size - 2)

    def rest(section, state):
        work(section, section * size - 1, size)
        return state

    lax.fori_loop(1, count, rest, 0)
    for move in moves(stores, 0, 1, size - 2, 8):
        move.wait()

    def finish(section, state):
        for move in moves(stores, section, section * size - 1, size, 8):
            move.wait()
        return state

    lax.fori_loop(1, count, finish, 0)


def frame_loads(source, low, high, target, semaphores, x_local, y_local):
    ends = [
        pltpu.make_async_copy(pick(ref, plane), pick(target, slot), semaphores.at[i])
        for i, (ref, plane, slot) in enumerate(
            [
                (low, 0, 0),
                (source, 0, 1),
                (source, 1, 2),
                (source, x_local - 2, x_local - 1),
                (source, x_local - 1, x_local),
                (high, 0, x_local + 1),
            ]
        )
    ]
    lines = [
        pltpu.make_async_copy(
            cut(source, 2, x_local - 4, row, 16),
            cut(target, 3, x_local - 4, row, 16),
            semaphores.at[6 + i],
        )
        for i, row in enumerate((0, y_local - 16))
    ]
    return ends, lines


def frame_parts(source, target, semaphores, x_local, y_local):
    return [
        pltpu.make_async_copy(pick(source, plane), pick(target, plane), semaphores.at[i])
        for i, plane in enumerate((0, x_local - 1))
    ] + [
        pltpu.make_async_copy(
            cut(source, 1, x_local - 2, row, 8),
            cut(target, 1, x_local - 2, row, 8),
            semaphores.at[2 + i],
        )
        for i, row in enumerate((0, y_local - 8))
    ]


def neighbour_rows(span, y_local, take, halo):
    before = take(8 * span[0] - 1) if span[0] else halo(0)
    after = take(8 * span[1]) if 8 * span[1] < y_local else halo(1)
    return before, after


def viscosity_plane(cells, slot, span, halo, warmth, warm_slot, outs, out_slot, y_local, z_cells):
    strips, rows = range(*span), row_numbers(z_cells)
    values = [{s: cells[c, slot, rows_of(s), :] for s in strips} for c in range(3)]
    up = [{s: pltpu.roll(v, 7, 0) for s, v in row.items()} for row in values]
    down = [{s: pltpu.roll(v, 1, 0) for s, v in row.items()} for row in values]
    sides = [
        neighbour_rows(
            span,
            y_local,
            lambda row: cells[c, slot, pl.ds(row, 1), :],
            lambda side: halo[side][c, out_slot],
        )
        for c in range(3)
    ]
    for s in strips:
        along_x, along_y, along_z = [], [], []
        for c in range(3):
            value = values[c][s]
            along_x.append(cells[c, slot + 1, rows_of(s), :] - cells[c, slot - 1, rows_of(s), :])
            ahead = jnp.where(
                rows == 7, up[c][s + 1] if s + 1 in strips else sides[c][1], up[c][s]
            )
            behind = jnp.where(
                rows == 0, down[c][s - 1] if s - 1 in strips else sides[c][0], down[c][s]
            )
            along_y.append(ahead - behind)
            along_z.append(pltpu.roll(value, z_cells - 1, 1) - pltpu.roll(value, 1, 1))
        s_xy = along_y[0] + along_x[1]
        s_xz = along_z[0] + along_x[2]
        s_yz = along_z[1] + along_y[2]
        extra = 0.5 * (
            along_x[0] * along_x[0] + along_y[1] * along_y[1] + along_z[2] * along_z[2]
        ) + 0.25 * (s_xy * s_xy + s_xz * s_xz + s_yz * s_yz)
        rate_sq = rate_base**2 + extra
        value = jnp.exp(
            (0.5 / stress_exponent) * jnp.log(rate_sq)
            + (zener_energy / stress_exponent) * (1.0 / warmth[warm_slot, rows_of(s), :] - 1.0)
        )
        square = value * value + 1.0
        mu = jnp.log(value + square * lax.rsqrt(square)) * lax.rsqrt(rate_sq)
        outs[0][out_slot, rows_of(s), :] = mu * (scaled_mu / 3.0)
        if len(outs) > 1:
            heat = (mu * (1.0 / 3.0)) * extra
            for b in range(z_cells // 128):
                outs[1][b, out_slot, rows_of(s), :] = heat[:, b * 128 : (b + 1) * 128]


def viscosity_frame(flow, x_sides, y_sides, warmth, inner):
    _, x_local, y_local, z_cells = flow.shape
    outputs, strips = len(inner), y_local // 8

    def kernel(flow_ref, low, high, before_ref, after_ref, warmth_ref, *rest):
        out_refs, rest = rest[outputs : 2 * outputs], rest[2 * outputs :]
        cells, cell_sem, warm, warm_sem = rest[:4]
        outs, sems = rest[4 : 4 + outputs], rest[4 + outputs :]
        ends, lines = frame_loads(flow_ref, low, high, cells, cell_sem, x_local, y_local)
        warms = frame_parts(warmth_ref, warm, warm_sem, x_local, y_local)
        stores = [
            frame_parts(outs[k], out_refs[k], sems[k], x_local, y_local) for k in range(outputs)
        ]
        for load in ends + warms[:2] + lines + warms[2:]:
            load.start()
        for load in ends + warms[:2]:
            load.wait()

        def work(plane, *span):
            viscosity_plane(
                cells,
                plane + 1,
                span,
                (before_ref, after_ref),
                warm,
                plane,
                outs,
                plane,
                y_local,
                z_cells,
            )

        def end_plane(i, state):
            work(i * (x_local - 1), 0, strips)
            return state

        lax.fori_loop(0, 2, end_plane, 0)
        for k in range(outputs):
            for store in stores[k][:2]:
                store.start()
        for load in lines + warms[2:]:
            load.wait()

        def side_strips(plane, state):
            work(plane, 0, 1)
            work(plane, strips - 1, strips)
            return state

        lax.fori_loop(1, x_local - 1, side_strips, 0)
        for k in range(outputs):
            for store in stores[k][2:]:
                store.start()
        for k in range(outputs):
            for store in stores[k]:
                store.wait()

    return pl.pallas_call(
        kernel,
        in_specs=[anywhere] * 3 + [in_vmem] * 2 + [anywhere] * (1 + outputs),
        out_specs=[anywhere] * outputs,
        out_shape=[jax.ShapeDtypeStruct(field.shape, jnp.float32) for field in inner],
        input_output_aliases={6 + k: k for k in range(outputs)},
        scratch_shapes=[
            pltpu.VMEM((3, x_local + 2, y_local, z_cells), jnp.float32),
            pltpu.SemaphoreType.DMA((8,)),
            pltpu.VMEM(warmth.shape, jnp.float32),
            pltpu.SemaphoreType.DMA((4,)),
        ]
        + [pltpu.VMEM(field.shape, jnp.float32) for field in inner]
        + [pltpu.SemaphoreType.DMA((4,))] * outputs,
        compiler_params=pltpu.CompilerParams(vmem_limit_bytes=vmem_limit),
        name="viscosity_frame",
    )(flow, *x_sides, *y_sides, warmth, *inner)


def viscosity_inner(flow, warmth, with_heat):
    _, x_local, y_local, z_cells = flow.shape
    z_blocks, size = z_cells // 128, 4
    outputs = 2 if with_heat else 1

    def kernel(flow_ref, warmth_ref, *rest):
        out_refs, (cells, cell_sem, warm, warm_sem, *heat) = rest[:outputs], rest[outputs:]
        outs = [out_refs[0]] + heat[:1]

        def body(slot, state):
            viscosity_plane(
                cells,
                slot,
                (1, y_local // 8 - 1),
                None,
                warm,
                slot,
                outs,
                slot,
                y_local,
                z_cells,
            )
            return state

        in_sections(
            x_local,
            size,
            [(flow_ref, cells, cell_sem), (warmth_ref, warm, warm_sem)],
            [(heat[0], out_refs[1], heat[1])] if with_heat else [],
            lambda: None,
            body,
        )

    shapes = [(x_local, y_local, z_cells), (z_blocks, x_local, y_local, 128)][:outputs]
    sems = pltpu.SemaphoreType.DMA((x_local // size,))
    return pl.pallas_call(
        kernel,
        in_specs=[anywhere, anywhere],
        out_specs=[in_vmem, anywhere][:outputs],
        out_shape=[jax.ShapeDtypeStruct(shape, jnp.float32) for shape in shapes],
        scratch_shapes=[
            pltpu.VMEM(flow.shape, jnp.float32),
            sems,
            pltpu.VMEM(warmth.shape, jnp.float32),
            sems,
        ]
        + ([pltpu.VMEM(shapes[1], jnp.float32), sems] if with_heat else []),
        compiler_params=pltpu.CompilerParams(vmem_limit_bytes=vmem_limit),
        name="viscosity_inner",
    )(flow, warmth)


def advance_plane(cells, mu, slot, mu_slot, span, halo, push, plane, flux, y_local, z_cells):
    strips, rows = range(*span), row_numbers(z_cells)
    m = {s: mu[mu_slot, rows_of(s), :] for s in strips}
    m_up = {s: pltpu.roll(v, 7, 0) for s, v in m.items()}
    mu_before, mu_after = neighbour_rows(
        span,
        y_local,
        lambda row: mu[mu_slot, pl.ds(row, 1), :],
        lambda side: halo[1][side][plane],
    )
    sums_y = {
        s: m[s] + jnp.where(rows == 7, m_up[s + 1] if s + 1 in strips else mu_after, m_up[s])
        for s in strips
    }
    start = pl.ds(8 * span[0], 1)
    first_sum = mu_before + mu[mu_slot, start, :]
    values = [{s: cells[c, slot, rows_of(s), :] for s in strips} for c in range(3)]
    up = [{s: pltpu.roll(v, 7, 0) for s, v in row.items()} for row in values]
    sides = [
        neighbour_rows(
            span,
            y_local,
            lambda row: cells[c, slot, pl.ds(row, 1), :],
            lambda side: halo[0][side][c, plane],
        )
        for c in range(3)
    ]
    carried = [first_sum * (cells[c, slot, start, :] - sides[c][0]) for c in range(3)]
    for s in strips:
        sum_x = m[s] + mu[mu_slot + 1, rows_of(s), :]
        sum_z_ahead = m[s] + pltpu.roll(m[s], z_cells - 1, 1)
        sum_z_behind = m[s] + pltpu.roll(m[s], 1, 1)
        for c in range(3):
            value = values[c][s]
            flux_x = sum_x * (cells[c, slot + 1, rows_of(s), :] - value)
            ahead = jnp.where(
                rows == 7, up[c][s + 1] if s + 1 in strips else sides[c][1], up[c][s]
            )
            flux_y = sums_y[s] * (ahead - value)
            turned = pltpu.roll(flux_y, 1, 0)
            total = (flux_x - flux[c, rows_of(s), :]) + (
                flux_y - jnp.where(rows == 0, carried[c], turned)
            ) + (
                sum_z_ahead * (pltpu.roll(value, z_cells - 1, 1) - value)
                - sum_z_behind * (value - pltpu.roll(value, 1, 1))
            )
            flux[c, rows_of(s), :] = flux_x
            carried[c] = turned
            push[c, plane, rows_of(s), :] = (
                value + time_step * push[c, plane, rows_of(s), :] + total
            )


def first_flux(cells, mu, slot, mu_slot, strips, flux):
    for s in strips:
        sum_x = mu[mu_slot - 1, rows_of(s), :] + mu[mu_slot, rows_of(s), :]
        for c in range(3):
            flux[c, rows_of(s), :] = sum_x * (
                cells[c, slot, rows_of(s), :] - cells[c, slot - 1, rows_of(s), :]
            )


def advance_frame(flow, flow_x, flow_y, mu, mu_x, mu_y, push, inner):
    _, x_local, y_local, z_cells = flow.shape
    strips = y_local // 8

    def kernel(
        flow_ref, flow_low, flow_high, flow_before, flow_after,
        mu_ref, mu_low, mu_high, mu_before, mu_after, push_ref, _,
        out_ref, cells, cell_sem, mu_cells, mu_sem, work, work_sem, out_sem, flux,
    ):
        ends, lines = frame_loads(
            flow_ref, flow_low, flow_high, cells, cell_sem, x_local, y_local
        )
        mu_ends, mu_lines = frame_loads(
            mu_ref, mu_low, mu_high, mu_cells, mu_sem, x_local, y_local
        )
        pushes = frame_parts(push_ref, work, work_sem, x_local, y_local)
        stores = frame_parts(work, out_ref, out_sem, x_local, y_local)
        early, late = ends + mu_ends + pushes[:2], lines + mu_lines + pushes[2:]
        for load in early + late:
            load.start()
        for load in early:
            load.wait()

        def advance(plane, *span):
            advance_plane(
                cells,
                mu_cells,
                plane + 1,
                plane + 1,
                span,
                ((flow_before, flow_after), (mu_before, mu_after)),
                work,
                plane,
                flux,
                y_local,
                z_cells,
            )

        def end_plane(i, state):
            plane = i * (x_local - 1)
            first_flux(cells, mu_cells, plane + 1, plane + 1, range(strips), flux)
            advance(plane, 0, strips)
            return state

        lax.fori_loop(0, 2, end_plane, 0)
        for store in stores[:2]:
            store.start()
        for load in late:
            load.wait()
        first_flux(cells, mu_cells, 2, 2, (0, strips - 1), flux)

        def side_strips(plane, state):
            advance(plane, 0, 1)
            advance(plane, strips - 1, strips)
            return state

        lax.fori_loop(1, x_local - 1, side_strips, 0)
        for store in stores[2:]:
            store.start()
        for store in stores:
            store.wait()

    return pl.pallas_call(
        kernel,
        in_specs=[anywhere] * 3
        + [in_vmem] * 2
        + [anywhere] * 3
        + [in_vmem] * 2
        + [anywhere] * 2,
        out_specs=anywhere,
        out_shape=jax.ShapeDtypeStruct(flow.shape, jnp.float32),
        input_output_aliases={11: 0},
        scratch_shapes=[
            pltpu.VMEM((3, x_local + 2, y_local, z_cells), jnp.float32),
            pltpu.SemaphoreType.DMA((8,)),
            pltpu.VMEM((x_local + 2, y_local, z_cells), jnp.float32),
            pltpu.SemaphoreType.DMA((8,)),
            pltpu.VMEM(flow.shape, jnp.float32),
            pltpu.SemaphoreType.DMA((4,)),
            pltpu.SemaphoreType.DMA((4,)),
            pltpu.VMEM((3, y_local, z_cells), jnp.float32),
        ],
        compiler_params=pltpu.CompilerParams(vmem_limit_bytes=vmem_limit),
        name="advance_frame",
    )(flow, *flow_x, *flow_y, mu, *mu_x, *mu_y, push, inner)


def advance_inner(flow, mu, push):
    _, x_local, y_local, z_cells = flow.shape
    size, span = 4, (1, y_local // 8 - 1)

    def kernel(
        flow_ref, mu_ref, push_ref, out_ref, cells, cell_sem, work, work_sem, out_sem, flux
    ):
        def body(slot, state):
            advance_plane(
                cells, mu_ref, slot, slot, span, None, work, slot, flux, y_local, z_cells
            )
            return state

        in_sections(
            x_local,
            size,
            [(flow_ref, cells, cell_sem), (push_ref, work, work_sem)],
            [(work, out_ref, out_sem)],
            lambda: first_flux(cells, mu_ref, 1, 1, range(*span), flux),
            body,
        )

    sems = pltpu.SemaphoreType.DMA((x_local // size,))
    return pl.pallas_call(
        kernel,
        in_specs=[anywhere, in_vmem, anywhere],
        out_specs=anywhere,
        out_shape=jax.ShapeDtypeStruct(flow.shape, jnp.float32),
        scratch_shapes=[
            pltpu.VMEM(flow.shape, jnp.float32),
            sems,
            pltpu.VMEM(flow.shape, jnp.float32),
            sems,
            sems,
            pltpu.VMEM((3, y_local, z_cells), jnp.float32),
        ],
        compiler_params=pltpu.CompilerParams(vmem_limit_bytes=vmem_limit),
        name="advance_inner",
    )(flow, mu, push)


def cosine_sine_basis(points, period, waves):
    columns, eigen = [], []
    for wave in waves:
        angle = 2.0 * np.pi * ((wave * np.arange(points)) % period) / period
        single = wave % period == 0 or 2 * wave == period
        size = math.sqrt((1.0 if single else 2.0) / period)
        columns.append(np.cos(angle) * size)
        eigen.append(math.sin(2.0 * math.pi * wave / period) ** 2)
        if not single:
            columns.append(np.sin(angle) * size)
            eigen.append(eigen[-1])
    return np.stack(columns, 1), np.array(eigen)


def halves(table):
    table = np.asarray(table, np.float32)
    high = table.astype(jnp.bfloat16)
    low = (table - high.astype(np.float32)).astype(jnp.bfloat16)
    return jnp.asarray(high), jnp.asarray(low)


def split(value):
    high = value.astype(jnp.bfloat16)
    return high, (value - high.astype(jnp.float32)).astype(jnp.bfloat16)


def triple_product(left, right):
    def product(one, two):
        return lax.dot_general(
            one, two, (((1,), (0,)), ((), ())), preferred_element_type=jnp.float32
        )

    return product(left[0], right[0]) + (product(left[0], right[1]) + product(left[1], right[0]))


def z_tables(z_cells):
    half = z_cells // 2
    even, eigen_even = cosine_sine_basis(half, z_cells, range(0, half + 1, 2))
    odd, eigen_odd = cosine_sine_basis(half, z_cells, range(1, half, 2))
    return even, odd, np.concatenate([eigen_even, eigen_odd])


def whole(*shape):
    return pl.BlockSpec(shape, lambda *index: (0,) * len(shape))


def modes_of(lines, even_high, even_low, odd_high, odd_low):
    half = lines.shape[1] // 2
    first, second = lines[:, :half], lines[:, half:]
    return jnp.concatenate(
        [
            triple_product(split(first + second), (even_high[...], even_low[...])),
            triple_product(split(first - second), (odd_high[...], odd_low[...])),
        ],
        1,
    )


def cells_of(modes, even_high, even_low, odd_high, odd_low):
    half = modes.shape[1] // 2
    first = triple_product(split(modes[:, :half]), (even_high[...], even_low[...]))
    second = triple_product(split(modes[:, half:]), (odd_high[...], odd_low[...]))
    return jnp.concatenate([first + second, first - second], 1)


def divergence_modes(flow, count):
    _, x_local, y_local, z_cells = flow.shape
    half, piece, strips = z_cells // 2, z_cells // count, y_local // 8
    step = min(8, x_local)
    even, odd, _ = z_tables(z_cells)
    tables = halves(even) + halves(odd)

    def kernel(
        flow_ref, even_high, even_low, odd_high, odd_low, out_ref,
        cells, semaphores, work, made, out_sem,
    ):
        planes = Planes(flow_ref, cells, semaphores)
        rows = row_numbers(z_cells)

        def begin(i, state):
            planes.start(i)
            return state

        lax.fori_loop(0, x_local, begin, 0)
        planes.wait(0)

        def stored(k):
            part = pl.ds(k * step, step)
            return pltpu.make_async_copy(made.at[:, part], out_ref.at[:, part], out_sem.at[k])

        def group(k, state):
            def plane(i, state):
                j = k * step + i

                @pl.when(j + 1 < x_local)
                def _():
                    planes.wait(j + 1)

                nearer = jnp.where(j > 0, 0.5, 0.0)
                further = jnp.where(j + 1 < x_local, 0.5, 0.0)
                last, following = jnp.maximum(j - 1, 0), jnp.minimum(j + 1, x_local - 1)
                across = [cells[1, j, rows_of(s), :] for s in range(strips)]
                up = [pltpu.roll(v, 7, 0) for v in across]
                down = [pltpu.roll(v, 1, 0) for v in across]
                for s in range(strips):
                    ahead = jnp.where(rows == 7, up[s + 1] if s + 1 < strips else 0.0, up[s])
                    behind = jnp.where(rows == 0, down[s - 1] if s else 0.0, down[s])
                    along = cells[2, j, rows_of(s), :]
                    work[i, rows_of(s), :] = (
                        further * cells[0, following, rows_of(s), :]
                        - nearer * cells[0, last, rows_of(s), :]
                    ) + 0.5 * (
                        (ahead - behind)
                        + (pltpu.roll(along, z_cells - 1, 1) - pltpu.roll(along, 1, 1))
                    )
                return state

            lax.fori_loop(0, step, plane, 0)
            modes = modes_of(
                work[...].reshape(step * y_local, z_cells), even_high, even_low, odd_high, odd_low
            )
            for n in range(count):
                made[n, pl.ds(k * step, step)] = modes[:, n * piece : (n + 1) * piece].reshape(
                    step, y_local, piece
                )
            stored(k).start()
            return state

        groups = x_local // step
        lax.fori_loop(0, groups, group, 0)
        for k in range(groups):
            stored(k).wait()

    return pl.pallas_call(
        kernel,
        in_specs=[anywhere] + [in_vmem] * 4,
        out_specs=anywhere,
        out_shape=jax.ShapeDtypeStruct((count, x_local, y_local, piece), jnp.float32),
        scratch_shapes=[
            pltpu.VMEM((3, x_local, y_local, z_cells), jnp.float32),
            pltpu.SemaphoreType.DMA((x_local,)),
            pltpu.VMEM((step, y_local, z_cells), jnp.float32),
            pltpu.VMEM((count, x_local, y_local, piece), jnp.float32),
            pltpu.SemaphoreType.DMA((x_local // step,)),
        ],
        name="divergence_modes",
    )(flow, *tables)


def add_halo_modes(modes, x_sides, y_sides):
    count, x_local, y_local, piece = modes.shape
    z_cells = count * piece
    even, odd, _ = z_tables(z_cells)
    tables = halves(even) + halves(odd)

    def kernel(
        modes_ref, low_ref, high_ref, before_ref, after_ref,
        even_high, even_low, odd_high, odd_low, out_ref, ends, lines, semaphores,
    ):
        def moves(back):
            pairs = [
                (ends.at[k], modes_ref.at[:, plane])
                for k, plane in enumerate((0, x_local - 1))
            ] + [
                (lines.at[k], modes_ref.at[:, 1 : x_local - 1, 8 * s : 8 * s + 8])
                for k, s in enumerate((0, y_local // 8 - 1))
            ]
            if back:
                pairs = [
                    (ends.at[k], out_ref.at[:, plane])
                    for k, plane in enumerate((0, x_local - 1))
                ] + [
                    (lines.at[k], out_ref.at[:, 1 : x_local - 1, 8 * s : 8 * s + 8])
                    for k, s in enumerate((0, y_local // 8 - 1))
                ]
                return [
                    pltpu.make_async_copy(here, there, semaphores.at[4 + i])
                    for i, (here, there) in enumerate(pairs)
                ]
            return [
                pltpu.make_async_copy(there, here, semaphores.at[i])
                for i, (here, there) in enumerate(pairs)
            ]

        loads, stores = moves(False), moves(True)
        for load in loads:
            load.start()
        added = modes_of(
            jnp.concatenate(
                [-0.5 * low_ref[0], 0.5 * high_ref[0], -0.5 * before_ref[...], 0.5 * after_ref[...]],
                0,
            ),
            even_high,
            even_low,
            odd_high,
            odd_low,
        )
        for load in loads:
            load.wait()
        rows = row_numbers(piece)
        for n in range(count):
            block = added[:, n * piece : (n + 1) * piece]
            side = [block[2 * y_local + k * x_local :][:x_local] for k in range(2)]
            for k, plane in enumerate((0, x_local - 1)):
                ends[k, n] = ends[k, n] + block[k * y_local : (k + 1) * y_local]
                for j, (strip, row) in enumerate(((0, 0), (y_local // 8 - 1, 7))):
                    part = pl.ds(8 * strip, 8)
                    ends[k, n, part, :] = ends[k, n, part, :] + jnp.where(
                        rows == row, side[j][plane : plane + 1], 0.0
                    )
            for j, row in enumerate((0, 7)):
                for x in range(1, x_local - 1):
                    lines[j, n, x - 1] = lines[j, n, x - 1] + jnp.where(
                        rows == row, side[j][x : x + 1], 0.0
                    )
        for store in stores:
            store.start()
        for store in stores:
            store.wait()

    return pl.pallas_call(
        kernel,
        in_specs=[anywhere] + [in_vmem] * 8,
        out_specs=anywhere,
        out_shape=jax.ShapeDtypeStruct(modes.shape, jnp.float32),
        input_output_aliases={0: 0},
        scratch_shapes=[
            pltpu.VMEM((2, count, y_local, piece), jnp.float32),
            pltpu.VMEM((2, count, x_local - 2, 8, piece), jnp.float32),
            pltpu.SemaphoreType.DMA((8,)),
        ],
        name="add_halo_modes",
    )(modes, *x_sides, *y_sides, *tables)


def corrected(flow, spectrum, y_sides):
    count, planes, y_local, piece = spectrum.shape
    x_local, z_cells = planes - 2, count * piece
    strips, part = y_local // 8, planes // 2
    even, odd, _ = z_tables(z_cells)
    tables = halves(even.T) + halves(odd.T)

    def kernel(
        flow_ref, in_ref, before_ref, after_ref,
        even_high, even_low, odd_high, odd_low, out_ref,
        modes, mode_sem, pressure, sides, work, flow_sem, out_sem,
    ):
        flow_planes = Planes(flow_ref, work, flow_sem)
        table_refs = (even_high, even_low, odd_high, odd_low)

        def load(k):
            span = pl.ds(k * part, part)
            return pltpu.make_async_copy(in_ref.at[:, span], modes.at[:, span], mode_sem.at[k])

        load(0).start()
        load(1).start()

        def begin(i, state):
            flow_planes.start(i)
            return state

        lax.fori_loop(0, x_local, begin, 0)
        sides[...] = cells_of(
            jnp.concatenate(
                [
                    jnp.concatenate([ref[n] for n in range(count)], 1)
                    for ref in (before_ref, after_ref)
                ],
                0,
            ),
            *table_refs,
        )
        rows = row_numbers(z_cells)

        def stored(i):
            return pltpu.make_async_copy(pick(work, i), pick(out_ref, i), out_sem.at[i])

        def plane(j, state):
            flow_planes.wait(j)
            values = [pressure[j + 1, rows_of(s), :] for s in range(strips)]
            up = [pltpu.roll(v, 7, 0) for v in values]
            down = [pltpu.roll(v, 1, 0) for v in values]
            for s in range(strips):
                ahead = up[s + 1] if s + 1 < strips else sides[pl.ds(x_local + j, 1), :]
                behind = down[s - 1] if s else sides[pl.ds(j, 1), :]
                slopes = (
                    pressure[j + 2, rows_of(s), :] - pressure[j, rows_of(s), :],
                    jnp.where(rows == 7, ahead, up[s]) - jnp.where(rows == 0, behind, down[s]),
                    pltpu.roll(values[s], z_cells - 1, 1) - pltpu.roll(values[s], 1, 1),
                )
                for c in range(3):
                    work[c, j, rows_of(s), :] = work[c, j, rows_of(s), :] - 0.5 * slopes[c]
            stored(j).start()
            return state

        for k in range(2):
            load(k).wait()
            span = pl.ds(k * part, part)
            pressure[span] = cells_of(
                jnp.concatenate(
                    [modes[n, span].reshape(part * y_local, piece) for n in range(count)], 1
                ),
                *table_refs,
            ).reshape(part, y_local, z_cells)
            lax.fori_loop(k * (part - 2), (part - 2) if k == 0 else x_local, plane, 0)

        def finish(i, state):
            stored(i).wait()
            return state

        lax.fori_loop(0, x_local, finish, 0)

    return pl.pallas_call(
        kernel,
        in_specs=[anywhere, anywhere] + [in_vmem] * 6,
        out_specs=anywhere,
        out_shape=jax.ShapeDtypeStruct(flow.shape, jnp.float32),
        scratch_shapes=[
            pltpu.VMEM(spectrum.shape, jnp.float32),
            pltpu.SemaphoreType.DMA((2,)),
            pltpu.VMEM((planes, y_local, z_cells), jnp.float32),
            pltpu.VMEM((2 * x_local, z_cells), jnp.float32),
            pltpu.VMEM(flow.shape, jnp.float32),
            pltpu.SemaphoreType.DMA((x_local,)),
            pltpu.SemaphoreType.DMA((x_local,)),
        ],
        compiler_params=pltpu.CompilerParams(vmem_limit_bytes=vmem_limit),
        name="corrected",
    )(flow, spectrum, *y_sides, *tables)


def y_forward(spectrum, ratio, wide_count):
    count, x_local, y_local, piece = spectrum.shape
    y_cells, pairs = count * y_local, x_local // 2
    share, group = y_cells // wide_count, max(2, x_local // 4)
    table, _ = cosine_sine_basis(y_cells, y_cells, range(y_cells // 2 + 1))
    tables = halves(table.T)

    def kernel(
        in_ref, high_ref, low_ref, ratio_ref, modes_ref, carry_ref,
        lines, in_sems, made, out_sems, sums, power,
    ):
        def load(k):
            part = pl.ds(k * group, group)
            return pltpu.make_async_copy(in_ref.at[:, part], lines.at[:, part], in_sems.at[k])

        def stored(k):
            part = pl.ds(k * group, group)
            return pltpu.make_async_copy(made.at[part], modes_ref.at[part], out_sems.at[k])

        for k in range(x_local // group):
            load(k).start()
        sums[...] = jnp.zeros_like(sums)
        power[...] = jnp.ones_like(power)

        def body(t, state):
            planes = [
                jnp.concatenate([lines[n, 2 * t + side] for n in range(count)], 0)
                for side in range(2)
            ]
            modes = triple_product(
                (high_ref[...], low_ref[...]), split(jnp.concatenate(planes, 1))
            )
            r, pw = ratio_ref[...], power[...]
            for side in range(2):
                plane = modes[:, side * piece : (side + 1) * piece]
                made[2 * t + side] = plane
                sums[side] = plane + r * sums[side]
                sums[2 + side] = sums[2 + side] + pw * plane
            power[...] = pw * r
            return state

        def section(k, state):
            load(k).wait()
            lax.fori_loop(k * (group // 2), (k + 1) * (group // 2), body, 0)
            stored(k).start()
            return state

        lax.fori_loop(0, x_local // group, section, 0)
        for kind in range(4):
            carry_ref[:, kind] = sums[kind].reshape(wide_count, share, piece)
        for k in range(x_local // group):
            stored(k).wait()

    return pl.pallas_call(
        kernel,
        in_specs=[anywhere] + [in_vmem] * 3,
        out_specs=[anywhere, in_vmem],
        out_shape=[
            jax.ShapeDtypeStruct((x_local, y_cells, piece), jnp.float32),
            jax.ShapeDtypeStruct((wide_count, 4, share, piece), jnp.float32),
        ],
        scratch_shapes=[
            pltpu.VMEM(spectrum.shape, jnp.float32),
            pltpu.SemaphoreType.DMA((x_local // group,)),
            pltpu.VMEM((x_local, y_cells, piece), jnp.float32),
            pltpu.SemaphoreType.DMA((x_local // group,)),
            pltpu.VMEM((4, y_cells, piece), jnp.float32),
            pltpu.VMEM((y_cells, piece), jnp.float32),
        ],
        name="y_forward",
    )(spectrum, *tables, ratio)


def power_of(value, exponent):
    result = None
    while exponent:
        if exponent & 1:
            result = value if result is None else result * value
        value = value * value
        exponent >>= 1
    return result


def join_carries(carries, ratio, block):
    count, kinds, share, piece = carries.shape

    def kernel(in_ref, ratio_ref, out_ref):
        step = power_of(ratio_ref[...], block)
        scale = 1.0 / (1.0 - power_of(step, count))
        for kind in range(kinds):
            order = list(range(count)) if kind < 2 else list(range(count))[::-1]
            total = in_ref[order[0], kind]
            for w in order[1:]:
                total = in_ref[w, kind] + step * total
            total = total * scale
            for w in order:
                out_ref[w, kind] = total
                total = in_ref[w, kind] + step * total

    return pl.pallas_call(
        kernel,
        in_specs=[in_vmem] * 2,
        out_specs=in_vmem,
        out_shape=jax.ShapeDtypeStruct(carries.shape, jnp.float32),
        compiler_params=pltpu.CompilerParams(vmem_limit_bytes=vmem_limit),
        name="join_carries",
    )(carries, ratio)


def y_inverse(modes, carries, ratio, gain, count):
    x_local, y_cells, piece = modes.shape
    y_local, pairs, group = y_cells // count, x_local // 2, max(2, x_local // 4)
    table, _ = cosine_sine_basis(y_cells, y_cells, range(y_cells // 2 + 1))
    tables = halves(table)

    def kernel(
        modes_in, carry_ref, high_ref, low_ref, ratio_ref, gain_ref, out_ref,
        planes, in_sems, behind, state, cells, out_sems,
    ):
        def load(k):
            part = pl.ds(k * group, group)
            return pltpu.make_async_copy(modes_in.at[part], planes.at[part], in_sems.at[k])

        def stored(t):
            part = pl.ds(2 * t, 2)
            return pltpu.make_async_copy(cells.at[:, part], out_ref.at[:, part], out_sems.at[t])

        def carry(kind):
            return carry_ref[:, kind].reshape(y_cells, piece)

        groups = x_local // group
        for k in range(groups)[::-1]:
            load(k).start()
        for kind in range(4):
            state[kind] = carry(kind)
        behind[x_local + 1] = carry(2)

        def back(i, done):
            m = pairs - 1 - i
            r = ratio_ref[...]
            for side in range(2):
                value = r * state[2 + side]
                behind[2 * m + 1 + side] = value
                state[2 + side] = planes[2 * m + side] + value
            return done

        def back_section(k, done):
            load(groups - 1 - k).wait()
            lax.fori_loop(k * (group // 2), (k + 1) * (group // 2), back, 0)
            return done

        lax.fori_loop(0, groups, back_section, 0)
        behind[0] = ratio_ref[...] * state[3]

        def body(t, done):
            r, gain_value = ratio_ref[...], gain_ref[...]
            even_plane = planes[jnp.minimum(2 * t, x_local - 2)]
            odd_plane = planes[jnp.maximum(2 * t - 1, 1)]
            even = r * state[0] + jnp.where(t < pairs, even_plane, 0.0)
            odd = jnp.where(t > 0, odd_plane + r * state[1], state[1])
            state[0] = even
            state[1] = odd
            joined = jnp.concatenate(
                [gain_value * (odd + behind[2 * t]), gain_value * (even + behind[2 * t + 1])], 1
            )
            result = triple_product((high_ref[...], low_ref[...]), split(joined))
            for n in range(count):
                for side in range(2):
                    cells[n, 2 * t + side] = result[
                        n * y_local : (n + 1) * y_local, side * piece : (side + 1) * piece
                    ]
            stored(t).start()
            return done

        lax.fori_loop(0, pairs + 1, body, 0)

        def finish(t, done):
            stored(t).wait()
            return done

        lax.fori_loop(0, pairs + 1, finish, 0)

    made = (count, x_local + 2, y_local, piece)
    return pl.pallas_call(
        kernel,
        in_specs=[anywhere] + [in_vmem] * 5,
        out_specs=anywhere,
        out_shape=jax.ShapeDtypeStruct(made, jnp.float32),
        scratch_shapes=[
            pltpu.VMEM(modes.shape, jnp.float32),
            pltpu.SemaphoreType.DMA((x_local // group,)),
            pltpu.VMEM((x_local + 2, y_cells, piece), jnp.float32),
            pltpu.VMEM((4, y_cells, piece), jnp.float32),
            pltpu.VMEM(made, jnp.float32),
            pltpu.SemaphoreType.DMA((pairs + 1,)),
        ],
        name="y_inverse",
    )(modes, carries, *tables, ratio, gain)


def turn(value, axis):
    return lax.all_to_all(value, axis, split_axis=0, concat_axis=0, tiled=True)


def project(spectrum):
    count, x_local, y_local, piece = spectrum.shape
    y_cells, z_cells = count * y_local, count * piece
    wide_count = lax.axis_size("wide")
    _, eigen_y = cosine_sine_basis(y_cells, y_cells, range(y_cells // 2 + 1))
    eigen_z = jnp.asarray(z_tables(z_cells)[2], jnp.float32)
    own_z = lax.dynamic_slice_in_dim(eigen_z, lax.axis_index("narrow") * piece, piece)
    excess = 4.0 * (jnp.asarray(eigen_y, jnp.float32)[:, None] + own_z[None, :] + penalty)
    root = jnp.sqrt(excess * (4.0 + excess))
    ratio = 2.0 / (2.0 + excess + root)
    gain = -4.0 / root
    share = y_cells // wide_count
    own_ratio = lax.dynamic_slice_in_dim(ratio, lax.axis_index("wide") * share, share)
    modes, carries = y_forward(turn(spectrum, "narrow"), ratio, wide_count)
    carries = turn(join_carries(turn(carries, "wide"), own_ratio, x_local // 2), "wide")
    return turn(y_inverse(modes, carries, ratio, gain, count), "narrow")


def conduct(profile, spread):
    sides = (("wide", 0), ("narrow", 1))
    spread = with_halo(spread, sides, STEPS - 1, False)
    profile = with_halo(profile, sides, STEPS, False)
    for step in range(STEPS):
        center = profile[1:-1, 1:-1]
        near = (
            profile[2:, 1:-1] + profile[:-2, 1:-1] + profile[1:-1, 2:] + profile[1:-1, :-2]
        )
        ahead = jnp.pad(center[:, :, 1:], ((0, 0), (0, 0), (0, 1)))
        behind = jnp.pad(center[:, :, :-1], ((0, 0), (0, 0), (1, 0)))
        profile = center + spread * (near + ahead + behind - 6.0 * center)
        spread = spread[1:-1, 1:-1]
    return profile


def per_device(
    material_flow_vector,
    tool_push_density,
    tool_warmth_excess,
    substrate_warmth_excess,
    spread_coefficient,
    source_owner_sheet,
    source_part_line,
):
    flow = material_flow_vector
    flow_x, flow_y = ring(flow, "wide", 1), ring(flow, "narrow", 2)
    current, current_x, current_y = flow, flow_x, flow_y
    for section in range(PASSES):
        last = section + 1 == PASSES
        inner = viscosity_inner(current, tool_warmth_excess, last)
        fields = viscosity_frame(current, current_x, current_y, tool_warmth_excess, inner)
        mu = fields[0]
        mu_x, mu_y = ring(mu, "wide", 0), ring(mu, "narrow", 1)
        inner = advance_inner(flow, mu, tool_push_density)
        current = advance_frame(
            flow, flow_x, flow_y, mu, mu_x, mu_y, tool_push_density, inner
        )
        if not last:
            current_x, current_y = ring(current, "wide", 1), ring(current, "narrow", 2)
    heat_cells = fields[1]
    end_x = ring(current[0], "wide", 0)
    y_local = flow.shape[2]
    end_y = [
        shift(current[1, :, y_local - 1 :], "narrow", 1)[:, 0],
        shift(current[1, :, :1], "narrow", -1)[:, 0],
    ]
    modes = divergence_modes(current, lax.axis_size("narrow"))
    spectrum = project(add_halo_modes(modes, end_x, end_y))
    inner = spectrum[:, 1:-1]
    corrected_flow_vector = corrected(
        current, spectrum, [side[:, :, 0] for side in ring(inner, "narrow", 2)]
    )
    z_blocks = heat_cells.shape[0]
    slab_count = lax.axis_size("wide")
    component_lines = substrate_warmth_excess.shape[0] * substrate_warmth_excess.shape[1]
    targets = source_owner_sheet[:, 0] * component_lines + source_part_line
    partial_value = (
        jnp.zeros((slab_count * component_lines, 128), jnp.float32)
        .at[targets.reshape(-1, z_blocks).T.reshape(-1)]
        .add(heat_cells.reshape(-1, 128))
    )
    substrate_energy_input = lax.psum_scatter(
        partial_value.reshape(slab_count, component_lines, 128),
        "wide",
        scatter_dimension=0,
        tiled=True,
    )
    thermal_profile = substrate_warmth_excess + dissipation_factor * substrate_energy_input.reshape(
        substrate_warmth_excess.shape
    )
    return (corrected_flow_vector, conduct(thermal_profile, spread_coefficient))


def solution(mesh):
    return jax.shard_map(
        per_device,
        mesh=mesh,
        in_specs=(
            P(None, "wide", "narrow", None),
            P(None, "wide", "narrow", None),
            P("wide", "narrow", None),
            P("wide", "narrow", None),
            P("wide", "narrow", None),
            P(("wide", "narrow"), None),
            P(("wide", "narrow")),
        ),
        out_specs=(P(None, "wide", "narrow", None), P("wide", "narrow", None)),
        check_vma=False,
    )
```

```python
import math

import jax
import jax.numpy as jnp
import numpy as np
from jax import lax
from jax.experimental import pallas as pl
from jax.experimental.pallas import tpu as pltpu
from jax.sharding import PartitionSpec as P


PASSES = 2
STEPS = 3


time_step = 0.15
rate_base = 0.5
zener_energy = 4.0
stress_exponent = 5.0
penalty = 0.001
dissipation_factor = 0.1


def with_halo(x, sides, width, wrap):
    for axis, dim in sides:
        size, length = (lax.axis_size(axis), x.shape[dim])
        up = [(i, (i + 1) % size) for i in range(size if wrap else size - 1)]
        down = [(j, i) for i, j in up]
        last = lax.slice_in_dim(x, length - width, length, axis=dim)
        initial = lax.slice_in_dim(x, 0, width, axis=dim)
        before = lax.ppermute(last, axis, up)
        after = lax.ppermute(initial, axis, down)
        x = jnp.concatenate([before, x, after], axis=dim)
    return x


def shift(value, axis, by):
    size = lax.axis_size(axis)
    return lax.ppermute(value, axis, [(i, (i + by) % size) for i in range(size)])


def ring(value, axis, dim):
    length = value.shape[dim]
    last = lax.slice_in_dim(value, length - 1, length, axis=dim)
    initial = lax.slice_in_dim(value, 0, 1, axis=dim)
    return shift(last, axis, 1), shift(initial, axis, -1)


anywhere = pl.BlockSpec(memory_space=pl.ANY)
in_vmem = pl.BlockSpec(memory_space=pltpu.VMEM)
scaled_mu = 0.5 * time_step


def row_numbers(width):
    return lax.broadcasted_iota(jnp.int32, (8, width), 0)


def rows_of(strip):
    return pl.ds(8 * strip, 8)


def pick(ref, index):
    return ref.at[:, index] if len(ref.shape) == 4 else ref.at[index]


class Planes:
    def __init__(self, source, target, semaphores, listed=None):
        self.source, self.target, self.semaphores = source, target, semaphores
        self.listed = listed

    def copy(self, slot, ref, plane):
        return pltpu.make_async_copy(
            pick(ref, plane), pick(self.target, slot), self.semaphores.at[slot]
        )

    def start(self, slot, plane=None):
        if self.listed is None:
            self.copy(slot, self.source, slot if plane is None else plane).start()
        else:
            self.copy(slot, *self.listed[slot]).start()

    def wait(self, slot):
        self.copy(slot, self.source, 0).wait()


def in_sections(x_local, size, loads, stores, start_up, body):
    count = x_local // size

    def cut(ref, first, planes):
        part = pl.ds(first, planes)
        return ref.at[:, part] if len(ref.shape) == 4 else ref.at[part]

    def moves(kinds, section, first, planes):
        return [
            pltpu.make_async_copy(
                cut(source, first, planes), cut(target, first, planes), semaphores.at[section]
            )
            for source, target, semaphores in kinds
        ]

    def begin(section, state):
        for move in moves(loads, section, section * size, size):
            move.start()
        return state

    lax.fori_loop(0, count, begin, 0)

    def work(section, first, planes):
        for move in moves(loads, section, section * size, size):
            move.wait()
        if isinstance(first, int):
            start_up()
        lax.fori_loop(first, first + planes, body, 0)
        for move in moves(stores, section, first, planes):
            move.start()

    work(0, 1, size - 2)

    def rest(section, state):
        work(section, section * size - 1, size)
        return state

    lax.fori_loop(1, count, rest, 0)
    for move in moves(stores, 0, 1, size - 2):
        move.wait()

    def finish(section, state):
        for move in moves(stores, section, section * size - 1, size):
            move.wait()
        return state

    lax.fori_loop(1, count, finish, 0)


def edge_list(ref, low, high, x_local):
    return [(low, 0), (ref, 0), (ref, 1), (ref, x_local - 2), (ref, x_local - 1), (high, 0)]


def viscosity_plane(cells, slot, edges, warmth, warm_slot, outs, out_slot, y_local, z_cells):
    strips, rows = y_local // 8, row_numbers(z_cells)
    before, after = edges
    values = [[cells[c, slot, rows_of(s), :] for s in range(strips)] for c in range(3)]
    up = [[pltpu.roll(v, 7, 0) for v in row] for row in values]
    down = [[pltpu.roll(v, 1, 0) for v in row] for row in values]
    for s in range(strips):
        along_x, along_y, along_z = [], [], []
        for c in range(3):
            value = values[c][s]
            along_x.append(cells[c, slot + 1, rows_of(s), :] - cells[c, slot - 1, rows_of(s), :])
            ahead = jnp.where(rows == 7, up[c][s + 1] if s + 1 < strips else after(c), up[c][s])
            behind = jnp.where(rows == 0, down[c][s - 1] if s else before(c), down[c][s])
            along_y.append(ahead - behind)
            along_z.append(pltpu.roll(value, z_cells - 1, 1) - pltpu.roll(value, 1, 1))
        s_xy = along_y[0] + along_x[1]
        s_xz = along_z[0] + along_x[2]
        s_yz = along_z[1] + along_y[2]
        extra = 0.5 * (
            along_x[0] * along_x[0] + along_y[1] * along_y[1] + along_z[2] * along_z[2]
        ) + 0.25 * (s_xy * s_xy + s_xz * s_xz + s_yz * s_yz)
        rate_sq = rate_base**2 + extra
        value = jnp.exp(
            (0.5 / stress_exponent) * jnp.log(rate_sq)
            + (zener_energy / stress_exponent) * (1.0 / warmth[warm_slot, rows_of(s), :] - 1.0)
        )
        square = value * value + 1.0
        mu = jnp.log(value + square * lax.rsqrt(square)) * lax.rsqrt(rate_sq)
        outs[0][out_slot, rows_of(s), :] = mu * (scaled_mu / 3.0)
        if len(outs) > 1:
            heat = (mu * (1.0 / 3.0)) * extra
            for b in range(z_cells // 128):
                outs[1][b, out_slot, rows_of(s), :] = heat[:, b * 128 : (b + 1) * 128]


def viscosity_call(flow, y_sides, warmth, with_heat, x_sides=None, inner=None):
    _, x_local, y_local, z_cells = flow.shape
    z_blocks = z_cells // 128
    edge = x_sides is not None
    slots, made = (6, 2) if edge else (x_local, x_local - 2)
    outputs = 2 if with_heat else 1

    def kernel(*refs):
        flow_ref, before_ref, after_ref, warmth_ref = refs[:4]
        rest = list(refs[4:])
        listed = None
        if edge:
            low, high = rest[:2]
            listed = edge_list(flow_ref, low, high, x_local)
            rest = rest[2 + outputs :]
        out_refs, rest = rest[:outputs], rest[outputs:]
        cells, cell_sem, warm, warm_sem = rest[:4]
        outs, out_sems = rest[4 : 4 + outputs], rest[4 + outputs :]
        flow_planes = Planes(flow_ref, cells, cell_sem, listed)
        warm_planes = Planes(warmth_ref, warm, warm_sem)

        def plane_of(i):
            return i * (x_local - 1) if edge else i + 1

        def slot_of(i):
            return 3 * i + 1 if edge else i + 1

        def stored(k, i):
            return pltpu.make_async_copy(
                pick(outs[k], i), pick(out_refs[k], plane_of(i)), out_sems[k].at[i]
            )

        if edge:
            for slot in range(6):
                flow_planes.start(slot)
            for i in range(2):
                warm_planes.start(i, plane_of(i))
        else:
            flow_planes.start(0)
            flow_planes.start(1)

            def begin(i, state):
                flow_planes.start(i + 2)
                warm_planes.start(i, i + 1)
                return state

            lax.fori_loop(0, made, begin, 0)
            flow_planes.wait(0)
            flow_planes.wait(1)

        def body(i, state):
            slot, plane = slot_of(i), plane_of(i)
            if edge:
                flow_planes.wait(slot - 1)
                flow_planes.wait(slot)
            flow_planes.wait(slot + 1)
            warm_planes.wait(i)
            viscosity_plane(
                cells,
                slot,
                (lambda c: before_ref[c, plane], lambda c: after_ref[c, plane]),
                warm,
                i,
                outs,
                i,
                y_local,
                z_cells,
            )
            for k in range(outputs):
                stored(k, i).start()
            return state

        lax.fori_loop(0, made, body, 0)

        def finish(i, state):
            for k in range(outputs):
                stored(k, i).wait()
            return state

        lax.fori_loop(0, made, finish, 0)

    shapes = [(x_local, y_local, z_cells), (z_blocks, x_local, y_local, 128)][:outputs]
    held = [(made, y_local, z_cells), (z_blocks, made, y_local, 128)][:outputs]
    operands = [flow, *y_sides, warmth]
    specs = [anywhere, in_vmem, in_vmem, anywhere]
    aliases = {}
    if edge:
        operands += [*x_sides, *inner]
        specs += [anywhere] * (2 + outputs)
        aliases = {6 + k: k for k in range(outputs)}
    return pl.pallas_call(
        kernel,
        in_specs=specs,
        out_specs=[anywhere] * outputs,
        out_shape=[jax.ShapeDtypeStruct(shape, jnp.float32) for shape in shapes],
        input_output_aliases=aliases,
        scratch_shapes=[
            pltpu.VMEM((3, slots, y_local, z_cells), jnp.float32),
            pltpu.SemaphoreType.DMA((slots,)),
            pltpu.VMEM((made, y_local, z_cells), jnp.float32),
            pltpu.SemaphoreType.DMA((made,)),
        ]
        + [pltpu.VMEM(shape, jnp.float32) for shape in held]
        + [pltpu.SemaphoreType.DMA((made,))] * outputs,
        compiler_params=pltpu.CompilerParams(vmem_limit_bytes=vmem_limit),
        name="viscosity_edge" if edge else "viscosity_inner",
    )(*operands)


def viscosity_inner(flow, y_sides, warmth, with_heat):
    _, x_local, y_local, z_cells = flow.shape
    z_blocks, size = z_cells // 128, 4
    outputs = 2 if with_heat else 1

    def kernel(flow_ref, before_ref, after_ref, warmth_ref, *rest):
        out_refs, (cells, cell_sem, warm, warm_sem, *heat) = rest[:outputs], rest[outputs:]
        outs = [out_refs[0]] + heat[:1]

        def body(slot, state):
            viscosity_plane(
                cells,
                slot,
                (lambda c: before_ref[c, slot], lambda c: after_ref[c, slot]),
                warm,
                slot,
                outs,
                slot,
                y_local,
                z_cells,
            )
            return state

        in_sections(
            x_local,
            size,
            [(flow_ref, cells, cell_sem), (warmth_ref, warm, warm_sem)],
            [(heat[0], out_refs[1], heat[1])] if with_heat else [],
            lambda: None,
            body,
        )

    shapes = [(x_local, y_local, z_cells), (z_blocks, x_local, y_local, 128)][:outputs]
    sems = pltpu.SemaphoreType.DMA((x_local // size,))
    return pl.pallas_call(
        kernel,
        in_specs=[anywhere, in_vmem, in_vmem, anywhere],
        out_specs=[in_vmem, anywhere][:outputs],
        out_shape=[jax.ShapeDtypeStruct(shape, jnp.float32) for shape in shapes],
        scratch_shapes=[
            pltpu.VMEM(flow.shape, jnp.float32),
            sems,
            pltpu.VMEM(warmth.shape, jnp.float32),
            sems,
        ]
        + ([pltpu.VMEM(shapes[1], jnp.float32), sems] if with_heat else []),
        compiler_params=pltpu.CompilerParams(vmem_limit_bytes=vmem_limit),
        name="viscosity_inner",
    )(flow, *y_sides, warmth)


vmem_limit = 48 << 20


def advance_plane(cells, mu, slot, edges, push, out_slot, flux, y_local, z_cells):
    strips, rows = y_local // 8, row_numbers(z_cells)
    flow_before, flow_after, mu_before, mu_after = edges
    m = [mu[slot, rows_of(s), :] for s in range(strips)]
    m_up = [pltpu.roll(v, 7, 0) for v in m]
    sums_y = [
        m[s] + jnp.where(rows == 7, m_up[s + 1] if s + 1 < strips else mu_after(), m_up[s])
        for s in range(strips)
    ]
    first_sum = mu_before() + mu[slot, pl.ds(0, 1), :]
    values = [[cells[c, slot, rows_of(s), :] for s in range(strips)] for c in range(3)]
    up = [[pltpu.roll(v, 7, 0) for v in row] for row in values]
    carried = [
        first_sum * (cells[c, slot, pl.ds(0, 1), :] - flow_before(c)) for c in range(3)
    ]
    for s in range(strips):
        sum_x = m[s] + mu[slot + 1, rows_of(s), :]
        sum_z_ahead = m[s] + pltpu.roll(m[s], z_cells - 1, 1)
        sum_z_behind = m[s] + pltpu.roll(m[s], 1, 1)
        for c in range(3):
            value = values[c][s]
            flux_x = sum_x * (cells[c, slot + 1, rows_of(s), :] - value)
            ahead = jnp.where(
                rows == 7, up[c][s + 1] if s + 1 < strips else flow_after(c), up[c][s]
            )
            flux_y = sums_y[s] * (ahead - value)
            turned = pltpu.roll(flux_y, 1, 0)
            total = (flux_x - flux[c, rows_of(s), :]) + (
                flux_y - jnp.where(rows == 0, carried[c], turned)
            ) + (
                sum_z_ahead * (pltpu.roll(value, z_cells - 1, 1) - value)
                - sum_z_behind * (value - pltpu.roll(value, 1, 1))
            )
            flux[c, rows_of(s), :] = flux_x
            carried[c] = turned
            push[c, out_slot, rows_of(s), :] = (
                value + time_step * push[c, out_slot, rows_of(s), :] + total
            )


def first_flux(cells, mu, slot, flux, y_local):
    for s in range(y_local // 8):
        sum_x = mu[slot - 1, rows_of(s), :] + mu[slot, rows_of(s), :]
        for c in range(3):
            flux[c, rows_of(s), :] = sum_x * (
                cells[c, slot, rows_of(s), :] - cells[c, slot - 1, rows_of(s), :]
            )


def advance_call(flow, flow_y, mu, mu_y, push, flow_x=None, mu_x=None, inner=None):
    _, x_local, y_local, z_cells = flow.shape
    edge = flow_x is not None
    slots, made = (6, 2) if edge else (x_local, x_local - 2)

    def kernel(*refs):
        flow_ref, flow_before, flow_after, mu_ref, mu_before, mu_after, push_ref = refs[:7]
        rest = refs[7:]
        flow_listed = mu_listed = None
        if edge:
            flow_listed = edge_list(flow_ref, rest[0], rest[1], x_local)
            mu_listed = edge_list(mu_ref, rest[2], rest[3], x_local)
            rest = rest[5:]
        out_ref, cells, cell_sem, mu_cells, mu_sem, work, work_sem, out_sem, flux = rest
        flow_planes = Planes(flow_ref, cells, cell_sem, flow_listed)
        mu_planes = Planes(mu_ref, mu_cells, mu_sem, mu_listed)
        push_planes = Planes(push_ref, work, work_sem)

        def plane_of(i):
            return i * (x_local - 1) if edge else i + 1

        def stored(i):
            return pltpu.make_async_copy(
                pick(work, i), pick(out_ref, plane_of(i)), out_sem.at[i]
            )

        if edge:
            for slot in range(6):
                flow_planes.start(slot)
                mu_planes.start(slot)
            for i in range(2):
                push_planes.start(i, plane_of(i))
        else:
            for slot in range(2):
                flow_planes.start(slot)
                mu_planes.start(slot)

            def begin(i, state):
                flow_planes.start(i + 2)
                mu_planes.start(i + 2)
                push_planes.start(i, i + 1)
                return state

            lax.fori_loop(0, made, begin, 0)
            for slot in range(2):
                flow_planes.wait(slot)
                mu_planes.wait(slot)
            first_flux(cells, mu_cells, 1, flux, y_local)

        def body(i, state):
            slot, plane = (3 * i + 1 if edge else i + 1), plane_of(i)
            if edge:
                for back in range(2):
                    flow_planes.wait(slot - back)
                    mu_planes.wait(slot - back)
                first_flux(cells, mu_cells, slot, flux, y_local)
            flow_planes.wait(slot + 1)
            mu_planes.wait(slot + 1)
            push_planes.wait(i)
            advance_plane(
                cells,
                mu_cells,
                slot,
                (
                    lambda c: flow_before[c, plane],
                    lambda c: flow_after[c, plane],
                    lambda: mu_before[plane],
                    lambda: mu_after[plane],
                ),
                work,
                i,
                flux,
                y_local,
                z_cells,
            )
            stored(i).start()
            return state

        lax.fori_loop(0, made, body, 0)

        def finish(i, state):
            stored(i).wait()
            return state

        lax.fori_loop(0, made, finish, 0)

    operands = [flow, *flow_y, mu, *mu_y, push]
    specs = [anywhere, in_vmem, in_vmem, anywhere, in_vmem, in_vmem, anywhere]
    aliases = {}
    if edge:
        operands += [*flow_x, *mu_x, inner]
        specs += [anywhere] * 5
        aliases = {11: 0}
    return pl.pallas_call(
        kernel,
        in_specs=specs,
        out_specs=anywhere,
        out_shape=jax.ShapeDtypeStruct(flow.shape, jnp.float32),
        input_output_aliases=aliases,
        scratch_shapes=[
            pltpu.VMEM((3, slots, y_local, z_cells), jnp.float32),
            pltpu.SemaphoreType.DMA((slots,)),
            pltpu.VMEM((slots, y_local, z_cells), jnp.float32),
            pltpu.SemaphoreType.DMA((slots,)),
            pltpu.VMEM((3, made, y_local, z_cells), jnp.float32),
            pltpu.SemaphoreType.DMA((made,)),
            pltpu.SemaphoreType.DMA((made,)),
            pltpu.VMEM((3, y_local, z_cells), jnp.float32),
        ],
        compiler_params=pltpu.CompilerParams(vmem_limit_bytes=vmem_limit),
        name="advance_edge" if edge else "advance_inner",
    )(*operands)


def advance_inner(flow, flow_y, mu, mu_y, push):
    _, x_local, y_local, z_cells = flow.shape
    size = 4

    def kernel(
        flow_ref, flow_before, flow_after, mu_ref, mu_before, mu_after, push_ref,
        out_ref, cells, cell_sem, work, work_sem, out_sem, flux,
    ):
        def body(slot, state):
            advance_plane(
                cells,
                mu_ref,
                slot,
                (
                    lambda c: flow_before[c, slot],
                    lambda c: flow_after[c, slot],
                    lambda: mu_before[slot],
                    lambda: mu_after[slot],
                ),
                work,
                slot,
                flux,
                y_local,
                z_cells,
            )
            return state

        in_sections(
            x_local,
            size,
            [(flow_ref, cells, cell_sem), (push_ref, work, work_sem)],
            [(work, out_ref, out_sem)],
            lambda: first_flux(cells, mu_ref, 1, flux, y_local),
            body,
        )

    sems = pltpu.SemaphoreType.DMA((x_local // size,))
    return pl.pallas_call(
        kernel,
        in_specs=[anywhere, in_vmem, in_vmem, in_vmem, in_vmem, in_vmem, anywhere],
        out_specs=anywhere,
        out_shape=jax.ShapeDtypeStruct(flow.shape, jnp.float32),
        scratch_shapes=[
            pltpu.VMEM(flow.shape, jnp.float32),
            sems,
            pltpu.VMEM(flow.shape, jnp.float32),
            sems,
            sems,
            pltpu.VMEM((3, y_local, z_cells), jnp.float32),
        ],
        compiler_params=pltpu.CompilerParams(vmem_limit_bytes=vmem_limit),
        name="advance_inner",
    )(flow, *flow_y, mu, *mu_y, push)


def cosine_sine_basis(points, period, waves):
    columns, eigen = [], []
    for wave in waves:
        angle = 2.0 * np.pi * ((wave * np.arange(points)) % period) / period
        single = wave % period == 0 or 2 * wave == period
        size = math.sqrt((1.0 if single else 2.0) / period)
        columns.append(np.cos(angle) * size)
        eigen.append(math.sin(2.0 * math.pi * wave / period) ** 2)
        if not single:
            columns.append(np.sin(angle) * size)
            eigen.append(eigen[-1])
    return np.stack(columns, 1), np.array(eigen)


def halves(table):
    table = np.asarray(table, np.float32)
    high = table.astype(jnp.bfloat16)
    low = (table - high.astype(np.float32)).astype(jnp.bfloat16)
    return jnp.asarray(high), jnp.asarray(low)


def split(value):
    high = value.astype(jnp.bfloat16)
    return high, (value - high.astype(jnp.float32)).astype(jnp.bfloat16)


def triple_product(left, right):
    def product(one, two):
        return lax.dot_general(
            one, two, (((1,), (0,)), ((), ())), preferred_element_type=jnp.float32
        )

    return product(left[0], right[0]) + (product(left[0], right[1]) + product(left[1], right[0]))


def z_tables(z_cells):
    half = z_cells // 2
    even, eigen_even = cosine_sine_basis(half, z_cells, range(0, half + 1, 2))
    odd, eigen_odd = cosine_sine_basis(half, z_cells, range(1, half, 2))
    return even, odd, np.concatenate([eigen_even, eigen_odd])


def modes_of(lines, even_high, even_low, odd_high, odd_low):
    half = lines.shape[1] // 2
    first, second = lines[:, :half], lines[:, half:]
    return jnp.concatenate(
        [
            triple_product(split(first + second), (even_high[...], even_low[...])),
            triple_product(split(first - second), (odd_high[...], odd_low[...])),
        ],
        1,
    )


def cells_of(modes, even_high, even_low, odd_high, odd_low):
    half = modes.shape[1] // 2
    first = triple_product(split(modes[:, :half]), (even_high[...], even_low[...]))
    second = triple_product(split(modes[:, half:]), (odd_high[...], odd_low[...]))
    return jnp.concatenate([first + second, first - second], 1)


def divergence_modes(flow, count):
    _, x_local, y_local, z_cells = flow.shape
    piece, strips = z_cells // count, y_local // 8
    step = min(8, x_local)
    even, odd, _ = z_tables(z_cells)
    tables = halves(even) + halves(odd)

    def kernel(
        flow_ref, even_high, even_low, odd_high, odd_low, out_ref,
        cells, semaphores, work, made, out_sem,
    ):
        planes = Planes(flow_ref, cells, semaphores)
        rows = row_numbers(z_cells)

        def begin(i, state):
            planes.start(i)
            return state

        lax.fori_loop(0, x_local, begin, 0)
        planes.wait(0)

        def stored(k):
            part = pl.ds(k * step, step)
            return pltpu.make_async_copy(made.at[:, part], out_ref.at[:, part], out_sem.at[k])

        def group(k, state):
            def plane(i, state):
                j = k * step + i

                @pl.when(j + 1 < x_local)
                def _():
                    planes.wait(j + 1)

                nearer = jnp.where(j > 0, 0.5, 0.0)
                further = jnp.where(j + 1 < x_local, 0.5, 0.0)
                last, following = jnp.maximum(j - 1, 0), jnp.minimum(j + 1, x_local - 1)
                across = [cells[1, j, rows_of(s), :] for s in range(strips)]
                up = [pltpu.roll(v, 7, 0) for v in across]
                down = [pltpu.roll(v, 1, 0) for v in across]
                for s in range(strips):
                    ahead = jnp.where(rows == 7, up[s + 1] if s + 1 < strips else 0.0, up[s])
                    behind = jnp.where(rows == 0, down[s - 1] if s else 0.0, down[s])
                    along = cells[2, j, rows_of(s), :]
                    work[i, rows_of(s), :] = (
                        further * cells[0, following, rows_of(s), :]
                        - nearer * cells[0, last, rows_of(s), :]
                    ) + 0.5 * (
                        (ahead - behind)
                        + (pltpu.roll(along, z_cells - 1, 1) - pltpu.roll(along, 1, 1))
                    )
                return state

            lax.fori_loop(0, step, plane, 0)
            modes = modes_of(
                work[...].reshape(step * y_local, z_cells), even_high, even_low, odd_high, odd_low
            )
            for n in range(count):
                made[n, pl.ds(k * step, step)] = modes[:, n * piece : (n + 1) * piece].reshape(
                    step, y_local, piece
                )
            stored(k).start()
            return state

        groups = x_local // step
        lax.fori_loop(0, groups, group, 0)
        for k in range(groups):
            stored(k).wait()

    return pl.pallas_call(
        kernel,
        in_specs=[anywhere] + [in_vmem] * 4,
        out_specs=anywhere,
        out_shape=jax.ShapeDtypeStruct((count, x_local, y_local, piece), jnp.float32),
        scratch_shapes=[
            pltpu.VMEM((3, x_local, y_local, z_cells), jnp.float32),
            pltpu.SemaphoreType.DMA((x_local,)),
            pltpu.VMEM((step, y_local, z_cells), jnp.float32),
            pltpu.VMEM((count, x_local, y_local, piece), jnp.float32),
            pltpu.SemaphoreType.DMA((x_local // step,)),
        ],
        name="divergence_modes",
    )(flow, *tables)


def add_halo_modes(modes, x_sides, y_sides):
    count, x_local, y_local, piece = modes.shape
    z_cells = count * piece
    even, odd, _ = z_tables(z_cells)
    tables = halves(even) + halves(odd)

    def kernel(
        modes_ref, low_ref, high_ref, before_ref, after_ref,
        even_high, even_low, odd_high, odd_low, out_ref, ends, lines, semaphores,
    ):
        def moves(back):
            pairs = [
                (ends.at[k], modes_ref.at[:, plane])
                for k, plane in enumerate((0, x_local - 1))
            ] + [
                (lines.at[k], modes_ref.at[:, 1 : x_local - 1, 8 * s : 8 * s + 8])
                for k, s in enumerate((0, y_local // 8 - 1))
            ]
            if back:
                pairs = [
                    (ends.at[k], out_ref.at[:, plane])
                    for k, plane in enumerate((0, x_local - 1))
                ] + [
                    (lines.at[k], out_ref.at[:, 1 : x_local - 1, 8 * s : 8 * s + 8])
                    for k, s in enumerate((0, y_local // 8 - 1))
                ]
                return [
                    pltpu.make_async_copy(here, there, semaphores.at[4 + i])
                    for i, (here, there) in enumerate(pairs)
                ]
            return [
                pltpu.make_async_copy(there, here, semaphores.at[i])
                for i, (here, there) in enumerate(pairs)
            ]

        loads, stores = moves(False), moves(True)
        for load in loads:
            load.start()
        added = modes_of(
            jnp.concatenate(
                [-0.5 * low_ref[0], 0.5 * high_ref[0], -0.5 * before_ref[...], 0.5 * after_ref[...]],
                0,
            ),
            even_high,
            even_low,
            odd_high,
            odd_low,
        )
        for load in loads:
            load.wait()
        rows = row_numbers(piece)
        for n in range(count):
            block = added[:, n * piece : (n + 1) * piece]
            side = [block[2 * y_local + k * x_local :][:x_local] for k in range(2)]
            for k, plane in enumerate((0, x_local - 1)):
                ends[k, n] = ends[k, n] + block[k * y_local : (k + 1) * y_local]
                for j, (strip, row) in enumerate(((0, 0), (y_local // 8 - 1, 7))):
                    part = pl.ds(8 * strip, 8)
                    ends[k, n, part, :] = ends[k, n, part, :] + jnp.where(
                        rows == row, side[j][plane : plane + 1], 0.0
                    )
            for j, row in enumerate((0, 7)):
                for x in range(1, x_local - 1):
                    lines[j, n, x - 1] = lines[j, n, x - 1] + jnp.where(
                        rows == row, side[j][x : x + 1], 0.0
                    )
        for store in stores:
            store.start()
        for store in stores:
            store.wait()

    return pl.pallas_call(
        kernel,
        in_specs=[anywhere] + [in_vmem] * 8,
        out_specs=anywhere,
        out_shape=jax.ShapeDtypeStruct(modes.shape, jnp.float32),
        input_output_aliases={0: 0},
        scratch_shapes=[
            pltpu.VMEM((2, count, y_local, piece), jnp.float32),
            pltpu.VMEM((2, count, x_local - 2, 8, piece), jnp.float32),
            pltpu.SemaphoreType.DMA((8,)),
        ],
        name="add_halo_modes",
    )(modes, *x_sides, *y_sides, *tables)


def corrected(flow, spectrum, y_sides):
    count, planes, y_local, piece = spectrum.shape
    x_local, z_cells = planes - 2, count * piece
    strips, part = y_local // 8, planes // 2
    even, odd, _ = z_tables(z_cells)
    tables = halves(even.T) + halves(odd.T)

    def kernel(
        flow_ref, in_ref, before_ref, after_ref,
        even_high, even_low, odd_high, odd_low, out_ref,
        modes, mode_sem, pressure, sides, work, flow_sem, out_sem,
    ):
        flow_planes = Planes(flow_ref, work, flow_sem)
        table_refs = (even_high, even_low, odd_high, odd_low)

        def load(k):
            span = pl.ds(k * part, part)
            return pltpu.make_async_copy(in_ref.at[:, span], modes.at[:, span], mode_sem.at[k])

        load(0).start()
        load(1).start()

        def begin(i, state):
            flow_planes.start(i)
            return state

        lax.fori_loop(0, x_local, begin, 0)
        sides[...] = cells_of(
            jnp.concatenate(
                [
                    jnp.concatenate([ref[n] for n in range(count)], 1)
                    for ref in (before_ref, after_ref)
                ],
                0,
            ),
            *table_refs,
        )
        rows = row_numbers(z_cells)

        def stored(i):
            return pltpu.make_async_copy(pick(work, i), pick(out_ref, i), out_sem.at[i])

        def plane(j, state):
            flow_planes.wait(j)
            values = [pressure[j + 1, rows_of(s), :] for s in range(strips)]
            up = [pltpu.roll(v, 7, 0) for v in values]
            down = [pltpu.roll(v, 1, 0) for v in values]
            for s in range(strips):
                ahead = up[s + 1] if s + 1 < strips else sides[pl.ds(x_local + j, 1), :]
                behind = down[s - 1] if s else sides[pl.ds(j, 1), :]
                slopes = (
                    pressure[j + 2, rows_of(s), :] - pressure[j, rows_of(s), :],
                    jnp.where(rows == 7, ahead, up[s]) - jnp.where(rows == 0, behind, down[s]),
                    pltpu.roll(values[s], z_cells - 1, 1) - pltpu.roll(values[s], 1, 1),
                )
                for c in range(3):
                    work[c, j, rows_of(s), :] = work[c, j, rows_of(s), :] - 0.5 * slopes[c]
            stored(j).start()
            return state

        for k in range(2):
            load(k).wait()
            span = pl.ds(k * part, part)
            pressure[span] = cells_of(
                jnp.concatenate(
                    [modes[n, span].reshape(part * y_local, piece) for n in range(count)], 1
                ),
                *table_refs,
            ).reshape(part, y_local, z_cells)
            lax.fori_loop(k * (part - 2), (part - 2) if k == 0 else x_local, plane, 0)

        def finish(i, state):
            stored(i).wait()
            return state

        lax.fori_loop(0, x_local, finish, 0)

    return pl.pallas_call(
        kernel,
        in_specs=[anywhere, anywhere] + [in_vmem] * 6,
        out_specs=anywhere,
        out_shape=jax.ShapeDtypeStruct(flow.shape, jnp.float32),
        scratch_shapes=[
            pltpu.VMEM(spectrum.shape, jnp.float32),
            pltpu.SemaphoreType.DMA((2,)),
            pltpu.VMEM((planes, y_local, z_cells), jnp.float32),
            pltpu.VMEM((2 * x_local, z_cells), jnp.float32),
            pltpu.VMEM(flow.shape, jnp.float32),
            pltpu.SemaphoreType.DMA((x_local,)),
            pltpu.SemaphoreType.DMA((x_local,)),
        ],
        compiler_params=pltpu.CompilerParams(vmem_limit_bytes=vmem_limit),
        name="corrected",
    )(flow, spectrum, *y_sides, *tables)


def y_forward(spectrum, ratio, wide_count):
    count, x_local, y_local, piece = spectrum.shape
    y_cells = count * y_local
    share, group = y_cells // wide_count, max(2, x_local // 4)
    table, _ = cosine_sine_basis(y_cells, y_cells, range(y_cells // 2 + 1))
    tables = halves(table.T)

    def kernel(
        in_ref, high_ref, low_ref, ratio_ref, modes_ref, carry_ref,
        lines, in_sems, made, out_sems, sums, power,
    ):
        def load(k):
            part = pl.ds(k * group, group)
            return pltpu.make_async_copy(in_ref.at[:, part], lines.at[:, part], in_sems.at[k])

        def stored(k):
            part = pl.ds(k * group, group)
            return pltpu.make_async_copy(made.at[part], modes_ref.at[part], out_sems.at[k])

        for k in range(x_local // group):
            load(k).start()
        sums[...] = jnp.zeros_like(sums)
        power[...] = jnp.ones_like(power)

        def body(t, state):
            planes = [
                jnp.concatenate([lines[n, 2 * t + side] for n in range(count)], 0)
                for side in range(2)
            ]
            modes = triple_product(
                (high_ref[...], low_ref[...]), split(jnp.concatenate(planes, 1))
            )
            r, pw = ratio_ref[...], power[...]
            for side in range(2):
                plane = modes[:, side * piece : (side + 1) * piece]
                made[2 * t + side] = plane
                sums[side] = plane + r * sums[side]
                sums[2 + side] = sums[2 + side] + pw * plane
            power[...] = pw * r
            return state

        def section(k, state):
            load(k).wait()
            lax.fori_loop(k * (group // 2), (k + 1) * (group // 2), body, 0)
            stored(k).start()
            return state

        lax.fori_loop(0, x_local // group, section, 0)
        for kind in range(4):
            carry_ref[:, kind] = sums[kind].reshape(wide_count, share, piece)
        for k in range(x_local // group):
            stored(k).wait()

    return pl.pallas_call(
        kernel,
        in_specs=[anywhere] + [in_vmem] * 3,
        out_specs=[anywhere, in_vmem],
        out_shape=[
            jax.ShapeDtypeStruct((x_local, y_cells, piece), jnp.float32),
            jax.ShapeDtypeStruct((wide_count, 4, share, piece), jnp.float32),
        ],
        scratch_shapes=[
            pltpu.VMEM(spectrum.shape, jnp.float32),
            pltpu.SemaphoreType.DMA((x_local // group,)),
            pltpu.VMEM((x_local, y_cells, piece), jnp.float32),
            pltpu.SemaphoreType.DMA((x_local // group,)),
            pltpu.VMEM((4, y_cells, piece), jnp.float32),
            pltpu.VMEM((y_cells, piece), jnp.float32),
        ],
        name="y_forward",
    )(spectrum, *tables, ratio)


def power_of(value, exponent):
    result = None
    while exponent:
        if exponent & 1:
            result = value if result is None else result * value
        value = value * value
        exponent >>= 1
    return result


def join_carries(carries, ratio, block):
    count, kinds, _, _ = carries.shape

    def kernel(in_ref, ratio_ref, out_ref):
        step = power_of(ratio_ref[...], block)
        scale = 1.0 / (1.0 - power_of(step, count))
        for kind in range(kinds):
            order = list(range(count)) if kind < 2 else list(range(count))[::-1]
            total = in_ref[order[0], kind]
            for w in order[1:]:
                total = in_ref[w, kind] + step * total
            total = total * scale
            for w in order:
                out_ref[w, kind] = total
                total = in_ref[w, kind] + step * total

    return pl.pallas_call(
        kernel,
        in_specs=[in_vmem] * 2,
        out_specs=in_vmem,
        out_shape=jax.ShapeDtypeStruct(carries.shape, jnp.float32),
        compiler_params=pltpu.CompilerParams(vmem_limit_bytes=vmem_limit),
        name="join_carries",
    )(carries, ratio)


def y_inverse(modes, carries, ratio, gain, count):
    x_local, y_cells, piece = modes.shape
    y_local, pairs, group = y_cells // count, x_local // 2, max(2, x_local // 4)
    table, _ = cosine_sine_basis(y_cells, y_cells, range(y_cells // 2 + 1))
    tables = halves(table)

    def kernel(
        modes_in, carry_ref, high_ref, low_ref, ratio_ref, gain_ref, out_ref,
        planes, in_sems, behind, state, cells, out_sems,
    ):
        def load(k):
            part = pl.ds(k * group, group)
            return pltpu.make_async_copy(modes_in.at[part], planes.at[part], in_sems.at[k])

        def stored(t):
            part = pl.ds(2 * t, 2)
            return pltpu.make_async_copy(cells.at[:, part], out_ref.at[:, part], out_sems.at[t])

        def carry(kind):
            return carry_ref[:, kind].reshape(y_cells, piece)

        groups = x_local // group
        for k in range(groups)[::-1]:
            load(k).start()
        for kind in range(4):
            state[kind] = carry(kind)
        behind[x_local + 1] = carry(2)

        def back(i, done):
            m = pairs - 1 - i
            r = ratio_ref[...]
            for side in range(2):
                value = r * state[2 + side]
                behind[2 * m + 1 + side] = value
                state[2 + side] = planes[2 * m + side] + value
            return done

        def back_section(k, done):
            load(groups - 1 - k).wait()
            lax.fori_loop(k * (group // 2), (k + 1) * (group // 2), back, 0)
            return done

        lax.fori_loop(0, groups, back_section, 0)
        behind[0] = ratio_ref[...] * state[3]

        def body(t, done):
            r, gain_value = ratio_ref[...], gain_ref[...]
            even_plane = planes[jnp.minimum(2 * t, x_local - 2)]
            odd_plane = planes[jnp.maximum(2 * t - 1, 1)]
            even = r * state[0] + jnp.where(t < pairs, even_plane, 0.0)
            odd = jnp.where(t > 0, odd_plane + r * state[1], state[1])
            state[0] = even
            state[1] = odd
            joined = jnp.concatenate(
                [gain_value * (odd + behind[2 * t]), gain_value * (even + behind[2 * t + 1])], 1
            )
            result = triple_product((high_ref[...], low_ref[...]), split(joined))
            for n in range(count):
                for side in range(2):
                    cells[n, 2 * t + side] = result[
                        n * y_local : (n + 1) * y_local, side * piece : (side + 1) * piece
                    ]
            stored(t).start()
            return done

        lax.fori_loop(0, pairs + 1, body, 0)

        def finish(t, done):
            stored(t).wait()
            return done

        lax.fori_loop(0, pairs + 1, finish, 0)

    made = (count, x_local + 2, y_local, piece)
    return pl.pallas_call(
        kernel,
        in_specs=[anywhere] + [in_vmem] * 5,
        out_specs=anywhere,
        out_shape=jax.ShapeDtypeStruct(made, jnp.float32),
        scratch_shapes=[
            pltpu.VMEM(modes.shape, jnp.float32),
            pltpu.SemaphoreType.DMA((x_local // group,)),
            pltpu.VMEM((x_local + 2, y_cells, piece), jnp.float32),
            pltpu.VMEM((4, y_cells, piece), jnp.float32),
            pltpu.VMEM(made, jnp.float32),
            pltpu.SemaphoreType.DMA((pairs + 1,)),
        ],
        name="y_inverse",
    )(modes, carries, *tables, ratio, gain)


def turn(value, axis):
    return lax.all_to_all(value, axis, split_axis=0, concat_axis=0, tiled=True)


def project(spectrum):
    count, x_local, y_local, piece = spectrum.shape
    y_cells, z_cells = count * y_local, count * piece
    wide_count = lax.axis_size("wide")
    _, eigen_y = cosine_sine_basis(y_cells, y_cells, range(y_cells // 2 + 1))
    eigen_z = jnp.asarray(z_tables(z_cells)[2], jnp.float32)
    own_z = lax.dynamic_slice_in_dim(eigen_z, lax.axis_index("narrow") * piece, piece)
    excess = 4.0 * (jnp.asarray(eigen_y, jnp.float32)[:, None] + own_z[None, :] + penalty)
    root = jnp.sqrt(excess * (4.0 + excess))
    ratio = 2.0 / (2.0 + excess + root)
    gain = -4.0 / root
    share = y_cells // wide_count
    own_ratio = lax.dynamic_slice_in_dim(ratio, lax.axis_index("wide") * share, share)
    modes, carries = y_forward(turn(spectrum, "narrow"), ratio, wide_count)
    carries = turn(join_carries(turn(carries, "wide"), own_ratio, x_local // 2), "wide")
    return turn(y_inverse(modes, carries, ratio, gain, count), "narrow")


def conduct(profile, spread):
    sides = (("wide", 0), ("narrow", 1))
    spread = with_halo(spread, sides, STEPS - 1, False)
    profile = with_halo(profile, sides, STEPS, False)
    for _ in range(STEPS):
        center = profile[1:-1, 1:-1]
        near = (
            profile[2:, 1:-1] + profile[:-2, 1:-1] + profile[1:-1, 2:] + profile[1:-1, :-2]
        )
        ahead = jnp.pad(center[:, :, 1:], ((0, 0), (0, 0), (0, 1)))
        behind = jnp.pad(center[:, :, :-1], ((0, 0), (0, 0), (1, 0)))
        profile = center + spread * (near + ahead + behind - 6.0 * center)
        spread = spread[1:-1, 1:-1]
    return profile


def both_rings(value, dim):
    y_sides = ring(value, "narrow", dim + 1)
    x_sides = ring(value, "wide", dim)
    return x_sides, y_sides


def device_step(
    material_flow_vector,
    tool_push_density,
    tool_warmth_excess,
    substrate_warmth_excess,
    spread_coefficient,
    source_owner_sheet,
    source_part_line,
):
    flow = material_flow_vector
    flow_x, flow_y = both_rings(flow, 1)
    current, current_x, current_y = flow, flow_x, flow_y
    for section in range(PASSES):
        last = section + 1 == PASSES
        inner = viscosity_inner(current, current_y, tool_warmth_excess, last)
        fields = viscosity_call(current, current_y, tool_warmth_excess, last, current_x, inner)
        mu = fields[0]
        mu_x, mu_y = both_rings(mu, 0)
        inner = advance_inner(flow, flow_y, mu, mu_y, tool_push_density)
        current = advance_call(flow, flow_y, mu, mu_y, tool_push_density, flow_x, mu_x, inner)
        if not last:
            current_x, current_y = both_rings(current, 1)
    heat_cells = fields[1]
    end_x = ring(current[0], "wide", 0)
    y_local = flow.shape[2]
    end_y = [
        shift(current[1, :, y_local - 1 :], "narrow", 1)[:, 0],
        shift(current[1, :, :1], "narrow", -1)[:, 0],
    ]
    modes = divergence_modes(current, lax.axis_size("narrow"))
    spectrum = project(add_halo_modes(modes, end_x, end_y))
    inner = spectrum[:, 1:-1]
    corrected_flow_vector = corrected(
        current, spectrum, [side[:, :, 0] for side in ring(inner, "narrow", 2)]
    )
    z_blocks = heat_cells.shape[0]
    slab_count = lax.axis_size("wide")
    component_lines = substrate_warmth_excess.shape[0] * substrate_warmth_excess.shape[1]
    targets = source_owner_sheet[:, 0] * component_lines + source_part_line
    partial_value = (
        jnp.zeros((slab_count * component_lines, 128), jnp.float32)
        .at[targets.reshape(-1, z_blocks).T.reshape(-1)]
        .add(heat_cells.reshape(-1, 128))
    )
    substrate_energy_input = lax.psum_scatter(
        partial_value.reshape(slab_count, component_lines, 128),
        "wide",
        scatter_dimension=0,
        tiled=True,
    )
    thermal_profile = substrate_warmth_excess + dissipation_factor * substrate_energy_input.reshape(
        substrate_warmth_excess.shape
    )
    return (corrected_flow_vector, conduct(thermal_profile, spread_coefficient))


def solution(mesh):
    return jax.shard_map(
        device_step,
        mesh=mesh,
        in_specs=(
            P(None, "wide", "narrow", None),
            P(None, "wide", "narrow", None),
            P("wide", "narrow", None),
            P("wide", "narrow", None),
            P("wide", "narrow", None),
            P(("wide", "narrow"), None),
            P(("wide", "narrow")),
        ),
        out_specs=(P(None, "wide", "narrow", None), P("wide", "narrow", None)),
        check_vma=False,
    )
```

```python
import math

import jax
import jax.numpy as jnp
import numpy as np
from jax import lax
from jax.experimental import pallas as pl
from jax.experimental.pallas import tpu as pltpu
from jax.sharding import PartitionSpec as P


PASSES = 2
STEPS = 3


time_step = 0.15
rate_base = 0.5
zener_energy = 4.0
stress_exponent = 5.0
penalty = 0.001
dissipation_factor = 0.1


def with_halo(x, sides, width, wrap):
    for axis, dim in sides:
        size, length = (lax.axis_size(axis), x.shape[dim])
        up = [(i, (i + 1) % size) for i in range(size if wrap else size - 1)]
        down = [(j, i) for i, j in up]
        last = lax.slice_in_dim(x, length - width, length, axis=dim)
        initial = lax.slice_in_dim(x, 0, width, axis=dim)
        before = lax.ppermute(last, axis, up)
        after = lax.ppermute(initial, axis, down)
        x = jnp.concatenate([before, x, after], axis=dim)
    return x


def shift(value, axis, by):
    size = lax.axis_size(axis)
    return lax.ppermute(value, axis, [(i, (i + by) % size) for i in range(size)])


def ring(value, axis, dim):
    length = value.shape[dim]
    last = lax.slice_in_dim(value, length - 1, length, axis=dim)
    initial = lax.slice_in_dim(value, 0, 1, axis=dim)
    return shift(last, axis, 1), shift(initial, axis, -1)


anywhere = pl.BlockSpec(memory_space=pl.ANY)
in_vmem = pl.BlockSpec(memory_space=pltpu.VMEM)
scaled_mu = 0.5 * time_step


def row_numbers(width):
    return lax.broadcasted_iota(jnp.int32, (8, width), 0)


def rows_of(strip):
    return pl.ds(8 * strip, 8)


def pick(ref, index):
    return ref.at[:, index] if len(ref.shape) == 4 else ref.at[index]


class Planes:
    def __init__(self, source, target, semaphores, listed=None):
        self.source, self.target, self.semaphores = source, target, semaphores
        self.listed = listed

    def copy(self, slot, ref, plane):
        return pltpu.make_async_copy(
            pick(ref, plane), pick(self.target, slot), self.semaphores.at[slot]
        )

    def start(self, slot, plane=None):
        if self.listed is None:
            self.copy(slot, self.source, slot if plane is None else plane).start()
        else:
            self.copy(slot, *self.listed[slot]).start()

    def wait(self, slot):
        self.copy(slot, self.source, 0).wait()


def in_sections(x_local, size, loads, stores, start_up, body):
    count = x_local // size

    def cut(ref, first, planes):
        part = pl.ds(first, planes)
        return ref.at[:, part] if len(ref.shape) == 4 else ref.at[part]

    def moves(kinds, section, first, planes):
        return [
            pltpu.make_async_copy(
                cut(source, first, planes), cut(target, first, planes), semaphores.at[section]
            )
            for source, target, semaphores in kinds
        ]

    def begin(section, state):
        for move in moves(loads, section, section * size, size):
            move.start()
        return state

    lax.fori_loop(0, count, begin, 0)

    def work(section, first, planes):
        for move in moves(loads, section, section * size, size):
            move.wait()
        if isinstance(first, int):
            start_up()
        lax.fori_loop(first, first + planes, body, 0)
        for move in moves(stores, section, first, planes):
            move.start()

    work(0, 1, size - 2)

    def rest(section, state):
        work(section, section * size - 1, size)
        return state

    lax.fori_loop(1, count, rest, 0)
    for move in moves(stores, 0, 1, size - 2):
        move.wait()

    def finish(section, state):
        for move in moves(stores, section, section * size - 1, size):
            move.wait()
        return state

    lax.fori_loop(1, count, finish, 0)


def edge_list(ref, low, high, x_local):
    return [(low, 0), (ref, 0), (ref, 1), (ref, x_local - 2), (ref, x_local - 1), (high, 0)]


def viscosity_plane(cells, slot, edges, warmth, warm_slot, outs, out_slot, y_local, z_cells):
    strips, rows = y_local // 8, row_numbers(z_cells)
    before, after = edges
    values = [[cells[c, slot, rows_of(s), :] for s in range(strips)] for c in range(3)]
    up = [[pltpu.roll(v, 7, 0) for v in row] for row in values]
    down = [[pltpu.roll(v, 1, 0) for v in row] for row in values]
    for s in range(strips):
        along_x, along_y, along_z = [], [], []
        for c in range(3):
            value = values[c][s]
            along_x.append(cells[c, slot + 1, rows_of(s), :] - cells[c, slot - 1, rows_of(s), :])
            ahead = jnp.where(rows == 7, up[c][s + 1] if s + 1 < strips else after(c), up[c][s])
            behind = jnp.where(rows == 0, down[c][s - 1] if s else before(c), down[c][s])
            along_y.append(ahead - behind)
            along_z.append(pltpu.roll(value, z_cells - 1, 1) - pltpu.roll(value, 1, 1))
        s_xy = along_y[0] + along_x[1]
        s_xz = along_z[0] + along_x[2]
        s_yz = along_z[1] + along_y[2]
        extra = 0.5 * (
            along_x[0] * along_x[0] + along_y[1] * along_y[1] + along_z[2] * along_z[2]
        ) + 0.25 * (s_xy * s_xy + s_xz * s_xz + s_yz * s_yz)
        rate_sq = rate_base**2 + extra
        value = jnp.exp(
            (0.5 / stress_exponent) * jnp.log(rate_sq)
            + (zener_energy / stress_exponent) * (1.0 / warmth[warm_slot, rows_of(s), :] - 1.0)
        )
        square = value * value + 1.0
        mu = jnp.log(value + square * lax.rsqrt(square)) * lax.rsqrt(rate_sq)
        outs[0][out_slot, rows_of(s), :] = mu * (scaled_mu / 3.0)
        if len(outs) > 1:
            heat = (mu * (1.0 / 3.0)) * extra
            for b in range(z_cells // 128):
                outs[1][b, out_slot, rows_of(s), :] = heat[:, b * 128 : (b + 1) * 128]


def viscosity_call(flow, y_sides, warmth, with_heat, x_sides=None, inner=None):
    _, x_local, y_local, z_cells = flow.shape
    z_blocks = z_cells // 128
    edge = x_sides is not None
    slots, made = (6, 2) if edge else (x_local, x_local - 2)
    outputs = 2 if with_heat else 1

    def kernel(*refs):
        flow_ref, before_ref, after_ref, warmth_ref = refs[:4]
        rest = list(refs[4:])
        listed = None
        if edge:
            low, high = rest[:2]
            listed = edge_list(flow_ref, low, high, x_local)
            rest = rest[2 + outputs :]
        out_refs, rest = rest[:outputs], rest[outputs:]
        cells, cell_sem, warm, warm_sem = rest[:4]
        outs, out_sems = rest[4 : 4 + outputs], rest[4 + outputs :]
        flow_planes = Planes(flow_ref, cells, cell_sem, listed)
        warm_planes = Planes(warmth_ref, warm, warm_sem)

        def plane_of(i):
            return i * (x_local - 1) if edge else i + 1

        def slot_of(i):
            return 3 * i + 1 if edge else i + 1

        def stored(k, i):
            return pltpu.make_async_copy(
                pick(outs[k], i), pick(out_refs[k], plane_of(i)), out_sems[k].at[i]
            )

        if edge:
            for slot in range(6):
                flow_planes.start(slot)
            for i in range(2):
                warm_planes.start(i, plane_of(i))
        else:
            flow_planes.start(0)
            flow_planes.start(1)

            def begin(i, state):
                flow_planes.start(i + 2)
                warm_planes.start(i, i + 1)
                return state

            lax.fori_loop(0, made, begin, 0)
            flow_planes.wait(0)
            flow_planes.wait(1)

        def body(i, state):
            slot, plane = slot_of(i), plane_of(i)
            if edge:
                flow_planes.wait(slot - 1)
                flow_planes.wait(slot)
            flow_planes.wait(slot + 1)
            warm_planes.wait(i)
            viscosity_plane(
                cells,
                slot,
                (lambda c: before_ref[c, plane], lambda c: after_ref[c, plane]),
                warm,
                i,
                outs,
                i,
                y_local,
                z_cells,
            )
            for k in range(outputs):
                stored(k, i).start()
            return state

        lax.fori_loop(0, made, body, 0)

        def finish(i, state):
            for k in range(outputs):
                stored(k, i).wait()
            return state

        lax.fori_loop(0, made, finish, 0)

    shapes = [(x_local, y_local, z_cells), (z_blocks, x_local, y_local, 128)][:outputs]
    held = [(made, y_local, z_cells), (z_blocks, made, y_local, 128)][:outputs]
    operands = [flow, *y_sides, warmth]
    specs = [anywhere, in_vmem, in_vmem, anywhere]
    aliases = {}
    if edge:
        operands += [*x_sides, *inner]
        specs += [anywhere] * (2 + outputs)
        aliases = {6 + k: k for k in range(outputs)}
    return pl.pallas_call(
        kernel,
        in_specs=specs,
        out_specs=[anywhere] * outputs,
        out_shape=[jax.ShapeDtypeStruct(shape, jnp.float32) for shape in shapes],
        input_output_aliases=aliases,
        scratch_shapes=[
            pltpu.VMEM((3, slots, y_local, z_cells), jnp.float32),
            pltpu.SemaphoreType.DMA((slots,)),
            pltpu.VMEM((made, y_local, z_cells), jnp.float32),
            pltpu.SemaphoreType.DMA((made,)),
        ]
        + [pltpu.VMEM(shape, jnp.float32) for shape in held]
        + [pltpu.SemaphoreType.DMA((made,))] * outputs,
        compiler_params=pltpu.CompilerParams(vmem_limit_bytes=vmem_limit),
        name="viscosity_edge" if edge else "viscosity_inner",
    )(*operands)


def viscosity_inner(flow, y_sides, warmth, with_heat):
    _, x_local, y_local, z_cells = flow.shape
    z_blocks, size = z_cells // 128, 4
    outputs = 2 if with_heat else 1

    def kernel(flow_ref, before_ref, after_ref, warmth_ref, *rest):
        out_refs, (cells, cell_sem, warm, warm_sem, *heat) = rest[:outputs], rest[outputs:]
        outs = [out_refs[0]] + heat[:1]

        def body(slot, state):
            viscosity_plane(
                cells,
                slot,
                (lambda c: before_ref[c, slot], lambda c: after_ref[c, slot]),
                warm,
                slot,
                outs,
                slot,
                y_local,
                z_cells,
            )
            return state

        in_sections(
            x_local,
            size,
            [(flow_ref, cells, cell_sem), (warmth_ref, warm, warm_sem)],
            [(heat[0], out_refs[1], heat[1])] if with_heat else [],
            lambda: None,
            body,
        )

    shapes = [(x_local, y_local, z_cells), (z_blocks, x_local, y_local, 128)][:outputs]
    sems = pltpu.SemaphoreType.DMA((x_local // size,))
    return pl.pallas_call(
        kernel,
        in_specs=[anywhere, in_vmem, in_vmem, anywhere],
        out_specs=[in_vmem, anywhere][:outputs],
        out_shape=[jax.ShapeDtypeStruct(shape, jnp.float32) for shape in shapes],
        scratch_shapes=[
            pltpu.VMEM(flow.shape, jnp.float32),
            sems,
            pltpu.VMEM(warmth.shape, jnp.float32),
            sems,
        ]
        + ([pltpu.VMEM(shapes[1], jnp.float32), sems] if with_heat else []),
        compiler_params=pltpu.CompilerParams(vmem_limit_bytes=vmem_limit),
        name="viscosity_inner",
    )(flow, *y_sides, warmth)


vmem_limit = 48 << 20


def advance_plane(cells, mu, slot, edges, push, out_slot, flux, y_local, z_cells):
    strips, rows = y_local // 8, row_numbers(z_cells)
    flow_before, flow_after, mu_before, mu_after = edges
    m = [mu[slot, rows_of(s), :] for s in range(strips)]
    m_up = [pltpu.roll(v, 7, 0) for v in m]
    sums_y = [
        m[s] + jnp.where(rows == 7, m_up[s + 1] if s + 1 < strips else mu_after(), m_up[s])
        for s in range(strips)
    ]
    first_sum = mu_before() + mu[slot, pl.ds(0, 1), :]
    values = [[cells[c, slot, rows_of(s), :] for s in range(strips)] for c in range(3)]
    up = [[pltpu.roll(v, 7, 0) for v in row] for row in values]
    carried = [
        first_sum * (cells[c, slot, pl.ds(0, 1), :] - flow_before(c)) for c in range(3)
    ]
    for s in range(strips):
        sum_x = m[s] + mu[slot + 1, rows_of(s), :]
        sum_z_ahead = m[s] + pltpu.roll(m[s], z_cells - 1, 1)
        sum_z_behind = m[s] + pltpu.roll(m[s], 1, 1)
        for c in range(3):
            value = values[c][s]
            flux_x = sum_x * (cells[c, slot + 1, rows_of(s), :] - value)
            ahead = jnp.where(
                rows == 7, up[c][s + 1] if s + 1 < strips else flow_after(c), up[c][s]
            )
            flux_y = sums_y[s] * (ahead - value)
            turned = pltpu.roll(flux_y, 1, 0)
            total = (flux_x - flux[c, rows_of(s), :]) + (
                flux_y - jnp.where(rows == 0, carried[c], turned)
            ) + (
                sum_z_ahead * (pltpu.roll(value, z_cells - 1, 1) - value)
                - sum_z_behind * (value - pltpu.roll(value, 1, 1))
            )
            flux[c, rows_of(s), :] = flux_x
            carried[c] = turned
            push[c, out_slot, rows_of(s), :] = (
                value + time_step * push[c, out_slot, rows_of(s), :] + total
            )


def first_flux(cells, mu, slot, flux, y_local):
    for s in range(y_local // 8):
        sum_x = mu[slot - 1, rows_of(s), :] + mu[slot, rows_of(s), :]
        for c in range(3):
            flux[c, rows_of(s), :] = sum_x * (
                cells[c, slot, rows_of(s), :] - cells[c, slot - 1, rows_of(s), :]
            )


def advance_call(flow, flow_y, mu, mu_y, push, flow_x=None, mu_x=None, inner=None):
    _, x_local, y_local, z_cells = flow.shape
    edge = flow_x is not None
    slots, made = (6, 2) if edge else (x_local, x_local - 2)

    def kernel(*refs):
        flow_ref, flow_before, flow_after, mu_ref, mu_before, mu_after, push_ref = refs[:7]
        rest = refs[7:]
        flow_listed = mu_listed = None
        if edge:
            flow_listed = edge_list(flow_ref, rest[0], rest[1], x_local)
            mu_listed = edge_list(mu_ref, rest[2], rest[3], x_local)
            rest = rest[5:]
        out_ref, cells, cell_sem, mu_cells, mu_sem, work, work_sem, out_sem, flux = rest
        flow_planes = Planes(flow_ref, cells, cell_sem, flow_listed)
        mu_planes = Planes(mu_ref, mu_cells, mu_sem, mu_listed)
        push_planes = Planes(push_ref, work, work_sem)

        def plane_of(i):
            return i * (x_local - 1) if edge else i + 1

        def stored(i):
            return pltpu.make_async_copy(
                pick(work, i), pick(out_ref, plane_of(i)), out_sem.at[i]
            )

        if edge:
            for slot in range(6):
                flow_planes.start(slot)
                mu_planes.start(slot)
            for i in range(2):
                push_planes.start(i, plane_of(i))
        else:
            for slot in range(2):
                flow_planes.start(slot)
                mu_planes.start(slot)

            def begin(i, state):
                flow_planes.start(i + 2)
                mu_planes.start(i + 2)
                push_planes.start(i, i + 1)
                return state

            lax.fori_loop(0, made, begin, 0)
            for slot in range(2):
                flow_planes.wait(slot)
                mu_planes.wait(slot)
            first_flux(cells, mu_cells, 1, flux, y_local)

        def body(i, state):
            slot, plane = (3 * i + 1 if edge else i + 1), plane_of(i)
            if edge:
                for back in range(2):
                    flow_planes.wait(slot - back)
                    mu_planes.wait(slot - back)
                first_flux(cells, mu_cells, slot, flux, y_local)
            flow_planes.wait(slot + 1)
            mu_planes.wait(slot + 1)
            push_planes.wait(i)
            advance_plane(
                cells,
                mu_cells,
                slot,
                (
                    lambda c: flow_before[c, plane],
                    lambda c: flow_after[c, plane],
                    lambda: mu_before[plane],
                    lambda: mu_after[plane],
                ),
                work,
                i,
                flux,
                y_local,
                z_cells,
            )
            stored(i).start()
            return state

        lax.fori_loop(0, made, body, 0)

        def finish(i, state):
            stored(i).wait()
            return state

        lax.fori_loop(0, made, finish, 0)

    operands = [flow, *flow_y, mu, *mu_y, push]
    specs = [anywhere, in_vmem, in_vmem, anywhere, in_vmem, in_vmem, anywhere]
    aliases = {}
    if edge:
        operands += [*flow_x, *mu_x, inner]
        specs += [anywhere] * 5
        aliases = {11: 0}
    return pl.pallas_call(
        kernel,
        in_specs=specs,
        out_specs=anywhere,
        out_shape=jax.ShapeDtypeStruct(flow.shape, jnp.float32),
        input_output_aliases=aliases,
        scratch_shapes=[
            pltpu.VMEM((3, slots, y_local, z_cells), jnp.float32),
            pltpu.SemaphoreType.DMA((slots,)),
            pltpu.VMEM((slots, y_local, z_cells), jnp.float32),
            pltpu.SemaphoreType.DMA((slots,)),
            pltpu.VMEM((3, made, y_local, z_cells), jnp.float32),
            pltpu.SemaphoreType.DMA((made,)),
            pltpu.SemaphoreType.DMA((made,)),
            pltpu.VMEM((3, y_local, z_cells), jnp.float32),
        ],
        compiler_params=pltpu.CompilerParams(vmem_limit_bytes=vmem_limit),
        name="advance_edge" if edge else "advance_inner",
    )(*operands)


def advance_inner(flow, flow_y, mu, mu_y, push):
    _, x_local, y_local, z_cells = flow.shape
    size = 4

    def kernel(
        flow_ref, flow_before, flow_after, mu_ref, mu_before, mu_after, push_ref,
        out_ref, cells, cell_sem, work, work_sem, out_sem, flux,
    ):
        def body(slot, state):
            advance_plane(
                cells,
                mu_ref,
                slot,
                (
                    lambda c: flow_before[c, slot],
                    lambda c: flow_after[c, slot],
                    lambda: mu_before[slot],
                    lambda: mu_after[slot],
                ),
                work,
                slot,
                flux,
                y_local,
                z_cells,
            )
            return state

        in_sections(
            x_local,
            size,
            [(flow_ref, cells, cell_sem), (push_ref, work, work_sem)],
            [(work, out_ref, out_sem)],
            lambda: first_flux(cells, mu_ref, 1, flux, y_local),
            body,
        )

    sems = pltpu.SemaphoreType.DMA((x_local // size,))
    return pl.pallas_call(
        kernel,
        in_specs=[anywhere, in_vmem, in_vmem, in_vmem, in_vmem, in_vmem, anywhere],
        out_specs=anywhere,
        out_shape=jax.ShapeDtypeStruct(flow.shape, jnp.float32),
        scratch_shapes=[
            pltpu.VMEM(flow.shape, jnp.float32),
            sems,
            pltpu.VMEM(flow.shape, jnp.float32),
            sems,
            sems,
            pltpu.VMEM((3, y_local, z_cells), jnp.float32),
        ],
        compiler_params=pltpu.CompilerParams(vmem_limit_bytes=vmem_limit),
        name="advance_inner",
    )(flow, *flow_y, mu, *mu_y, push)


def cosine_sine_basis(points, period, waves):
    columns, eigen = [], []
    for wave in waves:
        angle = 2.0 * np.pi * ((wave * np.arange(points)) % period) / period
        single = wave % period == 0 or 2 * wave == period
        size = math.sqrt((1.0 if single else 2.0) / period)
        columns.append(np.cos(angle) * size)
        eigen.append(math.sin(2.0 * math.pi * wave / period) ** 2)
        if not single:
            columns.append(np.sin(angle) * size)
            eigen.append(eigen[-1])
    return np.stack(columns, 1), np.array(eigen)


def halves(table):
    table = np.asarray(table, np.float32)
    high = table.astype(jnp.bfloat16)
    low = (table - high.astype(np.float32)).astype(jnp.bfloat16)
    return jnp.asarray(high), jnp.asarray(low)


def split(value):
    high = value.astype(jnp.bfloat16)
    return high, (value - high.astype(jnp.float32)).astype(jnp.bfloat16)


def triple_product(left, right):
    def product(one, two):
        return lax.dot_general(
            one, two, (((1,), (0,)), ((), ())), preferred_element_type=jnp.float32
        )

    return product(left[0], right[0]) + (product(left[0], right[1]) + product(left[1], right[0]))


def z_tables(z_cells):
    half = z_cells // 2
    even, eigen_even = cosine_sine_basis(half, z_cells, range(0, half + 1, 2))
    odd, eigen_odd = cosine_sine_basis(half, z_cells, range(1, half, 2))
    return even, odd, np.concatenate([eigen_even, eigen_odd])


def modes_of(lines, even_high, even_low, odd_high, odd_low):
    half = lines.shape[1] // 2
    first, second = lines[:, :half], lines[:, half:]
    return jnp.concatenate(
        [
            triple_product(split(first + second), (even_high[...], even_low[...])),
            triple_product(split(first - second), (odd_high[...], odd_low[...])),
        ],
        1,
    )


def cells_of(modes, even_high, even_low, odd_high, odd_low):
    half = modes.shape[1] // 2
    first = triple_product(split(modes[:, :half]), (even_high[...], even_low[...]))
    second = triple_product(split(modes[:, half:]), (odd_high[...], odd_low[...]))
    return jnp.concatenate([first + second, first - second], 1)


def divergence_modes(flow, count):
    _, x_local, y_local, z_cells = flow.shape
    piece, strips = z_cells // count, y_local // 8
    step = min(8, x_local)
    even, odd, _ = z_tables(z_cells)
    tables = halves(even) + halves(odd)

    def kernel(
        flow_ref, even_high, even_low, odd_high, odd_low, out_ref,
        cells, semaphores, work, made, out_sem,
    ):
        planes = Planes(flow_ref, cells, semaphores)
        rows = row_numbers(z_cells)

        def begin(i, state):
            planes.start(i)
            return state

        lax.fori_loop(0, x_local, begin, 0)
        planes.wait(0)

        def stored(k):
            part = pl.ds(k * step, step)
            return pltpu.make_async_copy(made.at[:, part], out_ref.at[:, part], out_sem.at[k])

        def group(k, state):
            def plane(i, state):
                j = k * step + i

                @pl.when(j + 1 < x_local)
                def _():
                    planes.wait(j + 1)

                nearer = jnp.where(j > 0, 0.5, 0.0)
                further = jnp.where(j + 1 < x_local, 0.5, 0.0)
                last, following = jnp.maximum(j - 1, 0), jnp.minimum(j + 1, x_local - 1)
                across = [cells[1, j, rows_of(s), :] for s in range(strips)]
                up = [pltpu.roll(v, 7, 0) for v in across]
                down = [pltpu.roll(v, 1, 0) for v in across]
                for s in range(strips):
                    ahead = jnp.where(rows == 7, up[s + 1] if s + 1 < strips else 0.0, up[s])
                    behind = jnp.where(rows == 0, down[s - 1] if s else 0.0, down[s])
                    along = cells[2, j, rows_of(s), :]
                    work[i, rows_of(s), :] = (
                        further * cells[0, following, rows_of(s), :]
                        - nearer * cells[0, last, rows_of(s), :]
                    ) + 0.5 * (
                        (ahead - behind)
                        + (pltpu.roll(along, z_cells - 1, 1) - pltpu.roll(along, 1, 1))
                    )
                return state

            lax.fori_loop(0, step, plane, 0)
            modes = modes_of(
                work[...].reshape(step * y_local, z_cells), even_high, even_low, odd_high, odd_low
            )
            for n in range(count):
                made[n, pl.ds(k * step, step)] = modes[:, n * piece : (n + 1) * piece].reshape(
                    step, y_local, piece
                )
            stored(k).start()
            return state

        groups = x_local // step
        lax.fori_loop(0, groups, group, 0)
        for k in range(groups):
            stored(k).wait()

    return pl.pallas_call(
        kernel,
        in_specs=[anywhere] + [in_vmem] * 4,
        out_specs=anywhere,
        out_shape=jax.ShapeDtypeStruct((count, x_local, y_local, piece), jnp.float32),
        scratch_shapes=[
            pltpu.VMEM((3, x_local, y_local, z_cells), jnp.float32),
            pltpu.SemaphoreType.DMA((x_local,)),
            pltpu.VMEM((step, y_local, z_cells), jnp.float32),
            pltpu.VMEM((count, x_local, y_local, piece), jnp.float32),
            pltpu.SemaphoreType.DMA((x_local // step,)),
        ],
        name="divergence_modes",
    )(flow, *tables)


def add_halo_modes(modes, x_sides, y_sides):
    count, x_local, y_local, piece = modes.shape
    z_cells = count * piece
    even, odd, _ = z_tables(z_cells)
    tables = halves(even) + halves(odd)

    def kernel(
        modes_ref, low_ref, high_ref, before_ref, after_ref,
        even_high, even_low, odd_high, odd_low, out_ref, ends, lines, semaphores,
    ):
        def moves(back):
            pairs = [
                (ends.at[k], modes_ref.at[:, plane])
                for k, plane in enumerate((0, x_local - 1))
            ] + [
                (lines.at[k], modes_ref.at[:, 1 : x_local - 1, 8 * s : 8 * s + 8])
                for k, s in enumerate((0, y_local // 8 - 1))
            ]
            if back:
                pairs = [
                    (ends.at[k], out_ref.at[:, plane])
                    for k, plane in enumerate((0, x_local - 1))
                ] + [
                    (lines.at[k], out_ref.at[:, 1 : x_local - 1, 8 * s : 8 * s + 8])
                    for k, s in enumerate((0, y_local // 8 - 1))
                ]
                return [
                    pltpu.make_async_copy(here, there, semaphores.at[4 + i])
                    for i, (here, there) in enumerate(pairs)
                ]
            return [
                pltpu.make_async_copy(there, here, semaphores.at[i])
                for i, (here, there) in enumerate(pairs)
            ]

        loads, stores = moves(False), moves(True)
        for load in loads:
            load.start()
        added = modes_of(
            jnp.concatenate(
                [-0.5 * low_ref[0], 0.5 * high_ref[0], -0.5 * before_ref[...], 0.5 * after_ref[...]],
                0,
            ),
            even_high,
            even_low,
            odd_high,
            odd_low,
        )
        for load in loads:
            load.wait()
        rows = row_numbers(piece)
        for n in range(count):
            block = added[:, n * piece : (n + 1) * piece]
            side = [block[2 * y_local + k * x_local :][:x_local] for k in range(2)]
            for k, plane in enumerate((0, x_local - 1)):
                ends[k, n] = ends[k, n] + block[k * y_local : (k + 1) * y_local]
                for j, (strip, row) in enumerate(((0, 0), (y_local // 8 - 1, 7))):
                    part = pl.ds(8 * strip, 8)
                    ends[k, n, part, :] = ends[k, n, part, :] + jnp.where(
                        rows == row, side[j][plane : plane + 1], 0.0
                    )
            for j, row in enumerate((0, 7)):
                for x in range(1, x_local - 1):
                    lines[j, n, x - 1] = lines[j, n, x - 1] + jnp.where(
                        rows == row, side[j][x : x + 1], 0.0
                    )
        for store in stores:
            store.start()
        for store in stores:
            store.wait()

    return pl.pallas_call(
        kernel,
        in_specs=[anywhere] + [in_vmem] * 8,
        out_specs=anywhere,
        out_shape=jax.ShapeDtypeStruct(modes.shape, jnp.float32),
        input_output_aliases={0: 0},
        scratch_shapes=[
            pltpu.VMEM((2, count, y_local, piece), jnp.float32),
            pltpu.VMEM((2, count, x_local - 2, 8, piece), jnp.float32),
            pltpu.SemaphoreType.DMA((8,)),
        ],
        name="add_halo_modes",
    )(modes, *x_sides, *y_sides, *tables)


def corrected(flow, spectrum, y_sides):
    count, planes, y_local, piece = spectrum.shape
    x_local, z_cells = planes - 2, count * piece
    strips, part = y_local // 8, planes // 2
    even, odd, _ = z_tables(z_cells)
    tables = halves(even.T) + halves(odd.T)

    def kernel(
        flow_ref, in_ref, before_ref, after_ref,
        even_high, even_low, odd_high, odd_low, out_ref,
        modes, mode_sem, pressure, sides, work, flow_sem, out_sem,
    ):
        flow_planes = Planes(flow_ref, work, flow_sem)
        table_refs = (even_high, even_low, odd_high, odd_low)

        def load(k):
            span = pl.ds(k * part, part)
            return pltpu.make_async_copy(in_ref.at[:, span], modes.at[:, span], mode_sem.at[k])

        load(0).start()
        load(1).start()

        def begin(i, state):
            flow_planes.start(i)
            return state

        lax.fori_loop(0, x_local, begin, 0)
        sides[...] = cells_of(
            jnp.concatenate(
                [
                    jnp.concatenate([ref[n] for n in range(count)], 1)
                    for ref in (before_ref, after_ref)
                ],
                0,
            ),
            *table_refs,
        )
        rows = row_numbers(z_cells)

        def stored(i):
            return pltpu.make_async_copy(pick(work, i), pick(out_ref, i), out_sem.at[i])

        def plane(j, state):
            flow_planes.wait(j)
            values = [pressure[j + 1, rows_of(s), :] for s in range(strips)]
            up = [pltpu.roll(v, 7, 0) for v in values]
            down = [pltpu.roll(v, 1, 0) for v in values]
            for s in range(strips):
                ahead = up[s + 1] if s + 1 < strips else sides[pl.ds(x_local + j, 1), :]
                behind = down[s - 1] if s else sides[pl.ds(j, 1), :]
                slopes = (
                    pressure[j + 2, rows_of(s), :] - pressure[j, rows_of(s), :],
                    jnp.where(rows == 7, ahead, up[s]) - jnp.where(rows == 0, behind, down[s]),
                    pltpu.roll(values[s], z_cells - 1, 1) - pltpu.roll(values[s], 1, 1),
                )
                for c in range(3):
                    work[c, j, rows_of(s), :] = work[c, j, rows_of(s), :] - 0.5 * slopes[c]
            stored(j).start()
            return state

        for k in range(2):
            load(k).wait()
            span = pl.ds(k * part, part)
            pressure[span] = cells_of(
                jnp.concatenate(
                    [modes[n, span].reshape(part * y_local, piece) for n in range(count)], 1
                ),
                *table_refs,
            ).reshape(part, y_local, z_cells)
            lax.fori_loop(k * (part - 2), (part - 2) if k == 0 else x_local, plane, 0)

        def finish(i, state):
            stored(i).wait()
            return state

        lax.fori_loop(0, x_local, finish, 0)

    return pl.pallas_call(
        kernel,
        in_specs=[anywhere, anywhere] + [in_vmem] * 6,
        out_specs=anywhere,
        out_shape=jax.ShapeDtypeStruct(flow.shape, jnp.float32),
        scratch_shapes=[
            pltpu.VMEM(spectrum.shape, jnp.float32),
            pltpu.SemaphoreType.DMA((2,)),
            pltpu.VMEM((planes, y_local, z_cells), jnp.float32),
            pltpu.VMEM((2 * x_local, z_cells), jnp.float32),
            pltpu.VMEM(flow.shape, jnp.float32),
            pltpu.SemaphoreType.DMA((x_local,)),
            pltpu.SemaphoreType.DMA((x_local,)),
        ],
        compiler_params=pltpu.CompilerParams(vmem_limit_bytes=vmem_limit),
        name="corrected",
    )(flow, spectrum, *y_sides, *tables)


def y_forward(spectrum, ratio, wide_count):
    count, x_local, y_local, piece = spectrum.shape
    y_cells = count * y_local
    share, group = y_cells // wide_count, max(2, x_local // 4)
    table, _ = cosine_sine_basis(y_cells, y_cells, range(y_cells // 2 + 1))
    tables = halves(table.T)

    def kernel(
        in_ref, high_ref, low_ref, ratio_ref, modes_ref, carry_ref,
        lines, in_sems, made, out_sems, sums, power,
    ):
        def load(k):
            part = pl.ds(k * group, group)
            return pltpu.make_async_copy(in_ref.at[:, part], lines.at[:, part], in_sems.at[k])

        def stored(k):
            part = pl.ds(k * group, group)
            return pltpu.make_async_copy(made.at[part], modes_ref.at[part], out_sems.at[k])

        for k in range(x_local // group):
            load(k).start()
        sums[...] = jnp.zeros_like(sums)
        power[...] = jnp.ones_like(power)

        def body(t, state):
            planes = [
                jnp.concatenate([lines[n, 2 * t + side] for n in range(count)], 0)
                for side in range(2)
            ]
            modes = triple_product(
                (high_ref[...], low_ref[...]), split(jnp.concatenate(planes, 1))
            )
            r, pw = ratio_ref[...], power[...]
            for side in range(2):
                plane = modes[:, side * piece : (side + 1) * piece]
                made[2 * t + side] = plane
                sums[side] = plane + r * sums[side]
                sums[2 + side] = sums[2 + side] + pw * plane
            power[...] = pw * r
            return state

        def section(k, state):
            load(k).wait()
            lax.fori_loop(k * (group // 2), (k + 1) * (group // 2), body, 0)
            stored(k).start()
            return state

        lax.fori_loop(0, x_local // group, section, 0)
        for kind in range(4):
            carry_ref[:, kind] = sums[kind].reshape(wide_count, share, piece)
        for k in range(x_local // group):
            stored(k).wait()

    return pl.pallas_call(
        kernel,
        in_specs=[anywhere] + [in_vmem] * 3,
        out_specs=[anywhere, in_vmem],
        out_shape=[
            jax.ShapeDtypeStruct((x_local, y_cells, piece), jnp.float32),
            jax.ShapeDtypeStruct((wide_count, 4, share, piece), jnp.float32),
        ],
        scratch_shapes=[
            pltpu.VMEM(spectrum.shape, jnp.float32),
            pltpu.SemaphoreType.DMA((x_local // group,)),
            pltpu.VMEM((x_local, y_cells, piece), jnp.float32),
            pltpu.SemaphoreType.DMA((x_local // group,)),
            pltpu.VMEM((4, y_cells, piece), jnp.float32),
            pltpu.VMEM((y_cells, piece), jnp.float32),
        ],
        name="y_forward",
    )(spectrum, *tables, ratio)


def power_of(value, exponent):
    result = None
    while exponent:
        if exponent & 1:
            result = value if result is None else result * value
        value = value * value
        exponent >>= 1
    return result


def join_carries(carries, ratio, block):
    count, kinds, _, _ = carries.shape

    def kernel(in_ref, ratio_ref, out_ref):
        step = power_of(ratio_ref[...], block)
        scale = 1.0 / (1.0 - power_of(step, count))
        for kind in range(kinds):
            order = list(range(count)) if kind < 2 else list(range(count))[::-1]
            total = in_ref[order[0], kind]
            for w in order[1:]:
                total = in_ref[w, kind] + step * total
            total = total * scale
            for w in order:
                out_ref[w, kind] = total
                total = in_ref[w, kind] + step * total

    return pl.pallas_call(
        kernel,
        in_specs=[in_vmem] * 2,
        out_specs=in_vmem,
        out_shape=jax.ShapeDtypeStruct(carries.shape, jnp.float32),
        compiler_params=pltpu.CompilerParams(vmem_limit_bytes=vmem_limit),
        name="join_carries",
    )(carries, ratio)


def y_inverse(modes, carries, ratio, gain, count):
    x_local, y_cells, piece = modes.shape
    y_local, pairs, group = y_cells // count, x_local // 2, max(2, x_local // 4)
    table, _ = cosine_sine_basis(y_cells, y_cells, range(y_cells // 2 + 1))
    tables = halves(table)

    def kernel(
        modes_in, carry_ref, high_ref, low_ref, ratio_ref, gain_ref, out_ref,
        planes, in_sems, behind, state, cells, out_sems,
    ):
        def load(k):
            part = pl.ds(k * group, group)
            return pltpu.make_async_copy(modes_in.at[part], planes.at[part], in_sems.at[k])

        def stored(t):
            part = pl.ds(2 * t, 2)
            return pltpu.make_async_copy(cells.at[:, part], out_ref.at[:, part], out_sems.at[t])

        def carry(kind):
            return carry_ref[:, kind].reshape(y_cells, piece)

        groups = x_local // group
        for k in range(groups)[::-1]:
            load(k).start()
        for kind in range(4):
            state[kind] = carry(kind)
        behind[x_local + 1] = carry(2)

        def back(i, done):
            m = pairs - 1 - i
            r = ratio_ref[...]
            for side in range(2):
                value = r * state[2 + side]
                behind[2 * m + 1 + side] = value
                state[2 + side] = planes[2 * m + side] + value
            return done

        def back_section(k, done):
            load(groups - 1 - k).wait()
            lax.fori_loop(k * (group // 2), (k + 1) * (group // 2), back, 0)
            return done

        lax.fori_loop(0, groups, back_section, 0)
        behind[0] = ratio_ref[...] * state[3]

        def body(t, done):
            r, gain_value = ratio_ref[...], gain_ref[...]
            even_plane = planes[jnp.minimum(2 * t, x_local - 2)]
            odd_plane = planes[jnp.maximum(2 * t - 1, 1)]
            even = r * state[0] + jnp.where(t < pairs, even_plane, 0.0)
            odd = jnp.where(t > 0, odd_plane + r * state[1], state[1])
            state[0] = even
            state[1] = odd
            joined = jnp.concatenate(
                [gain_value * (odd + behind[2 * t]), gain_value * (even + behind[2 * t + 1])], 1
            )
            result = triple_product((high_ref[...], low_ref[...]), split(joined))
            for n in range(count):
                for side in range(2):
                    cells[n, 2 * t + side] = result[
                        n * y_local : (n + 1) * y_local, side * piece : (side + 1) * piece
                    ]
            stored(t).start()
            return done

        lax.fori_loop(0, pairs + 1, body, 0)

        def finish(t, done):
            stored(t).wait()
            return done

        lax.fori_loop(0, pairs + 1, finish, 0)

    made = (count, x_local + 2, y_local, piece)
    return pl.pallas_call(
        kernel,
        in_specs=[anywhere] + [in_vmem] * 5,
        out_specs=anywhere,
        out_shape=jax.ShapeDtypeStruct(made, jnp.float32),
        scratch_shapes=[
            pltpu.VMEM(modes.shape, jnp.float32),
            pltpu.SemaphoreType.DMA((x_local // group,)),
            pltpu.VMEM((x_local + 2, y_cells, piece), jnp.float32),
            pltpu.VMEM((4, y_cells, piece), jnp.float32),
            pltpu.VMEM(made, jnp.float32),
            pltpu.SemaphoreType.DMA((pairs + 1,)),
        ],
        name="y_inverse",
    )(modes, carries, *tables, ratio, gain)


def turn(value, axis):
    return lax.all_to_all(value, axis, split_axis=0, concat_axis=0, tiled=True)


def project(spectrum, late):
    count, x_local, y_local, piece = spectrum.shape
    y_cells, z_cells = count * y_local, count * piece
    wide_count = lax.axis_size("wide")
    _, eigen_y = cosine_sine_basis(y_cells, y_cells, range(y_cells // 2 + 1))
    eigen_z = jnp.asarray(z_tables(z_cells)[2], jnp.float32)
    own_z = lax.dynamic_slice_in_dim(eigen_z, lax.axis_index("narrow") * piece, piece)
    excess = 4.0 * (jnp.asarray(eigen_y, jnp.float32)[:, None] + own_z[None, :] + penalty)
    root = jnp.sqrt(excess * (4.0 + excess))
    ratio = 2.0 / (2.0 + excess + root)
    gain = -4.0 / root
    share = y_cells // wide_count
    own_ratio = lax.dynamic_slice_in_dim(ratio, lax.axis_index("wide") * share, share)
    spectrum = turn(spectrum, "narrow")
    modes, carries = y_forward(spectrum, ratio, wide_count)
    carries, late = lax.optimization_barrier((turn(carries, "wide"), late))
    carries = turn(join_carries(carries, own_ratio, x_local // 2), "wide")
    return turn(y_inverse(modes, carries, ratio, gain, count), "narrow"), late


def conduct(profile, spread):
    sides = (("wide", 0), ("narrow", 1))
    spread = with_halo(spread, sides, STEPS - 1, False)
    profile = with_halo(profile, sides, STEPS, False)
    for _ in range(STEPS):
        center = profile[1:-1, 1:-1]
        near = (
            profile[2:, 1:-1] + profile[:-2, 1:-1] + profile[1:-1, 2:] + profile[1:-1, :-2]
        )
        ahead = jnp.pad(center[:, :, 1:], ((0, 0), (0, 0), (0, 1)))
        behind = jnp.pad(center[:, :, :-1], ((0, 0), (0, 0), (1, 0)))
        profile = center + spread * (near + ahead + behind - 6.0 * center)
        spread = spread[1:-1, 1:-1]
    return profile


def both_rings(value, dim):
    y_sides = ring(value, "narrow", dim + 1)
    x_sides = ring(value, "wide", dim)
    return x_sides, y_sides


def device_step(
    material_flow_vector,
    tool_push_density,
    tool_warmth_excess,
    substrate_warmth_excess,
    spread_coefficient,
    source_owner_sheet,
    source_part_line,
):
    flow = material_flow_vector
    flow_x, flow_y = both_rings(flow, 1)
    current, current_x, current_y = flow, flow_x, flow_y
    for section in range(PASSES):
        last = section + 1 == PASSES
        inner = viscosity_inner(current, current_y, tool_warmth_excess, last)
        fields = viscosity_call(current, current_y, tool_warmth_excess, last, current_x, inner)
        mu = fields[0]
        mu_x, mu_y = both_rings(mu, 0)
        inner = advance_inner(flow, flow_y, mu, mu_y, tool_push_density)
        current = advance_call(flow, flow_y, mu, mu_y, tool_push_density, flow_x, mu_x, inner)
        if not last:
            current_x, current_y = both_rings(current, 1)
    heat_cells = fields[1]
    end_x = ring(current[0], "wide", 0)
    y_local = flow.shape[2]
    end_y = [
        shift(current[1, :, y_local - 1 :], "narrow", 1)[:, 0],
        shift(current[1, :, :1], "narrow", -1)[:, 0],
    ]
    modes = divergence_modes(current, lax.axis_size("narrow"))
    z_blocks = heat_cells.shape[0]
    slab_count = lax.axis_size("wide")
    component_lines = substrate_warmth_excess.shape[0] * substrate_warmth_excess.shape[1]
    targets = source_owner_sheet[:, 0] * component_lines + source_part_line
    partial_value = (
        jnp.zeros((slab_count * component_lines, 128), jnp.float32)
        .at[targets.reshape(-1, z_blocks).T.reshape(-1)]
        .add(heat_cells.reshape(-1, 128))
    )
    spectrum, partial_value = project(add_halo_modes(modes, end_x, end_y), partial_value)
    inner = spectrum[:, 1:-1]
    corrected_flow_vector = corrected(
        current, spectrum, [side[:, :, 0] for side in ring(inner, "narrow", 2)]
    )
    substrate_energy_input = lax.psum_scatter(
        partial_value.reshape(slab_count, component_lines, 128),
        "wide",
        scatter_dimension=0,
        tiled=True,
    )
    thermal_profile = substrate_warmth_excess + dissipation_factor * substrate_energy_input.reshape(
        substrate_warmth_excess.shape
    )
    return (corrected_flow_vector, conduct(thermal_profile, spread_coefficient))


def solution(mesh):
    return jax.shard_map(
        device_step,
        mesh=mesh,
        in_specs=(
            P(None, "wide", "narrow", None),
            P(None, "wide", "narrow", None),
            P("wide", "narrow", None),
            P("wide", "narrow", None),
            P("wide", "narrow", None),
            P(("wide", "narrow"), None),
            P(("wide", "narrow")),
        ),
        out_specs=(P(None, "wide", "narrow", None), P("wide", "narrow", None)),
        check_vma=False,
    )
```

```python
import math

import jax
import jax.numpy as jnp
import numpy as np
from jax import lax
from jax.experimental import pallas as pl
from jax.experimental.pallas import tpu as pltpu
from jax.sharding import PartitionSpec as P


PASSES = 2
STEPS = 3


time_step = 0.15
rate_base = 0.5
zener_energy = 4.0
stress_exponent = 5.0
penalty = 0.001
dissipation_factor = 0.1


def with_halo(x, sides, width, wrap):
    for axis, dim in sides:
        size, length = (lax.axis_size(axis), x.shape[dim])
        up = [(i, (i + 1) % size) for i in range(size if wrap else size - 1)]
        down = [(j, i) for i, j in up]
        last = lax.slice_in_dim(x, length - width, length, axis=dim)
        initial = lax.slice_in_dim(x, 0, width, axis=dim)
        before = lax.ppermute(last, axis, up)
        after = lax.ppermute(initial, axis, down)
        x = jnp.concatenate([before, x, after], axis=dim)
    return x


def shift(value, axis, by):
    size = lax.axis_size(axis)
    return lax.ppermute(value, axis, [(i, (i + by) % size) for i in range(size)])


def ring(value, axis, dim):
    length = value.shape[dim]
    last = lax.slice_in_dim(value, length - 1, length, axis=dim)
    initial = lax.slice_in_dim(value, 0, 1, axis=dim)
    return shift(last, axis, 1), shift(initial, axis, -1)


anywhere = pl.BlockSpec(memory_space=pl.ANY)
in_vmem = pl.BlockSpec(memory_space=pltpu.VMEM)
scaled_mu = 0.5 * time_step


def row_numbers(width):
    return lax.broadcasted_iota(jnp.int32, (8, width), 0)


def rows_of(strip):
    return pl.ds(8 * strip, 8)


def pick(ref, index):
    return ref.at[:, index] if len(ref.shape) == 4 else ref.at[index]


class Planes:
    def __init__(self, source, target, semaphores, listed=None):
        self.source, self.target, self.semaphores = source, target, semaphores
        self.listed = listed

    def copy(self, slot, ref, plane):
        return pltpu.make_async_copy(
            pick(ref, plane), pick(self.target, slot), self.semaphores.at[slot]
        )

    def start(self, slot, plane=None):
        if self.listed is None:
            self.copy(slot, self.source, slot if plane is None else plane).start()
        else:
            self.copy(slot, *self.listed[slot]).start()

    def wait(self, slot):
        self.copy(slot, self.source, 0).wait()


def in_sections(x_local, size, loads, stores, start_up, body):
    count = x_local // size

    def cut(ref, first, planes):
        part = pl.ds(first, planes)
        return ref.at[:, part] if len(ref.shape) == 4 else ref.at[part]

    def moves(kinds, section, first, planes):
        return [
            pltpu.make_async_copy(
                cut(source, first, planes), cut(target, first, planes), semaphores.at[section]
            )
            for source, target, semaphores in kinds
        ]

    def begin(section, state):
        for move in moves(loads, section, section * size, size):
            move.start()
        return state

    lax.fori_loop(0, count, begin, 0)

    def work(section, first, planes):
        for move in moves(loads, section, section * size, size):
            move.wait()
        if isinstance(first, int):
            start_up()
        lax.fori_loop(first, first + planes, body, 0)
        for move in moves(stores, section, first, planes):
            move.start()

    work(0, 1, size - 2)

    def rest(section, state):
        work(section, section * size - 1, size)
        return state

    lax.fori_loop(1, count, rest, 0)
    for move in moves(stores, 0, 1, size - 2):
        move.wait()

    def finish(section, state):
        for move in moves(stores, section, section * size - 1, size):
            move.wait()
        return state

    lax.fori_loop(1, count, finish, 0)


def edge_list(ref, low, high, x_local):
    return [(low, 0), (ref, 0), (ref, 1), (ref, x_local - 2), (ref, x_local - 1), (high, 0)]


def viscosity_plane(cells, slot, edges, warmth, warm_slot, outs, out_slot, y_local, z_cells):
    strips, rows = y_local // 8, row_numbers(z_cells)
    before, after = edges
    values = [[cells[c, slot, rows_of(s), :] for s in range(strips)] for c in range(3)]
    up = [[pltpu.roll(v, 7, 0) for v in row] for row in values]
    down = [[pltpu.roll(v, 1, 0) for v in row] for row in values]
    for s in range(strips):
        along_x, along_y, along_z = [], [], []
        for c in range(3):
            value = values[c][s]
            along_x.append(cells[c, slot + 1, rows_of(s), :] - cells[c, slot - 1, rows_of(s), :])
            ahead = jnp.where(rows == 7, up[c][s + 1] if s + 1 < strips else after(c), up[c][s])
            behind = jnp.where(rows == 0, down[c][s - 1] if s else before(c), down[c][s])
            along_y.append(ahead - behind)
            along_z.append(pltpu.roll(value, z_cells - 1, 1) - pltpu.roll(value, 1, 1))
        s_xy = along_y[0] + along_x[1]
        s_xz = along_z[0] + along_x[2]
        s_yz = along_z[1] + along_y[2]
        extra = 0.5 * (
            along_x[0] * along_x[0] + along_y[1] * along_y[1] + along_z[2] * along_z[2]
        ) + 0.25 * (s_xy * s_xy + s_xz * s_xz + s_yz * s_yz)
        rate_sq = rate_base**2 + extra
        value = jnp.exp(
            (0.5 / stress_exponent) * jnp.log(rate_sq)
            + (zener_energy / stress_exponent) * (1.0 / warmth[warm_slot, rows_of(s), :] - 1.0)
        )
        square = value * value + 1.0
        mu = jnp.log(value + square * lax.rsqrt(square)) * lax.rsqrt(rate_sq)
        outs[0][out_slot, rows_of(s), :] = mu * (scaled_mu / 3.0)
        if len(outs) > 1:
            heat = (mu * (1.0 / 3.0)) * extra
            for b in range(z_cells // 128):
                outs[1][b, out_slot, rows_of(s), :] = heat[:, b * 128 : (b + 1) * 128]


def viscosity_call(flow, y_sides, warmth, with_heat, x_sides=None, inner=None):
    _, x_local, y_local, z_cells = flow.shape
    z_blocks = z_cells // 128
    edge = x_sides is not None
    slots, made = (6, 2) if edge else (x_local, x_local - 2)
    outputs = 2 if with_heat else 1

    def kernel(*refs):
        flow_ref, before_ref, after_ref, warmth_ref = refs[:4]
        rest = list(refs[4:])
        listed = None
        if edge:
            low, high = rest[:2]
            listed = edge_list(flow_ref, low, high, x_local)
            rest = rest[2 + outputs :]
        out_refs, rest = rest[:outputs], rest[outputs:]
        cells, cell_sem, warm, warm_sem = rest[:4]
        outs, out_sems = rest[4 : 4 + outputs], rest[4 + outputs :]
        flow_planes = Planes(flow_ref, cells, cell_sem, listed)
        warm_planes = Planes(warmth_ref, warm, warm_sem)

        def plane_of(i):
            return i * (x_local - 1) if edge else i + 1

        def slot_of(i):
            return 3 * i + 1 if edge else i + 1

        def stored(k, i):
            return pltpu.make_async_copy(
                pick(outs[k], i), pick(out_refs[k], plane_of(i)), out_sems[k].at[i]
            )

        if edge:
            for slot in range(6):
                flow_planes.start(slot)
            for i in range(2):
                warm_planes.start(i, plane_of(i))
        else:
            flow_planes.start(0)
            flow_planes.start(1)

            def begin(i, state):
                flow_planes.start(i + 2)
                warm_planes.start(i, i + 1)
                return state

            lax.fori_loop(0, made, begin, 0)
            flow_planes.wait(0)
            flow_planes.wait(1)

        def body(i, state):
            slot, plane = slot_of(i), plane_of(i)
            if edge:
                flow_planes.wait(slot - 1)
                flow_planes.wait(slot)
            flow_planes.wait(slot + 1)
            warm_planes.wait(i)
            viscosity_plane(
                cells,
                slot,
                (lambda c: before_ref[c, plane], lambda c: after_ref[c, plane]),
                warm,
                i,
                outs,
                i,
                y_local,
                z_cells,
            )
            for k in range(outputs):
                stored(k, i).start()
            return state

        lax.fori_loop(0, made, body, 0)

        def finish(i, state):
            for k in range(outputs):
                stored(k, i).wait()
            return state

        lax.fori_loop(0, made, finish, 0)

    shapes = [(x_local, y_local, z_cells), (z_blocks, x_local, y_local, 128)][:outputs]
    held = [(made, y_local, z_cells), (z_blocks, made, y_local, 128)][:outputs]
    operands = [flow, *y_sides, warmth]
    specs = [anywhere, in_vmem, in_vmem, anywhere]
    aliases = {}
    if edge:
        operands += [*x_sides, *inner]
        specs += [anywhere] * (2 + outputs)
        aliases = {6 + k: k for k in range(outputs)}
    return pl.pallas_call(
        kernel,
        in_specs=specs,
        out_specs=[anywhere] * outputs,
        out_shape=[jax.ShapeDtypeStruct(shape, jnp.float32) for shape in shapes],
        input_output_aliases=aliases,
        scratch_shapes=[
            pltpu.VMEM((3, slots, y_local, z_cells), jnp.float32),
            pltpu.SemaphoreType.DMA((slots,)),
            pltpu.VMEM((made, y_local, z_cells), jnp.float32),
            pltpu.SemaphoreType.DMA((made,)),
        ]
        + [pltpu.VMEM(shape, jnp.float32) for shape in held]
        + [pltpu.SemaphoreType.DMA((made,))] * outputs,
        compiler_params=pltpu.CompilerParams(vmem_limit_bytes=vmem_limit),
        name="viscosity_edge" if edge else "viscosity_inner",
    )(*operands)


def viscosity_inner(flow, y_sides, warmth, with_heat):
    _, x_local, y_local, z_cells = flow.shape
    z_blocks, size = z_cells // 128, 4
    outputs = 2 if with_heat else 1

    def kernel(flow_ref, before_ref, after_ref, warmth_ref, *rest):
        out_refs, (cells, cell_sem, warm, warm_sem, *heat) = rest[:outputs], rest[outputs:]
        outs = [out_refs[0]] + heat[:1]

        def body(slot, state):
            viscosity_plane(
                cells,
                slot,
                (lambda c: before_ref[c, slot], lambda c: after_ref[c, slot]),
                warm,
                slot,
                outs,
                slot,
                y_local,
                z_cells,
            )
            return state

        in_sections(
            x_local,
            size,
            [(flow_ref, cells, cell_sem), (warmth_ref, warm, warm_sem)],
            [(heat[0], out_refs[1], heat[1])] if with_heat else [],
            lambda: None,
            body,
        )

    shapes = [(x_local, y_local, z_cells), (z_blocks, x_local, y_local, 128)][:outputs]
    sems = pltpu.SemaphoreType.DMA((x_local // size,))
    return pl.pallas_call(
        kernel,
        in_specs=[anywhere, in_vmem, in_vmem, anywhere],
        out_specs=[in_vmem, anywhere][:outputs],
        out_shape=[jax.ShapeDtypeStruct(shape, jnp.float32) for shape in shapes],
        scratch_shapes=[
            pltpu.VMEM(flow.shape, jnp.float32),
            sems,
            pltpu.VMEM(warmth.shape, jnp.float32),
            sems,
        ]
        + ([pltpu.VMEM(shapes[1], jnp.float32), sems] if with_heat else []),
        compiler_params=pltpu.CompilerParams(vmem_limit_bytes=vmem_limit),
        name="viscosity_inner",
    )(flow, *y_sides, warmth)


vmem_limit = 48 << 20


def advance_plane(cells, mu, slot, edges, push, out_slot, flux, y_local, z_cells):
    strips, rows = y_local // 8, row_numbers(z_cells)
    flow_before, flow_after, mu_before, mu_after = edges
    m = [mu[slot, rows_of(s), :] for s in range(strips)]
    m_up = [pltpu.roll(v, 7, 0) for v in m]
    sums_y = [
        m[s] + jnp.where(rows == 7, m_up[s + 1] if s + 1 < strips else mu_after(), m_up[s])
        for s in range(strips)
    ]
    first_sum = mu_before() + mu[slot, pl.ds(0, 1), :]
    values = [[cells[c, slot, rows_of(s), :] for s in range(strips)] for c in range(3)]
    up = [[pltpu.roll(v, 7, 0) for v in row] for row in values]
    carried = [
        first_sum * (cells[c, slot, pl.ds(0, 1), :] - flow_before(c)) for c in range(3)
    ]
    for s in range(strips):
        sum_x = m[s] + mu[slot + 1, rows_of(s), :]
        sum_z_ahead = m[s] + pltpu.roll(m[s], z_cells - 1, 1)
        sum_z_behind = m[s] + pltpu.roll(m[s], 1, 1)
        for c in range(3):
            value = values[c][s]
            flux_x = sum_x * (cells[c, slot + 1, rows_of(s), :] - value)
            ahead = jnp.where(
                rows == 7, up[c][s + 1] if s + 1 < strips else flow_after(c), up[c][s]
            )
            flux_y = sums_y[s] * (ahead - value)
            turned = pltpu.roll(flux_y, 1, 0)
            total = (flux_x - flux[c, rows_of(s), :]) + (
                flux_y - jnp.where(rows == 0, carried[c], turned)
            ) + (
                sum_z_ahead * (pltpu.roll(value, z_cells - 1, 1) - value)
                - sum_z_behind * (value - pltpu.roll(value, 1, 1))
            )
            flux[c, rows_of(s), :] = flux_x
            carried[c] = turned
            push[c, out_slot, rows_of(s), :] = (
                value + time_step * push[c, out_slot, rows_of(s), :] + total
            )


def first_flux(cells, mu, slot, flux, y_local):
    for s in range(y_local // 8):
        sum_x = mu[slot - 1, rows_of(s), :] + mu[slot, rows_of(s), :]
        for c in range(3):
            flux[c, rows_of(s), :] = sum_x * (
                cells[c, slot, rows_of(s), :] - cells[c, slot - 1, rows_of(s), :]
            )


def advance_call(flow, flow_y, mu, mu_y, push, flow_x=None, mu_x=None, inner=None):
    _, x_local, y_local, z_cells = flow.shape
    edge = flow_x is not None
    slots, made = (6, 2) if edge else (x_local, x_local - 2)

    def kernel(*refs):
        flow_ref, flow_before, flow_after, mu_ref, mu_before, mu_after, push_ref = refs[:7]
        rest = refs[7:]
        flow_listed = mu_listed = None
        if edge:
            flow_listed = edge_list(flow_ref, rest[0], rest[1], x_local)
            mu_listed = edge_list(mu_ref, rest[2], rest[3], x_local)
            rest = rest[5:]
        out_ref, cells, cell_sem, mu_cells, mu_sem, work, work_sem, out_sem, flux = rest
        flow_planes = Planes(flow_ref, cells, cell_sem, flow_listed)
        mu_planes = Planes(mu_ref, mu_cells, mu_sem, mu_listed)
        push_planes = Planes(push_ref, work, work_sem)

        def plane_of(i):
            return i * (x_local - 1) if edge else i + 1

        def stored(i):
            return pltpu.make_async_copy(
                pick(work, i), pick(out_ref, plane_of(i)), out_sem.at[i]
            )

        if edge:
            for slot in range(6):
                flow_planes.start(slot)
                mu_planes.start(slot)
            for i in range(2):
                push_planes.start(i, plane_of(i))
        else:
            for slot in range(2):
                flow_planes.start(slot)
                mu_planes.start(slot)

            def begin(i, state):
                flow_planes.start(i + 2)
                mu_planes.start(i + 2)
                push_planes.start(i, i + 1)
                return state

            lax.fori_loop(0, made, begin, 0)
            for slot in range(2):
                flow_planes.wait(slot)
                mu_planes.wait(slot)
            first_flux(cells, mu_cells, 1, flux, y_local)

        def body(i, state):
            slot, plane = (3 * i + 1 if edge else i + 1), plane_of(i)
            if edge:
                for back in range(2):
                    flow_planes.wait(slot - back)
                    mu_planes.wait(slot - back)
                first_flux(cells, mu_cells, slot, flux, y_local)
            flow_planes.wait(slot + 1)
            mu_planes.wait(slot + 1)
            push_planes.wait(i)
            advance_plane(
                cells,
                mu_cells,
                slot,
                (
                    lambda c: flow_before[c, plane],
                    lambda c: flow_after[c, plane],
                    lambda: mu_before[plane],
                    lambda: mu_after[plane],
                ),
                work,
                i,
                flux,
                y_local,
                z_cells,
            )
            stored(i).start()
            return state

        lax.fori_loop(0, made, body, 0)

        def finish(i, state):
            stored(i).wait()
            return state

        lax.fori_loop(0, made, finish, 0)

    operands = [flow, *flow_y, mu, *mu_y, push]
    specs = [anywhere, in_vmem, in_vmem, anywhere, in_vmem, in_vmem, anywhere]
    aliases = {}
    if edge:
        operands += [*flow_x, *mu_x, inner]
        specs += [anywhere] * 5
        aliases = {11: 0}
    return pl.pallas_call(
        kernel,
        in_specs=specs,
        out_specs=anywhere,
        out_shape=jax.ShapeDtypeStruct(flow.shape, jnp.float32),
        input_output_aliases=aliases,
        scratch_shapes=[
            pltpu.VMEM((3, slots, y_local, z_cells), jnp.float32),
            pltpu.SemaphoreType.DMA((slots,)),
            pltpu.VMEM((slots, y_local, z_cells), jnp.float32),
            pltpu.SemaphoreType.DMA((slots,)),
            pltpu.VMEM((3, made, y_local, z_cells), jnp.float32),
            pltpu.SemaphoreType.DMA((made,)),
            pltpu.SemaphoreType.DMA((made,)),
            pltpu.VMEM((3, y_local, z_cells), jnp.float32),
        ],
        compiler_params=pltpu.CompilerParams(vmem_limit_bytes=vmem_limit),
        name="advance_edge" if edge else "advance_inner",
    )(*operands)


def advance_inner(flow, flow_y, mu, mu_y, push):
    _, x_local, y_local, z_cells = flow.shape
    size = 4

    def kernel(
        flow_ref, flow_before, flow_after, mu_ref, mu_before, mu_after, push_ref,
        out_ref, cells, cell_sem, work, work_sem, out_sem, flux,
    ):
        def body(slot, state):
            advance_plane(
                cells,
                mu_ref,
                slot,
                (
                    lambda c: flow_before[c, slot],
                    lambda c: flow_after[c, slot],
                    lambda: mu_before[slot],
                    lambda: mu_after[slot],
                ),
                work,
                slot,
                flux,
                y_local,
                z_cells,
            )
            return state

        in_sections(
            x_local,
            size,
            [(flow_ref, cells, cell_sem), (push_ref, work, work_sem)],
            [(work, out_ref, out_sem)],
            lambda: first_flux(cells, mu_ref, 1, flux, y_local),
            body,
        )

    sems = pltpu.SemaphoreType.DMA((x_local // size,))
    return pl.pallas_call(
        kernel,
        in_specs=[anywhere, in_vmem, in_vmem, in_vmem, in_vmem, in_vmem, anywhere],
        out_specs=anywhere,
        out_shape=jax.ShapeDtypeStruct(flow.shape, jnp.float32),
        scratch_shapes=[
            pltpu.VMEM(flow.shape, jnp.float32),
            sems,
            pltpu.VMEM(flow.shape, jnp.float32),
            sems,
            sems,
            pltpu.VMEM((3, y_local, z_cells), jnp.float32),
        ],
        compiler_params=pltpu.CompilerParams(vmem_limit_bytes=vmem_limit),
        name="advance_inner",
    )(flow, *flow_y, mu, *mu_y, push)


def cosine_sine_basis(points, period, waves):
    columns, eigen = [], []
    for wave in waves:
        angle = 2.0 * np.pi * ((wave * np.arange(points)) % period) / period
        single = wave % period == 0 or 2 * wave == period
        size = math.sqrt((1.0 if single else 2.0) / period)
        columns.append(np.cos(angle) * size)
        eigen.append(math.sin(2.0 * math.pi * wave / period) ** 2)
        if not single:
            columns.append(np.sin(angle) * size)
            eigen.append(eigen[-1])
    return np.stack(columns, 1), np.array(eigen)


def halves(table):
    table = np.asarray(table, np.float32)
    high = table.astype(jnp.bfloat16)
    low = (table - high.astype(np.float32)).astype(jnp.bfloat16)
    return jnp.asarray(high), jnp.asarray(low)


def split(value):
    high = value.astype(jnp.bfloat16)
    return high, (value - high.astype(jnp.float32)).astype(jnp.bfloat16)


def triple_product(left, right):
    def product(one, two):
        return lax.dot_general(
            one, two, (((1,), (0,)), ((), ())), preferred_element_type=jnp.float32
        )

    return product(left[0], right[0]) + (product(left[0], right[1]) + product(left[1], right[0]))


def z_tables(z_cells):
    half = z_cells // 2
    even, eigen_even = cosine_sine_basis(half, z_cells, range(0, half + 1, 2))
    odd, eigen_odd = cosine_sine_basis(half, z_cells, range(1, half, 2))
    return even, odd, np.concatenate([eigen_even, eigen_odd])


def modes_of(lines, even_high, even_low, odd_high, odd_low):
    half = lines.shape[1] // 2
    first, second = lines[:, :half], lines[:, half:]
    return jnp.concatenate(
        [
            triple_product(split(first + second), (even_high[...], even_low[...])),
            triple_product(split(first - second), (odd_high[...], odd_low[...])),
        ],
        1,
    )


def cells_of(modes, even_high, even_low, odd_high, odd_low):
    half = modes.shape[1] // 2
    first = triple_product(split(modes[:, :half]), (even_high[...], even_low[...]))
    second = triple_product(split(modes[:, half:]), (odd_high[...], odd_low[...]))
    return jnp.concatenate([first + second, first - second], 1)


def divergence_modes(flow, count):
    _, x_local, y_local, z_cells = flow.shape
    piece, strips = z_cells // count, y_local // 8
    step = min(8, x_local)
    even, odd, _ = z_tables(z_cells)
    tables = halves(even) + halves(odd)

    def kernel(
        flow_ref, even_high, even_low, odd_high, odd_low, out_ref,
        cells, semaphores, work, made, out_sem,
    ):
        planes = Planes(flow_ref, cells, semaphores)
        rows = row_numbers(z_cells)

        def begin(i, state):
            planes.start(i)
            return state

        lax.fori_loop(0, x_local, begin, 0)
        planes.wait(0)

        def stored(k):
            part = pl.ds(k * step, step)
            return pltpu.make_async_copy(made.at[:, part], out_ref.at[:, part], out_sem.at[k])

        def group(k, state):
            def plane(i, state):
                j = k * step + i

                @pl.when(j + 1 < x_local)
                def _():
                    planes.wait(j + 1)

                nearer = jnp.where(j > 0, 0.5, 0.0)
                further = jnp.where(j + 1 < x_local, 0.5, 0.0)
                last, following = jnp.maximum(j - 1, 0), jnp.minimum(j + 1, x_local - 1)
                across = [cells[1, j, rows_of(s), :] for s in range(strips)]
                up = [pltpu.roll(v, 7, 0) for v in across]
                down = [pltpu.roll(v, 1, 0) for v in across]
                for s in range(strips):
                    ahead = jnp.where(rows == 7, up[s + 1] if s + 1 < strips else 0.0, up[s])
                    behind = jnp.where(rows == 0, down[s - 1] if s else 0.0, down[s])
                    along = cells[2, j, rows_of(s), :]
                    work[i, rows_of(s), :] = (
                        further * cells[0, following, rows_of(s), :]
                        - nearer * cells[0, last, rows_of(s), :]
                    ) + 0.5 * (
                        (ahead - behind)
                        + (pltpu.roll(along, z_cells - 1, 1) - pltpu.roll(along, 1, 1))
                    )
                return state

            lax.fori_loop(0, step, plane, 0)
            modes = modes_of(
                work[...].reshape(step * y_local, z_cells), even_high, even_low, odd_high, odd_low
            )
            for n in range(count):
                made[n, pl.ds(k * step, step)] = modes[:, n * piece : (n + 1) * piece].reshape(
                    step, y_local, piece
                )
            stored(k).start()
            return state

        groups = x_local // step
        lax.fori_loop(0, groups, group, 0)
        for k in range(groups):
            stored(k).wait()

    return pl.pallas_call(
        kernel,
        in_specs=[anywhere] + [in_vmem] * 4,
        out_specs=anywhere,
        out_shape=jax.ShapeDtypeStruct((count, x_local, y_local, piece), jnp.float32),
        scratch_shapes=[
            pltpu.VMEM((3, x_local, y_local, z_cells), jnp.float32),
            pltpu.SemaphoreType.DMA((x_local,)),
            pltpu.VMEM((step, y_local, z_cells), jnp.float32),
            pltpu.VMEM((count, x_local, y_local, piece), jnp.float32),
            pltpu.SemaphoreType.DMA((x_local // step,)),
        ],
        name="divergence_modes",
    )(flow, *tables)


def add_halo_modes(modes, x_sides, y_sides):
    count, x_local, y_local, piece = modes.shape
    z_cells = count * piece
    even, odd, _ = z_tables(z_cells)
    tables = halves(even) + halves(odd)

    def kernel(
        modes_ref, low_ref, high_ref, before_ref, after_ref,
        even_high, even_low, odd_high, odd_low, out_ref, ends, lines, semaphores,
    ):
        def moves(back):
            pairs = [
                (ends.at[k], modes_ref.at[:, plane])
                for k, plane in enumerate((0, x_local - 1))
            ] + [
                (lines.at[k], modes_ref.at[:, 1 : x_local - 1, 8 * s : 8 * s + 8])
                for k, s in enumerate((0, y_local // 8 - 1))
            ]
            if back:
                pairs = [
                    (ends.at[k], out_ref.at[:, plane])
                    for k, plane in enumerate((0, x_local - 1))
                ] + [
                    (lines.at[k], out_ref.at[:, 1 : x_local - 1, 8 * s : 8 * s + 8])
                    for k, s in enumerate((0, y_local // 8 - 1))
                ]
                return [
                    pltpu.make_async_copy(here, there, semaphores.at[4 + i])
                    for i, (here, there) in enumerate(pairs)
                ]
            return [
                pltpu.make_async_copy(there, here, semaphores.at[i])
                for i, (here, there) in enumerate(pairs)
            ]

        loads, stores = moves(False), moves(True)
        for load in loads:
            load.start()
        added = modes_of(
            jnp.concatenate(
                [-0.5 * low_ref[0], 0.5 * high_ref[0], -0.5 * before_ref[...], 0.5 * after_ref[...]],
                0,
            ),
            even_high,
            even_low,
            odd_high,
            odd_low,
        )
        for load in loads:
            load.wait()
        rows = row_numbers(piece)
        for n in range(count):
            block = added[:, n * piece : (n + 1) * piece]
            side = [block[2 * y_local + k * x_local :][:x_local] for k in range(2)]
            for k, plane in enumerate((0, x_local - 1)):
                ends[k, n] = ends[k, n] + block[k * y_local : (k + 1) * y_local]
                for j, (strip, row) in enumerate(((0, 0), (y_local // 8 - 1, 7))):
                    part = pl.ds(8 * strip, 8)
                    ends[k, n, part, :] = ends[k, n, part, :] + jnp.where(
                        rows == row, side[j][plane : plane + 1], 0.0
                    )
            for j, row in enumerate((0, 7)):
                for x in range(1, x_local - 1):
                    lines[j, n, x - 1] = lines[j, n, x - 1] + jnp.where(
                        rows == row, side[j][x : x + 1], 0.0
                    )
        for store in stores:
            store.start()
        for store in stores:
            store.wait()

    return pl.pallas_call(
        kernel,
        in_specs=[anywhere] + [in_vmem] * 8,
        out_specs=anywhere,
        out_shape=jax.ShapeDtypeStruct(modes.shape, jnp.float32),
        input_output_aliases={0: 0},
        scratch_shapes=[
            pltpu.VMEM((2, count, y_local, piece), jnp.float32),
            pltpu.VMEM((2, count, x_local - 2, 8, piece), jnp.float32),
            pltpu.SemaphoreType.DMA((8,)),
        ],
        name="add_halo_modes",
    )(modes, *x_sides, *y_sides, *tables)


def corrected(flow, spectrum, y_sides):
    count, planes, y_local, piece = spectrum.shape
    x_local, z_cells = planes - 2, count * piece
    strips, part = y_local // 8, planes // 2
    even, odd, _ = z_tables(z_cells)
    tables = halves(even.T) + halves(odd.T)

    def kernel(
        flow_ref, in_ref, before_ref, after_ref,
        even_high, even_low, odd_high, odd_low, out_ref,
        modes, mode_sem, pressure, sides, work, flow_sem, out_sem,
    ):
        table_refs = (even_high, even_low, odd_high, odd_low)

        def load(k):
            span = pl.ds(k * part, part)
            return pltpu.make_async_copy(in_ref.at[:, span], modes.at[:, span], mode_sem.at[k])

        load(0).start()
        load(1).start()

        def brought(k):
            span = pl.ds(k * (part - 2), part - 2 if k == 0 else x_local + 2 - part)
            return pltpu.make_async_copy(flow_ref.at[:, span], work.at[:, span], flow_sem.at[k])

        brought(0).start()
        brought(1).start()
        sides[...] = cells_of(
            jnp.concatenate(
                [
                    jnp.concatenate([ref[n] for n in range(count)], 1)
                    for ref in (before_ref, after_ref)
                ],
                0,
            ),
            *table_refs,
        )
        rows = row_numbers(z_cells)

        def stored(i):
            return pltpu.make_async_copy(pick(work, i), pick(out_ref, i), out_sem.at[i])

        def plane(j, state):
            values = [pressure[j + 1, rows_of(s), :] for s in range(strips)]
            up = [pltpu.roll(v, 7, 0) for v in values]
            down = [pltpu.roll(v, 1, 0) for v in values]
            for s in range(strips):
                ahead = up[s + 1] if s + 1 < strips else sides[pl.ds(x_local + j, 1), :]
                behind = down[s - 1] if s else sides[pl.ds(j, 1), :]
                slopes = (
                    pressure[j + 2, rows_of(s), :] - pressure[j, rows_of(s), :],
                    jnp.where(rows == 7, ahead, up[s]) - jnp.where(rows == 0, behind, down[s]),
                    pltpu.roll(values[s], z_cells - 1, 1) - pltpu.roll(values[s], 1, 1),
                )
                for c in range(3):
                    work[c, j, rows_of(s), :] = work[c, j, rows_of(s), :] - 0.5 * slopes[c]
            stored(j).start()
            return state

        for k in range(2):
            load(k).wait()
            span = pl.ds(k * part, part)
            pressure[span] = cells_of(
                jnp.concatenate(
                    [modes[n, span].reshape(part * y_local, piece) for n in range(count)], 1
                ),
                *table_refs,
            ).reshape(part, y_local, z_cells)
            brought(k).wait()
            lax.fori_loop(k * (part - 2), (part - 2) if k == 0 else x_local, plane, 0)

        def finish(i, state):
            stored(i).wait()
            return state

        lax.fori_loop(0, x_local, finish, 0)

    return pl.pallas_call(
        kernel,
        in_specs=[anywhere, anywhere] + [in_vmem] * 6,
        out_specs=anywhere,
        out_shape=jax.ShapeDtypeStruct(flow.shape, jnp.float32),
        scratch_shapes=[
            pltpu.VMEM(spectrum.shape, jnp.float32),
            pltpu.SemaphoreType.DMA((2,)),
            pltpu.VMEM((planes, y_local, z_cells), jnp.float32),
            pltpu.VMEM((2 * x_local, z_cells), jnp.float32),
            pltpu.VMEM(flow.shape, jnp.float32),
            pltpu.SemaphoreType.DMA((2,)),
            pltpu.SemaphoreType.DMA((x_local,)),
        ],
        compiler_params=pltpu.CompilerParams(vmem_limit_bytes=vmem_limit),
        name="corrected",
    )(flow, spectrum, *y_sides, *tables)


def y_forward(spectrum, ratio, wide_count):
    count, x_local, y_local, piece = spectrum.shape
    y_cells = count * y_local
    share, group = y_cells // wide_count, max(2, x_local // 4)
    table, _ = cosine_sine_basis(y_cells, y_cells, range(y_cells // 2 + 1))
    tables = halves(table.T)

    def kernel(
        in_ref, high_ref, low_ref, ratio_ref, modes_ref, carry_ref,
        lines, in_sems, made, out_sems, sums, power,
    ):
        def load(k):
            part = pl.ds(k * group, group)
            return pltpu.make_async_copy(in_ref.at[:, part], lines.at[:, part], in_sems.at[k])

        def stored(k):
            part = pl.ds(k * group, group)
            return pltpu.make_async_copy(made.at[part], modes_ref.at[part], out_sems.at[k])

        for k in range(x_local // group):
            load(k).start()
        sums[...] = jnp.zeros_like(sums)
        power[...] = jnp.ones_like(power)

        def body(t, state):
            planes = [
                jnp.concatenate([lines[n, 2 * t + side] for n in range(count)], 0)
                for side in range(2)
            ]
            modes = triple_product(
                (high_ref[...], low_ref[...]), split(jnp.concatenate(planes, 1))
            )
            r, pw = ratio_ref[...], power[...]
            for side in range(2):
                plane = modes[:, side * piece : (side + 1) * piece]
                made[2 * t + side] = plane
                sums[side] = plane + r * sums[side]
                sums[2 + side] = sums[2 + side] + pw * plane
            power[...] = pw * r
            return state

        def section(k, state):
            load(k).wait()
            lax.fori_loop(k * (group // 2), (k + 1) * (group // 2), body, 0)
            stored(k).start()
            return state

        lax.fori_loop(0, x_local // group, section, 0)
        for kind in range(4):
            carry_ref[:, kind] = sums[kind].reshape(wide_count, share, piece)
        for k in range(x_local // group):
            stored(k).wait()

    return pl.pallas_call(
        kernel,
        in_specs=[anywhere] + [in_vmem] * 3,
        out_specs=[anywhere, in_vmem],
        out_shape=[
            jax.ShapeDtypeStruct((x_local, y_cells, piece), jnp.float32),
            jax.ShapeDtypeStruct((wide_count, 4, share, piece), jnp.float32),
        ],
        scratch_shapes=[
            pltpu.VMEM(spectrum.shape, jnp.float32),
            pltpu.SemaphoreType.DMA((x_local // group,)),
            pltpu.VMEM((x_local, y_cells, piece), jnp.float32),
            pltpu.SemaphoreType.DMA((x_local // group,)),
            pltpu.VMEM((4, y_cells, piece), jnp.float32),
            pltpu.VMEM((y_cells, piece), jnp.float32),
        ],
        name="y_forward",
    )(spectrum, *tables, ratio)


def power_of(value, exponent):
    result = None
    while exponent:
        if exponent & 1:
            result = value if result is None else result * value
        value = value * value
        exponent >>= 1
    return result


def join_carries(carries, ratio, block):
    count, kinds, _, _ = carries.shape

    def kernel(in_ref, ratio_ref, out_ref):
        step = power_of(ratio_ref[...], block)
        scale = 1.0 / (1.0 - power_of(step, count))
        for kind in range(kinds):
            order = list(range(count)) if kind < 2 else list(range(count))[::-1]
            total = in_ref[order[0], kind]
            for w in order[1:]:
                total = in_ref[w, kind] + step * total
            total = total * scale
            for w in order:
                out_ref[w, kind] = total
                total = in_ref[w, kind] + step * total

    return pl.pallas_call(
        kernel,
        in_specs=[in_vmem] * 2,
        out_specs=in_vmem,
        out_shape=jax.ShapeDtypeStruct(carries.shape, jnp.float32),
        compiler_params=pltpu.CompilerParams(vmem_limit_bytes=vmem_limit),
        name="join_carries",
    )(carries, ratio)


def y_inverse(modes, carries, ratio, gain, count):
    x_local, y_cells, piece = modes.shape
    y_local, pairs, group = y_cells // count, x_local // 2, max(2, x_local // 4)
    table, _ = cosine_sine_basis(y_cells, y_cells, range(y_cells // 2 + 1))
    tables = halves(table)

    def kernel(
        modes_in, carry_ref, high_ref, low_ref, ratio_ref, gain_ref, out_ref,
        planes, in_sems, behind, state, cells, out_sems,
    ):
        def load(k):
            part = pl.ds(k * group, group)
            return pltpu.make_async_copy(modes_in.at[part], planes.at[part], in_sems.at[k])

        def stored(t):
            part = pl.ds(2 * t, 2)
            return pltpu.make_async_copy(cells.at[:, part], out_ref.at[:, part], out_sems.at[t])

        def carry(kind):
            return carry_ref[:, kind].reshape(y_cells, piece)

        groups = x_local // group
        for k in range(groups)[::-1]:
            load(k).start()
        for kind in range(4):
            state[kind] = carry(kind)
        behind[x_local + 1] = carry(2)

        def back(i, done):
            m = pairs - 1 - i
            r = ratio_ref[...]
            for side in range(2):
                value = r * state[2 + side]
                behind[2 * m + 1 + side] = value
                state[2 + side] = planes[2 * m + side] + value
            return done

        def back_section(k, done):
            load(groups - 1 - k).wait()
            lax.fori_loop(k * (group // 2), (k + 1) * (group // 2), back, 0)
            return done

        lax.fori_loop(0, groups, back_section, 0)
        behind[0] = ratio_ref[...] * state[3]

        def body(t, done):
            r, gain_value = ratio_ref[...], gain_ref[...]
            even_plane = planes[jnp.minimum(2 * t, x_local - 2)]
            odd_plane = planes[jnp.maximum(2 * t - 1, 1)]
            even = r * state[0] + jnp.where(t < pairs, even_plane, 0.0)
            odd = jnp.where(t > 0, odd_plane + r * state[1], state[1])
            state[0] = even
            state[1] = odd
            joined = jnp.concatenate(
                [gain_value * (odd + behind[2 * t]), gain_value * (even + behind[2 * t + 1])], 1
            )
            result = triple_product((high_ref[...], low_ref[...]), split(joined))
            for n in range(count):
                for side in range(2):
                    cells[n, 2 * t + side] = result[
                        n * y_local : (n + 1) * y_local, side * piece : (side + 1) * piece
                    ]
            stored(t).start()
            return done

        lax.fori_loop(0, pairs + 1, body, 0)

        def finish(t, done):
            stored(t).wait()
            return done

        lax.fori_loop(0, pairs + 1, finish, 0)

    made = (count, x_local + 2, y_local, piece)
    return pl.pallas_call(
        kernel,
        in_specs=[anywhere] + [in_vmem] * 5,
        out_specs=anywhere,
        out_shape=jax.ShapeDtypeStruct(made, jnp.float32),
        scratch_shapes=[
            pltpu.VMEM(modes.shape, jnp.float32),
            pltpu.SemaphoreType.DMA((x_local // group,)),
            pltpu.VMEM((x_local + 2, y_cells, piece), jnp.float32),
            pltpu.VMEM((4, y_cells, piece), jnp.float32),
            pltpu.VMEM(made, jnp.float32),
            pltpu.SemaphoreType.DMA((pairs + 1,)),
        ],
        name="y_inverse",
    )(modes, carries, *tables, ratio, gain)


def turn(value, axis):
    return lax.all_to_all(value, axis, split_axis=0, concat_axis=0, tiled=True)


def project(spectrum):
    count, x_local, y_local, piece = spectrum.shape
    y_cells, z_cells = count * y_local, count * piece
    wide_count = lax.axis_size("wide")
    _, eigen_y = cosine_sine_basis(y_cells, y_cells, range(y_cells // 2 + 1))
    eigen_z = jnp.asarray(z_tables(z_cells)[2], jnp.float32)
    own_z = lax.dynamic_slice_in_dim(eigen_z, lax.axis_index("narrow") * piece, piece)
    excess = 4.0 * (jnp.asarray(eigen_y, jnp.float32)[:, None] + own_z[None, :] + penalty)
    root = jnp.sqrt(excess * (4.0 + excess))
    ratio = 2.0 / (2.0 + excess + root)
    gain = -4.0 / root
    share = y_cells // wide_count
    own_ratio = lax.dynamic_slice_in_dim(ratio, lax.axis_index("wide") * share, share)
    modes, carries = y_forward(turn(spectrum, "narrow"), ratio, wide_count)
    carries = turn(join_carries(turn(carries, "wide"), own_ratio, x_local // 2), "wide")
    return turn(y_inverse(modes, carries, ratio, gain, count), "narrow")


def conduct(profile, spread):
    sides = (("wide", 0), ("narrow", 1))
    spread = with_halo(spread, sides, STEPS - 1, False)
    profile = with_halo(profile, sides, STEPS, False)
    for _ in range(STEPS):
        center = profile[1:-1, 1:-1]
        near = (
            profile[2:, 1:-1] + profile[:-2, 1:-1] + profile[1:-1, 2:] + profile[1:-1, :-2]
        )
        ahead = jnp.pad(center[:, :, 1:], ((0, 0), (0, 0), (0, 1)))
        behind = jnp.pad(center[:, :, :-1], ((0, 0), (0, 0), (1, 0)))
        profile = center + spread * (near + ahead + behind - 6.0 * center)
        spread = spread[1:-1, 1:-1]
    return profile


def both_rings(value, dim):
    y_sides = ring(value, "narrow", dim + 1)
    x_sides = ring(value, "wide", dim)
    return x_sides, y_sides


def device_step(
    material_flow_vector,
    tool_push_density,
    tool_warmth_excess,
    substrate_warmth_excess,
    spread_coefficient,
    source_owner_sheet,
    source_part_line,
):
    flow = material_flow_vector
    flow_x, flow_y = both_rings(flow, 1)
    current, current_x, current_y = flow, flow_x, flow_y
    for section in range(PASSES):
        last = section + 1 == PASSES
        inner = viscosity_inner(current, current_y, tool_warmth_excess, last)
        fields = viscosity_call(current, current_y, tool_warmth_excess, last, current_x, inner)
        mu = fields[0]
        mu_x, mu_y = both_rings(mu, 0)
        inner = advance_inner(flow, flow_y, mu, mu_y, tool_push_density)
        current = advance_call(flow, flow_y, mu, mu_y, tool_push_density, flow_x, mu_x, inner)
        if not last:
            current_x, current_y = both_rings(current, 1)
    heat_cells = fields[1]
    end_x = ring(current[0], "wide", 0)
    y_local = flow.shape[2]
    end_y = [
        shift(current[1, :, y_local - 1 :], "narrow", 1)[:, 0],
        shift(current[1, :, :1], "narrow", -1)[:, 0],
    ]
    modes = divergence_modes(current, lax.axis_size("narrow"))
    spectrum = project(add_halo_modes(modes, end_x, end_y))
    inner = spectrum[:, 1:-1]
    corrected_flow_vector = corrected(
        current, spectrum, [side[:, :, 0] for side in ring(inner, "narrow", 2)]
    )
    z_blocks = heat_cells.shape[0]
    slab_count = lax.axis_size("wide")
    component_lines = substrate_warmth_excess.shape[0] * substrate_warmth_excess.shape[1]
    targets = source_owner_sheet[:, 0] * component_lines + source_part_line
    partial_value = (
        jnp.zeros((slab_count * component_lines, 128), jnp.float32)
        .at[targets.reshape(-1, z_blocks).T.reshape(-1)]
        .add(heat_cells.reshape(-1, 128))
    )
    substrate_energy_input = lax.psum_scatter(
        partial_value.reshape(slab_count, component_lines, 128),
        "wide",
        scatter_dimension=0,
        tiled=True,
    )
    thermal_profile = substrate_warmth_excess + dissipation_factor * substrate_energy_input.reshape(
        substrate_warmth_excess.shape
    )
    return (corrected_flow_vector, conduct(thermal_profile, spread_coefficient))


def solution(mesh):
    return jax.shard_map(
        device_step,
        mesh=mesh,
        in_specs=(
            P(None, "wide", "narrow", None),
            P(None, "wide", "narrow", None),
            P("wide", "narrow", None),
            P("wide", "narrow", None),
            P("wide", "narrow", None),
            P(("wide", "narrow"), None),
            P(("wide", "narrow")),
        ),
        out_specs=(P(None, "wide", "narrow", None), P("wide", "narrow", None)),
        check_vma=False,
    )
```
